32 devices in a mesh: dp: 8 (over y, x, core), tensor: 4 (over z).
Axes of the slice: x: 2, y: 2, z: 4, core: 2. Of those that a mesh axis runs over, the one named last changes fastest.
Arguments:
- inputs: bfloat16 [16384, 768], P(('dp', 'tensor')), may hold values from -6 to 6
- doc_ids: int32 [8, 2048], P('dp'), may hold values from 0 to 2, never falling along the last dimension, each value on 1 to 1024 neighbouring positions
- gain_attn: bfloat16 [768], P('dp'), may hold values from 0.099609375 to 1.8984375
- w_qkv: bfloat16 [3, 768, 768], P(None, 'dp', 'tensor'), may hold values from -0.3125 to 0.3125
- w_out: bfloat16 [768, 768], P('tensor', 'dp'), may hold values from -1.75 to 1.75
- gain_mlp: bfloat16 [768], P('dp'), may hold values from 0.099609375 to 1.8984375
- w_up: bfloat16 [768, 3072], P('dp', 'tensor'), may hold values from -0.21875 to 0.21875
- w_down: bfloat16 [3072, 768], P('tensor', 'dp'), may hold values from -0.109375 to 0.109375
- grad_out: bfloat16 [16384, 768], P(('dp', 'tensor')), may hold values from -6 to 6
Outputs:
- layer_out: bfloat16 [16384, 768], P(('dp', 'tensor'))
- grad_inputs: float32 [16384, 768], P(('dp', 'tensor'))
- grad_gain_attn: float32 [768], P('dp')
- grad_w_qkv: float32 [3, 768, 768], P(None, 'dp', 'tensor')
- grad_w_out: float32 [768, 768], P('tensor', 'dp')
- grad_gain_mlp: float32 [768], P('dp')
- grad_w_up: float32 [768, 3072], P('dp', 'tensor')
- grad_w_down: float32 [3072, 768], P('tensor', 'dp')
The draws below stay inside these ranges and needn't reach their ends.
Inputs may be any that keep to these rules, and one draw needn't show every extreme that they name: `doc_ids`: each row holds the 3 documents of one group in order, each of one or more positions, the longest exactly 1024 positions.
All inputs are finite; a program needn't handle non-finite values.
Results may differ from the reference program's by a relative error of at most 0.015.
The reference program's roundings to bfloat16 on the way count: a program that leaves them out, or rounds other values in their place, can miss the bound.
Values may be sent and summed in bfloat16 or wider, within the bound.
No kernel may reach another device: no remote copies, remote signals or barrier semaphores. Data moves between devices by JAX's collectives and lax.ppermute only.
A program may use at most 192 MiB of HBM per device.

```python
import math
import jax
import jax.numpy as jnp
import numpy as np
from jax import lax

D = 768
HEADS = 12
HEAD_DIM = 64
FF = 3072
TOK_GRP = 2048
DOCS = 3
BLOCK = 256
MOST_DOC = 1024
GROUPS = 8
TOKENS = 16384


def raised(array, own_key, source, target, blocks, factor):
    def block_of(position):
        return (jnp.arange(array.shape[position]) // (array.shape[position] // blocks)).reshape((-1,) + (1,) * (array.ndim - 1 - position))

    first = jax.random.permutation(own_key, blocks)[block_of(target)]
    other_side = (block_of(target) + blocks // 2) % blocks
    return jnp.where((block_of(source) == first) | (block_of(source) == other_side), factor * array, array)


def levels(stream_key, dims, shards, least, high):
    factor_of = 1.0
    for position, parts in shards:
        steps = jax.random.uniform(jax.random.fold_in(jax.random.fold_in(stream_key, 6), position), (parts,), jnp.float32, least / len(shards), high / len(shards))
        factor_of = factor_of * jnp.repeat(jnp.exp(steps), dims[position] // parts).reshape((-1,) + (1,) * (len(dims) - 1 - position))
    return factor_of


def profile(amount, total, limit, lean):
    portions = [(1 << 20) // math.isqrt(standing ** lean) + 1 for standing in range(2, amount + 1)]
    spare, holding = total - limit - (amount - 1), [1] * (amount - 1)
    while spare > 0:
        candidates = [i for i in range(amount - 1) if holding[i] < limit]
        mass, left = sum([portions[i] for i in candidates]), spare
        for i in candidates:
            extra = min(limit - holding[i], max(1, left * portions[i] // mass), spare)
            holding[i] = holding[i] + extra
            spare = spare - extra
    return np.array([limit] + holding)


def ragged(rng, count, total, most, lean):
    if count == 2:
        one = jax.random.randint(rng, (), max(1, total - most), min(most, total - 1) + 1)
        return jnp.stack([one, total - one])
    tallies = jnp.asarray(profile(count, total, most, lean), jnp.int32)
    twos = (count - 1) // 2
    donor, receiver = tallies[1:1 + 2 * twos:2], tallies[2:2 + 2 * twos:2]
    room = jnp.minimum(donor - 1, most - receiver)
    shifted = jax.random.randint(jax.random.fold_in(rng, 1), (twos,), 0, 1 << 20) % (room + 1)
    tallies = tallies.at[1:1 + 2 * twos:2].set(donor - shifted).at[2:2 + 2 * twos:2].set(receiver + shifted)
    return tallies[jax.random.permutation(jax.random.fold_in(rng, 2), count)]


def scatter_about(stream_key, extent, scale, reach, shards=(), kind=jnp.bfloat16):
    entries = scale * jax.random.normal(stream_key, extent, jnp.float32)
    if shards:
        entries = entries * levels(stream_key, extent, shards, -0.22, 0.18)
    return jnp.clip(entries, -reach, reach).astype(kind)


def bell_draw_with(key, dims, deviation, most, shards, heavy, held_as=jnp.bfloat16):
    values = deviation * jax.random.normal(key, dims, jnp.float32)
    if shards:
        values = values * levels(key, dims, shards, -0.22, 0.18)
    return jnp.clip(raised(values, jax.random.fold_in(key, 3), *heavy), -most, most).astype(held_as)


def setup_inputs(seed: int = 0) -> dict:
    key_list = jax.random.split(jax.random.key(seed), 10)
    return {
        "inputs": scatter_about(key_list[0], (TOKENS, D), 1.0, 6.0, ((0, 32),)),
        "doc_ids": jax.vmap(lambda own: jnp.searchsorted(jnp.cumsum(ragged(own, DOCS, TOK_GRP, MOST_DOC, 0)), jnp.arange(TOK_GRP), side="right"))(jax.random.split(key_list[1], GROUPS)).reshape((GROUPS, TOK_GRP)).astype(jnp.int32),
        "gain_attn": jnp.clip(1.0 + 0.18 * jax.random.normal(key_list[2], (D,), jnp.float32), 0.099609375, 1.8984375).astype(jnp.bfloat16),
        "w_qkv": scatter_about(key_list[3], (3, D, D), (D // 2) ** -0.5, 0.3125, ((1, 8), (2, 4))),
        "w_out": scatter_about(key_list[4], (D, D), (D // 64) ** -0.5, 1.75, ((0, 4), (1, 8))),
        "gain_mlp": jnp.clip(1.0 + 0.18 * jax.random.normal(key_list[5], (D,), jnp.float32), 0.099609375, 1.8984375).astype(jnp.bfloat16),
        "w_up": scatter_about(key_list[6], (D, FF), D ** -0.5, 0.21875, ((0, 8), (1, 4))),
        "w_down": scatter_about(key_list[7], (FF, D), FF ** -0.5, 0.109375, ((0, 4), (1, 8))),
        "grad_out": bell_draw_with(key_list[8], (TOKENS, D), 1.0, 6.0, ((0, 32),), (0, 1, 32, 2.75)),
    }


@jax.custom_vjp
def low(v):
    return lax.optimization_barrier(v.astype(jnp.bfloat16)).astype(jnp.float32)

@jax.custom_vjp
def low_back(v):
    return v

def low_keep(v):
    return (low(v), None)

def low_pass(kept, grad):
    return (grad,)

def back_keep(v):
    return (v, None)

def back_low(kept, grad):
    return (low(grad),)
low.defvjp(low_keep, low_pass)
low_back.defvjp(back_keep, back_low)
eps = 1e-05

def norm_rows(row_data, gain):
    row_mean = lax.optimization_barrier(jnp.mean(row_data, axis=-1, keepdims=True))
    centered = row_data - row_mean
    variance = lax.optimization_barrier(jnp.mean(centered * centered, axis=-1, keepdims=True))
    return centered * lax.rsqrt(variance + eps) * gain

def gelu_tanh(values):
    return 0.5 * values * (1.0 + jnp.tanh(0.7978845608028654 * (values + 0.044715 * values * values * values)))

def cog_weights(scores, visible):
    absolute = jnp.abs(scores)
    largest = lax.optimization_barrier(jnp.max(jnp.where(visible, absolute, 0.0), axis=-1, keepdims=True))
    summed = lax.optimization_barrier(jnp.sum(jnp.where(visible, jnp.exp(absolute - largest), 0.0), axis=-1, keepdims=True))
    log_total = largest + jnp.log(summed)
    magnitude = jnp.where(visible, jnp.exp(absolute - log_total), 0.0)
    return (jnp.sign(scores) * magnitude, log_total)

def layer_group(group_rows, gain_attn, w_qkv, w_out, gain_mlp, w_up, w_down, documents):
    token_count = group_rows.shape[0]
    normed = low(norm_rows(group_rows, gain_attn))
    projected = low_back(low(jnp.einsum('td,cde->cte', normed, w_qkv, precision=lax.Precision.HIGHEST)))
    split_heads = projected.reshape(3, token_count, HEADS, HEAD_DIM)
    queries = split_heads[0]
    key_rows = split_heads[1]
    value_rows = split_heads[2]
    row_count = min(512, token_count)
    places = jnp.arange(token_count, dtype=jnp.int32)
    score_scale = HEAD_DIM ** (-0.5)

    def attend(block_index):
        row_start = block_index * row_count
        query_block = lax.dynamic_slice_in_dim(queries, row_start, row_count, 0)
        scores = low_back(jnp.einsum('qhd,khd->hqk', query_block, key_rows, precision=lax.Precision.HIGHEST) * score_scale)
        query_places = row_start + jnp.arange(row_count, dtype=jnp.int32)
        query_docs = lax.dynamic_slice_in_dim(documents, row_start, row_count, 0)
        visible = (query_docs[:, None] == documents[None, :]) & (places[None, :] // BLOCK <= query_places[:, None] // BLOCK)
        weights, log_total = cog_weights(scores, visible[None])
        return jnp.einsum('hqk,khd->qhd', low(weights), value_rows, precision=lax.Precision.HIGHEST)
    attended = lax.map(jax.checkpoint(attend), jnp.arange(token_count // row_count, dtype=jnp.int32))
    attended = low_back(low(attended.reshape(token_count, HEADS * HEAD_DIM)))
    mixed = group_rows + low_back(jnp.dot(attended, w_out, precision=lax.Precision.HIGHEST))
    normed_mlp = low(norm_rows(mixed, gain_mlp))
    hidden = low_back(jnp.dot(normed_mlp, w_up, precision=lax.Precision.HIGHEST))
    active = low(gelu_tanh(hidden))
    return mixed + jnp.dot(active, w_down, precision=lax.Precision.HIGHEST)

def reference(inputs, doc_ids, gain_attn, w_qkv, w_out, gain_mlp, w_up, w_down, grad_out):
    params = tuple((weight.astype(jnp.float32) for weight in (gain_attn, w_qkv, w_out, gain_mlp, w_up, w_down)))
    groups_in = inputs.astype(jnp.float32).reshape(GROUPS, TOK_GRP, D)
    groups_grad = grad_out.astype(jnp.float32).reshape(GROUPS, TOK_GRP, D)

    def one_group(totals, member):
        group_in, documents, group_grad = member

        def forward(group_rows, gain_one, w_proj, w_back, gain_two, w_first, w_second):
            return layer_group(group_rows, gain_one, w_proj, w_back, gain_two, w_first, w_second, documents)
        result, pull = jax.vjp(forward, group_in, *params)
        gradients = pull(group_grad)
        totals = tuple((running + grad_part for running, grad_part in zip(totals, gradients[1:])))
        return (totals, (result.astype(jnp.bfloat16), gradients[0]))
    start_totals = tuple((jnp.zeros(weight.shape, jnp.float32) for weight in params))
    totals, (outs_all, grad_all) = lax.scan(one_group, start_totals, (groups_in, doc_ids, groups_grad))
    return (outs_all.reshape(TOKENS, D), grad_all.reshape(TOKENS, D), totals[0], totals[1], totals[2], totals[3], totals[4], totals[5])
```

```python
import functools

import jax
import jax.numpy as jnp
from jax import lax
from jax.experimental import pallas as pl
from jax.experimental.pallas import tpu as pltpu
from jax.sharding import PartitionSpec as P

HEAD_DIM = 64
BLOCK = 256
f32 = jnp.float32
bf16 = jnp.bfloat16
HIDE = -1e30


def nn(a, b):
    return lax.dot_general(a, b, (((1,), (0,)), ((), ())), preferred_element_type=f32)


def nt(a, b):
    return lax.dot_general(a, b, (((1,), (1,)), ((), ())), preferred_element_type=f32)


def doc_of(place, ends):
    return jnp.where(place >= ends[1], 2, jnp.where(place >= ends[0], 1, 0))


def first_block(row, ends):
    start = jnp.where(row >= ends[1], ends[1], jnp.where(row >= ends[0], ends[0], 0))
    return lax.div(start, BLOCK)


def hidden_bias(i, j, ends):
    keys = j * BLOCK + lax.broadcasted_iota(jnp.int32, (BLOCK, BLOCK), 0)
    rows = i * BLOCK + lax.broadcasted_iota(jnp.int32, (BLOCK, BLOCK), 1)
    return jnp.where(doc_of(keys, ends) == doc_of(rows, ends), 0.0, HIDE)


def sign_of(s):
    return jnp.clip(s * 3e38, -1.0, 1.0)


def ring_blocks(z, count):
    for n in range(count):
        yield n, lax.rem(z - n // 2 + 4, 4) * 2 + n % 2


def attn_fwd_body(scal, *refs):
    parts, (out, lse, qs, vs, ks, acc) = refs[:-6], refs[-6:]
    i = pl.program_id(0)
    width = qs.shape[1]
    heads = width // HEAD_DIM
    z = scal[0]
    ends = (scal[1], scal[2])

    @pl.when(i == 0)
    def _():
        for n, b in ring_blocks(z, len(parts)):
            ref = parts[n]
            qs[b] = ref[0:width] * bf16(0.125)
            vs[b] = ref[2 * width : 3 * width]
            for h in range(heads):
                ks[h, b] = ref[width + h * HEAD_DIM : width + (h + 1) * HEAD_DIM].T

    acc[...] = jnp.zeros_like(acc)

    def step(j, carry):
        bias = hidden_bias(i, j, ends)
        new = []
        for h in range(heads):
            rows = slice(h * HEAD_DIM, (h + 1) * HEAD_DIM)
            m, l = carry[h]
            s = nn(ks[h, j], qs[i, rows])
            a = jnp.abs(s) + bias
            m_new = jnp.maximum(m, jnp.max(a, axis=0, keepdims=True))
            p = jnp.exp(a - m_new)
            alpha = jnp.exp(m - m_new)
            w = (sign_of(s) * p).astype(bf16)
            acc[rows] = acc[rows] * alpha + nn(vs[j, rows], w)
            new.append((m_new, l * alpha + jnp.sum(p, axis=0, keepdims=True)))
        return tuple(new)

    zero = jnp.zeros((1, BLOCK), f32)
    stats = lax.fori_loop(first_block(i * BLOCK, ends), i + 1, step, ((zero, zero),) * heads)
    t = lax.div(i, 2)
    cols = pl.ds(pl.multiple_of(lax.rem(i, 2) * BLOCK, BLOCK), BLOCK)
    dest = lax.rem(t - z + 4, 4)
    for h in range(heads):
        rows = slice(h * HEAD_DIM, (h + 1) * HEAD_DIM)
        m, l = stats[h]
        out[dest, rows, cols] = (acc[rows] / l).astype(bf16)
        lse[i, h : h + 1, :] = m + jnp.log(l)


def whole(shape):
    return pl.BlockSpec(shape, lambda *_: (0,) * len(shape))


def attn_fwd(scal, parts):
    width, nb = parts[0].shape[0] // 3, len(parts)
    heads = width // HEAD_DIM
    cols = nb // 4 * BLOCK
    return pl.pallas_call(
        attn_fwd_body,
        out_shape=(
            jax.ShapeDtypeStruct((4, width, cols), bf16),
            jax.ShapeDtypeStruct((nb, 8, BLOCK), f32),
        ),
        grid_spec=pltpu.PrefetchScalarGridSpec(
            num_scalar_prefetch=1,
            grid=(nb,),
            in_specs=[whole(p.shape) for p in parts],
            out_specs=(whole((4, width, cols)), whole((nb, 8, BLOCK))),
            scratch_shapes=[
                pltpu.VMEM((nb, width, BLOCK), bf16),
                pltpu.VMEM((nb, width, BLOCK), bf16),
                pltpu.VMEM((heads, nb, BLOCK, HEAD_DIM), bf16),
                pltpu.VMEM((width, BLOCK), f32),
            ],
        ),
        compiler_params=pltpu.CompilerParams(dimension_semantics=("arbitrary",)),
        cost_estimate=pl.CostEstimate(
            flops=4 * heads * 20 * BLOCK * BLOCK * 256, bytes_accessed=4_000_000, transcendentals=heads * 20 * BLOCK * BLOCK
        ),
        name="attn_fwd",
    )(scal, *parts)


def attn_bwd_body(scal, *refs):
    parts, refs = refs[:-16], refs[-16:]
    o, g0, g1, g2, g3, lse, grad, qs, kts, gs, ks, vns, inner, dq, dk, dv = refs
    i = pl.program_id(0)
    nb = pl.num_programs(0)
    width = qs.shape[1]
    heads = width // HEAD_DIM
    z = scal[0]
    ends = (scal[1], scal[2])

    @pl.when(i == 0)
    def _():
        for n, b in ring_blocks(z, len(parts)):
            ref = parts[n]
            qs[b] = ref[0:width] * bf16(0.125)
            kts[b] = ref[width : 2 * width]
            for h in range(heads):
                ks[h, b] = ref[width + h * HEAD_DIM : width + (h + 1) * HEAD_DIM].T
                vns[h, b] = ref[2 * width + h * HEAD_DIM : 2 * width + (h + 1) * HEAD_DIM].T
        for s, ref in enumerate((g0, g1, g2, g3)):
            t = lax.rem(z + s, 4)
            for half in range(2):
                cols = slice(half * BLOCK, (half + 1) * BLOCK)
                gs[t * 2 + half] = ref[:, cols]
                both = ref[:, cols].astype(f32) * o[s, :, cols].astype(f32)
                for h in range(heads):
                    inner[t * 2 + half, h : h + 1, :] = jnp.sum(
                        both[h * HEAD_DIM : (h + 1) * HEAD_DIM], axis=0, keepdims=True
                    )
        dk[...] = jnp.zeros_like(dk)
        dv[...] = jnp.zeros_like(dv)

    dq[i] = jnp.zeros(dq.shape[1:], f32)

    def step(j, carry):
        bias = hidden_bias(i, j, ends)
        for h in range(heads):
            rows = slice(h * HEAD_DIM, (h + 1) * HEAD_DIM)
            q = qs[i, rows]
            g = gs[i, rows]
            s = nn(ks[h, j], q)
            pushed = nn(vns[h, j], g)
            mag = jnp.exp(jnp.abs(s) + bias - lse[i, h : h + 1, :])
            w = sign_of(s) * mag
            ds = (mag * pushed - w * inner[i, h : h + 1, :]).astype(bf16)
            dv[j, rows] += nt(g, w.astype(bf16))
            dk[j, rows] += nt(q, ds)
            dq[i, rows] += nn(kts[j, rows], ds)
        return carry

    lax.fori_loop(first_block(i * BLOCK, ends), i + 1, step, 0)

    @pl.when(i == nb - 1)
    def _():
        for n, b in ring_blocks(z, len(parts)):
            cols = slice(n * BLOCK, (n + 1) * BLOCK)
            grad[0:width, cols] = (dq[b] * 0.125).astype(bf16)
            grad[width : 2 * width, cols] = dk[b].astype(bf16)
            grad[2 * width : 3 * width, cols] = dv[b].astype(bf16)


def attn_bwd(scal, parts, attended, grads, lse):
    width, nb = parts[0].shape[0] // 3, len(parts)
    heads = width // HEAD_DIM
    cols = nb // 4 * BLOCK
    block16 = pltpu.VMEM((nb, width, BLOCK), bf16)
    natural = pltpu.VMEM((heads, nb, BLOCK, HEAD_DIM), bf16)
    block32 = pltpu.VMEM((nb, width, BLOCK), f32)
    ops = (*parts, attended, *grads, lse)
    return pl.pallas_call(
        attn_bwd_body,
        out_shape=jax.ShapeDtypeStruct((3 * width, nb * BLOCK), bf16),
        grid_spec=pltpu.PrefetchScalarGridSpec(
            num_scalar_prefetch=1,
            grid=(nb,),
            in_specs=[whole(p.shape) for p in ops],
            out_specs=whole((3 * width, nb * BLOCK)),
            scratch_shapes=[block16, block16, block16, natural, natural, pltpu.VMEM((nb, 8, BLOCK), f32), block32, block32, block32],
        ),
        compiler_params=pltpu.CompilerParams(dimension_semantics=("arbitrary",)),
        cost_estimate=pl.CostEstimate(
            flops=10 * heads * 20 * BLOCK * BLOCK * 256, bytes_accessed=8_000_000, transcendentals=heads * 20 * BLOCK * BLOCK
        ),
        name="attn_bwd",
    )(scal, *ops)


EPS = 1e-05
RING = 4


def turn(x, shift):
    return lax.ppermute(x, "tensor", [(i, (i + shift) % RING) for i in range(RING)])


def swap(x, axis, bit, size):
    return lax.ppermute(x, axis, [(i, i ^ bit) for i in range(size)])


def pick(x, index, axis=0):
    return lax.dynamic_index_in_dim(x, index, axis, keepdims=False)


def ring_gather(x):
    got = [x]
    for _ in range(RING - 1):
        got.append(turn(got[-1], 1))
    return got


def ring_reduce(chunks):
    moving = chunks[1].astype(bf16)
    for r in range(1, RING):
        moved = turn(moving, 1)
        total = moved.astype(f32) + chunks[(r + 1) % RING]
        moving = total.astype(bf16)
    return total


def spread_blocks(x, bits, size):
    for bit in bits:
        x = jnp.concatenate([x, swap(x, "dp", bit, size)])
    return x


def place_of(mask, bits):
    place = 0
    for k, bit in enumerate(bits):
        place = place + jnp.where(mask & bit != 0, 1 << k, 0)
    return place


def halve(blocks, left, bit, me, size):
    at = left.index(bit)
    lead, tail = 1 << at, 1 << (len(left) - at - 1)
    split = blocks.reshape((lead, 2, tail) + blocks.shape[1:])
    mine = jnp.where(me & bit != 0, 1, 0)
    send = pick(split, 1 - mine, 1).astype(bf16)
    keep = pick(split, mine, 1)
    total = keep.astype(f32) + swap(send, "dp", bit, size).astype(f32)
    return total.reshape((lead * tail,) + blocks.shape[1:]), [b for b in left if b != bit]


def centre(rows):
    shifted = rows - jnp.mean(rows, axis=-1, keepdims=True)
    rstd = lax.rsqrt(jnp.mean(shifted * shifted, axis=-1, keepdims=True) + EPS)
    return shifted * rstd, rstd


def norm_back(grad_hat, hat, rstd):
    return rstd * (
        grad_hat
        - jnp.mean(grad_hat, axis=-1, keepdims=True)
        - hat * jnp.mean(grad_hat * hat, axis=-1, keepdims=True)
    )


def gelu_both(v):
    inner = 0.7978845608028654 * (v + 0.044715 * v * v * v)
    t = jnp.tanh(inner)
    value = 0.5 * v * (1.0 + t)
    slope = 0.5 * (1.0 + t) + 0.5 * v * (1.0 - t * t) * 0.7978845608028654 * (1.0 + 3 * 0.044715 * v * v)
    return value, slope


def einf(spec, a, b):
    return jnp.einsum(spec, a, b, preferred_element_type=f32)


def shards(size, inputs, doc_ids, gain_attn, w_qkv, w_out, gain_mlp, w_up, w_down, grad_out):
    me = lax.axis_index("dp")
    z = lax.axis_index("tensor")
    odd = me & 1
    others = [1 << k for k in range(1, size.bit_length() - 1)]
    documents = doc_ids[0]
    tokens, dim = inputs.shape
    rows = dim // size
    hid = w_up.shape[1]
    half = hid // 2
    width = w_out.shape[0]
    scal = jnp.stack([z, jnp.sum(documents < 1), jnp.sum(documents < 2)]).astype(jnp.int32)

    pieces = [ring_gather(inputs[k : k + BLOCK]) for k in range(0, tokens, BLOCK)]

    gains = jnp.stack([gain_attn, gain_mlp])
    own = jnp.concatenate([w_qkv[0], w_qkv[1], w_qkv[2], jnp.pad(gains, ((0, 62), (0, 0))).T], axis=1)
    order = others + [1]
    spread_qkv = spread_blocks(own[None], order, size)
    full = jnp.concatenate([pick(spread_qkv, place_of(me ^ b, order)) for b in range(size)])
    full_qkv = full[:, : 3 * width]
    gain_one = full[:, 3 * width].astype(f32)
    gain_two = full[:, 3 * width + 1].astype(f32)

    out_rows = jnp.concatenate([w_out.T[: rows // 2], w_out.T[rows // 2 :]], axis=1)

    def pair_half(w):
        parts = w.reshape(rows, 2, half)
        return jnp.concatenate([pick(parts, odd, 1), swap(pick(parts, 1 - odd, 1), "dp", 1, size)])

    pack_a = jnp.concatenate([pair_half(w_up), out_rows])
    pack_b = pair_half(w_down.T)
    ring_a = jnp.stack(ring_gather(pack_a))
    ring_b = jnp.stack(ring_gather(pack_b))
    order_b = others[::-1]
    spread_a = spread_blocks(ring_a[None], others, size)
    spread_b = spread_blocks(ring_b[None], order_b, size)

    def assemble(spread_w, bits):
        blocks = []
        for b in range(size):
            mask = me ^ b
            block = pick(spread_w, place_of(mask, bits))[:, : 2 * rows]
            block = pick(block.reshape(RING, 2, rows, half), mask & 1, 1)
            blocks.append(block.transpose(1, 0, 2).reshape(rows, RING * half))
        return jnp.concatenate(blocks)

    full_up = assemble(spread_a, others)
    full_down = assemble(spread_b, order_b)
    out_part = spread_a[:, :, 2 * rows :]
    out_both = jnp.stack([out_part, swap(out_part, "dp", 1, size)])

    def out_block(b):
        mask = me ^ b
        block = pick(pick(out_both, mask & 1), place_of(mask, others))
        block = jnp.concatenate([block[..., :width], block[..., width:]], axis=1)
        return block.transpose(1, 0, 2).reshape(rows, RING * width)

    full_out = jnp.concatenate([out_block(b) for b in range(size)])
    grad_both = jnp.concatenate([grad_out, swap(grad_out, "dp", 1, size)])
    grad_active = einf("td,df->tf", grad_both, full_down)

    normed = []
    parts = []
    for s in range(RING):
        for piece in pieces:
            hat, _ = centre(piece[s].astype(f32))
            normed.append((hat * gain_one).astype(bf16))
            parts.append(einf("de,td->et", full_qkv, normed[-1]).astype(bf16))
    normed = jnp.concatenate(normed)
    sent, lse = attn_fwd(scal, parts)
    attended = jnp.concatenate([sent[0]] + [turn(sent[s], s) for s in range(1, RING)])
    mixed = inputs.astype(f32) + einf("et,de->td", attended, full_out)
    hat_two, rstd_two = centre(mixed)
    mlp_rows = (hat_two * gain_two).astype(bf16)
    mlp_both = jnp.concatenate([mlp_rows, swap(mlp_rows, "dp", 1, size)])
    hidden = einf("td,df->tf", mlp_both, full_up)
    value, slope = gelu_both(hidden)
    active = value.astype(bf16)
    grad_hidden = (grad_active * slope).astype(bf16)
    grad_part = einf("tf,df->td", grad_hidden, full_up)
    grad_mlp = grad_part[:tokens] + swap(grad_part[tokens:].astype(bf16), "dp", 1, size).astype(f32)
    grad_mixed = grad_out.astype(f32) + norm_back(grad_mlp * gain_two, hat_two, rstd_two)
    grad_branch = grad_mixed.astype(bf16)
    grad_att = einf("de,td->et", full_out, grad_branch).astype(bf16).reshape(RING, width, tokens)
    grads = [grad_att[0]] + [turn(grad_att[s], -s) for s in range(1, RING)]

    out_pair = einf("tf,df->td", active, full_down)
    layer_out = (
        mixed + out_pair[:tokens] + swap(out_pair[tokens:].astype(bf16), "dp", 1, size).astype(f32)
    ).astype(bf16)

    bits = [1 << k for k in reversed(range(size.bit_length() - 1))]

    def scatter(grad, stages, last_width):
        blocks, left = grad.reshape(size, rows, grad.shape[1]), list(bits)
        for bit in stages:
            blocks, left = halve(blocks, left, bit, me, size)
        blocks = blocks.reshape(-1, blocks.shape[-1])
        return ring_reduce([blocks[:, s * last_width : (s + 1) * last_width] for s in range(RING)])

    def pair_whole(block):
        block = block.reshape(2, rows, half)
        send = pick(block, 1 - odd).astype(bf16)
        keep = pick(block, odd)
        other = swap(send, "dp", 1, size).astype(f32)
        return jnp.where(odd == 0, jnp.concatenate([keep, other], axis=1), jnp.concatenate([other, keep], axis=1))

    grad_down = pair_whole(scatter(einf("td,tf->df", grad_both, active), others, half)).T
    grad_up = pair_whole(scatter(einf("td,tf->df", mlp_both, grad_hidden), order_b, half))
    grad_o = scatter(einf("td,et->de", grad_branch, attended), [1] + order_b, width).T

    grad_parts = attn_bwd(scal, parts, sent, grads, lse)
    grad_proj = einf("td,et->de", normed, grad_parts)
    blocks, left = grad_proj.reshape(size, rows, 3 * width), list(bits)
    for bit in [1] + order_b:
        blocks, left = halve(blocks, left, bit, me, size)
    grad_qkv = blocks[0].reshape(rows, 3, width).transpose(1, 0, 2)

    back = []
    for k in range(0, tokens, BLOCK):
        back.append(
            ring_reduce(
                [
                    einf("et,de->td", grad_parts[:, s * tokens + k : s * tokens + k + BLOCK], full_qkv)
                    for s in range(RING)
                ]
            )
        )
    grad_normed = jnp.concatenate(back)
    hat_one, rstd_one = centre(inputs.astype(f32))
    grad_inputs = grad_mixed + norm_back(grad_normed * gain_one, hat_one, rstd_one)

    sums = jnp.stack(
        [
            jnp.sum(w_qkv.astype(f32) * grad_qkv, axis=(0, 2)),
            jnp.sum(w_up.astype(f32) * grad_up, axis=1),
        ]
    )
    for bit in (1, 2):
        sums = sums + swap(sums, "tensor", bit, RING)
    sums = sums / gains.astype(f32)
    return layer_out, grad_inputs, sums[0], grad_qkv, grad_o, sums[1], grad_up, grad_down


def solution(mesh):
    both = P(("dp", "tensor"), None)
    weights = (P(None, "dp", "tensor"), P("tensor", "dp"), P("dp"), P("dp", "tensor"), P("tensor", "dp"))
    return jax.shard_map(
        functools.partial(shards, mesh.shape["dp"]),
        mesh=mesh,
        in_specs=(both, P("dp", None), P("dp"), *weights, both),
        out_specs=(both, both, P("dp"), *weights),
        check_vma=False,
    )
```

```python
import functools

import jax
import jax.numpy as jnp
from jax import lax
from jax.experimental import pallas as pl
from jax.experimental.pallas import tpu as pltpu
from jax.sharding import PartitionSpec as P

HEAD_DIM = 64
BLOCK = 256
PAD = 256
RING = 4
EPS = 1e-05
LOG2E = 1.4426950408889634
f32 = jnp.float32
bf16 = jnp.bfloat16
HIDE = -1e30


def nn(a, b):
    return lax.dot_general(a, b, (((1,), (0,)), ((), ())), preferred_element_type=f32)


def nt(a, b):
    return lax.dot_general(a, b, (((1,), (1,)), ((), ())), preferred_element_type=f32)


def doc_of(place, ends):
    return jnp.where(place >= ends[1], 2, jnp.where(place >= ends[0], 1, 0))


def doc_start(row, ends):
    return jnp.where(row >= ends[1], ends[1], jnp.where(row >= ends[0], ends[0], 0))


def hidden_bias(i, j, ends):
    keys = j * BLOCK + lax.broadcasted_iota(jnp.int32, (BLOCK, BLOCK), 0)
    rows = i * BLOCK + lax.broadcasted_iota(jnp.int32, (1, BLOCK), 1)
    start = doc_start(rows, ends)
    stop = jnp.where(rows >= ends[1], 1 << 30, jnp.where(rows >= ends[0], ends[1], ends[0]))
    return jnp.where((keys >= start) & (keys < stop), 0.0, HIDE)


def signed(s, size):
    low = size.astype(bf16)
    return jnp.clip(s.astype(bf16) * bf16(1e38), -low, low)


def ring_blocks(z, count):
    for n in range(count):
        yield n, lax.rem(z - n // 2 + RING, RING) * 2 + n % 2


def walk(i, ends, step, carry):
    def body(j, carry):
        mixed = doc_of(j * BLOCK, ends) != doc_of(i * BLOCK + BLOCK - 1, ends)
        return lax.cond(mixed, lambda c: step(j, c, hidden_bias(i, j, ends)), lambda c: step(j, c, None), carry)

    first = lax.div(doc_start(i * BLOCK, ends), BLOCK)
    return lax.fori_loop(first, i + 1, body, carry)


def head_rows(h, base=0):
    return slice(base + h * HEAD_DIM, base + (h + 1) * HEAD_DIM)


def two_parts(q):
    scaled = q.astype(f32) * (0.125 * LOG2E)
    high = scaled.astype(bf16)
    return high, (scaled - high.astype(f32)).astype(bf16)


def twice(k):
    return jnp.concatenate([k, k], axis=0).T


CHUNK = 64


def chunks():
    return [slice(r, r + CHUNK) for r in range(0, BLOCK, CHUNK)]


def size_of(s, bias, rows):
    a = jnp.abs(s)
    return a if bias is None else a + bias[rows]


def attn_fwd_body(scal, *refs):
    parts, (out, lse, qs, vs, ks, acc, held, low) = refs[:-8], refs[-8:]
    i = pl.program_id(0)
    heads, width = ks.shape[0], vs.shape[1]
    z = scal[0]
    ends = (scal[1], scal[2])

    @pl.when(i == 0)
    def _():
        for n, b in ring_blocks(z, len(parts)):
            ref = parts[n]
            vs[b] = ref[2 * PAD : 2 * PAD + width]
            for h in range(heads):
                high, rest = two_parts(ref[head_rows(h)])
                qs[h, b, 0:HEAD_DIM] = high
                qs[h, b, HEAD_DIM : 2 * HEAD_DIM] = rest
                ks[h, b] = twice(ref[head_rows(h, PAD)])

    acc[...] = jnp.zeros_like(acc)

    def largest(j, carry, bias):
        new = []
        for h in range(heads):
            s = nn(ks[h, j], qs[h, i])
            held[h, j] = s
            top = carry[h]
            for rows in chunks():
                top = jnp.maximum(top, jnp.max(size_of(s[rows], bias, rows).reshape(-1, 8, BLOCK), axis=0))
            new.append(top)
        return tuple(new)

    zero = jnp.zeros((8, BLOCK), f32)
    tops = walk(i, ends, largest, (zero,) * heads)
    tops = [jnp.max(t, axis=0, keepdims=True) for t in tops]

    def weigh(j, carry, bias):
        new = []
        for h in range(heads):
            total = carry[h]
            for rows in chunks():
                s = held[h, j, rows]
                p = jnp.exp2(size_of(s, bias, rows) - tops[h])
                total = total + jnp.sum(p.reshape(-1, 8, BLOCK), axis=0)
                low[h, rows] = signed(s, p)
            new.append(total)
        for h in range(heads):
            acc[head_rows(h)] += nn(vs[j, head_rows(h)], low[h])
        return tuple(new)

    totals = walk(i, ends, weigh, (zero,) * heads)
    t = lax.div(i, 2)
    cols = pl.ds(pl.multiple_of(lax.rem(i, 2) * BLOCK, BLOCK), BLOCK)
    dest = lax.rem(t - z + RING, RING)
    for h in range(heads):
        l = jnp.sum(totals[h], axis=0, keepdims=True)
        out[dest, head_rows(h), cols] = (acc[head_rows(h)] / l).astype(bf16)
        lse[i, h : h + 1, :] = tops[h] + jnp.log(l) * LOG2E


def whole(shape):
    return pl.BlockSpec(shape, lambda *_: (0,) * len(shape))


def sds(shape, dtype=bf16):
    return jax.ShapeDtypeStruct(shape, dtype)


def attn_fwd(scal, parts, heads):
    nb = len(parts)
    width, cols = heads * HEAD_DIM, nb // RING * BLOCK
    return pl.pallas_call(
        attn_fwd_body,
        out_shape=(sds((RING, width, cols)), sds((nb, 8, BLOCK), f32)),
        grid_spec=pltpu.PrefetchScalarGridSpec(
            num_scalar_prefetch=1,
            grid=(nb,),
            in_specs=[whole(p.shape) for p in parts],
            out_specs=(whole((RING, width, cols)), whole((nb, 8, BLOCK))),
            scratch_shapes=[
                pltpu.VMEM((heads, nb, 2 * HEAD_DIM, BLOCK), bf16),
                pltpu.VMEM((nb, width, BLOCK), bf16),
                pltpu.VMEM((heads, nb, BLOCK, 2 * HEAD_DIM), bf16),
                pltpu.VMEM((width, BLOCK), f32),
                pltpu.VMEM((heads, nb, BLOCK, BLOCK), f32),
                pltpu.VMEM((heads, BLOCK, BLOCK), bf16),
            ],
        ),
        compiler_params=pltpu.CompilerParams(dimension_semantics=("arbitrary",)),
        cost_estimate=pl.CostEstimate(flops=5_000_000_000, bytes_accessed=4_000_000, transcendentals=0),
        name="attn_fwd",
    )(scal, *parts)


def attn_bwd_body(scal, *refs):
    parts, refs = refs[:-21], refs[-21:]
    o, g0, g1, g2, g3, lse, grad, q2, qs, kts, gs, ks, vns, inner, dq, dk, dv, held, push, low, dlow = refs
    i = pl.program_id(0)
    nb = pl.num_programs(0)
    heads, width = ks.shape[0], qs.shape[1]
    z = scal[0]
    ends = (scal[1], scal[2])

    @pl.when(i == 0)
    def _():
        for n, b in ring_blocks(z, len(parts)):
            ref = parts[n]
            qs[b] = ref[0:width] * bf16(0.125)
            kts[b] = ref[PAD : PAD + width]
            for h in range(heads):
                high, low = two_parts(ref[head_rows(h)])
                q2[h, b, 0:HEAD_DIM] = high
                q2[h, b, HEAD_DIM : 2 * HEAD_DIM] = low
                ks[h, b] = twice(ref[head_rows(h, PAD)])
                vns[h, b] = ref[head_rows(h, 2 * PAD)].T
        for s, ref in enumerate((g0, g1, g2, g3)):
            t = lax.rem(z + s, RING)
            for half in range(2):
                cols = slice(half * BLOCK, (half + 1) * BLOCK)
                gs[t * 2 + half] = ref[:, cols]
                both = ref[:, cols].astype(f32) * o[s, :, cols].astype(f32)
                for h in range(heads):
                    inner[t * 2 + half, h : h + 1, :] = jnp.sum(both[head_rows(h)], axis=0, keepdims=True)
        dk[...] = jnp.zeros_like(dk)
        dv[...] = jnp.zeros_like(dv)

    dq[i] = jnp.zeros(dq.shape[1:], f32)

    bounds, levers = [], []
    for h in range(heads):
        part = inner[i, h : h + 1, :]
        bounds.append(jnp.abs(part))
        levers.append(jnp.where(part < 0, -1e38, 1e38))

    def products(j, h):
        held[h] = nn(ks[h, j], q2[h, i])
        push[h] = nn(vns[h, j], gs[i, head_rows(h)])

    def step(j, carry, bias):
        products(j, 0)
        for h in range(heads):
            if h + 1 < heads:
                products(j, h + 1)
            for rows in chunks():
                s = held[h, rows]
                mag = jnp.exp2(size_of(s, bias, rows) - lse[i, h : h + 1, :])
                low[h, rows] = signed(s, mag)
                ds = mag * (push[h, rows] - jnp.clip(s * levers[h], -bounds[h], bounds[h]))
                dlow[h, rows] = ds.astype(bf16)
            rows = head_rows(h)
            dv[j, rows] += nt(gs[i, rows], low[h])
            dk[j, rows] += nt(qs[i, rows], dlow[h])
            dq[i, rows] += nn(kts[j, rows], dlow[h])
        return carry

    walk(i, ends, step, 0)

    @pl.when(i == nb - 1)
    def _():
        grad[...] = jnp.zeros_like(grad)
        for n, b in ring_blocks(z, len(parts)):
            cols = slice(n * BLOCK, (n + 1) * BLOCK)
            grad[0:width, cols] = (dq[b] * 0.125).astype(bf16)
            grad[PAD : PAD + width, cols] = dk[b].astype(bf16)
            grad[2 * PAD : 2 * PAD + width, cols] = dv[b].astype(bf16)


def attn_bwd(scal, parts, attended, grads, lse):
    nb = len(parts)
    width = attended.shape[1]
    heads = width // HEAD_DIM
    ops = (*parts, attended, *grads, lse)
    result = (3 * PAD, nb * BLOCK)
    return pl.pallas_call(
        attn_bwd_body,
        out_shape=sds(result),
        grid_spec=pltpu.PrefetchScalarGridSpec(
            num_scalar_prefetch=1,
            grid=(nb,),
            in_specs=[whole(p.shape) for p in ops],
            out_specs=whole(result),
            scratch_shapes=[
                pltpu.VMEM((heads, nb, 2 * HEAD_DIM, BLOCK), bf16),
                pltpu.VMEM((nb, width, BLOCK), bf16),
                pltpu.VMEM((nb, width, BLOCK), bf16),
                pltpu.VMEM((nb, width, BLOCK), bf16),
                pltpu.VMEM((heads, nb, BLOCK, 2 * HEAD_DIM), bf16),
                pltpu.VMEM((heads, nb, BLOCK, HEAD_DIM), bf16),
                pltpu.VMEM((nb, 8, BLOCK), f32),
                pltpu.VMEM((nb, width, BLOCK), f32),
                pltpu.VMEM((nb, width, BLOCK), f32),
                pltpu.VMEM((nb, width, BLOCK), f32),
                pltpu.VMEM((heads, BLOCK, BLOCK), f32),
                pltpu.VMEM((heads, BLOCK, BLOCK), f32),
                pltpu.VMEM((heads, BLOCK, BLOCK), bf16),
                pltpu.VMEM((heads, BLOCK, BLOCK), bf16),
            ],
        ),
        compiler_params=pltpu.CompilerParams(dimension_semantics=("arbitrary",)),
        cost_estimate=pl.CostEstimate(flops=8_000_000_000, bytes_accessed=8_000_000, transcendentals=0),
        name="attn_bwd",
    )(scal, *ops)


LANE = 128


def call(body, outs, *ops, scratch=(), name=None, flops=1_000_000):
    near = pl.BlockSpec(memory_space=pltpu.VMEM)
    return pl.pallas_call(
        body,
        out_shape=tuple(outs),
        in_specs=[near] * len(ops),
        out_specs=(near,) * len(outs),
        scratch_shapes=list(scratch),
        cost_estimate=pl.CostEstimate(flops=flops, bytes_accessed=100_000, transcendentals=0),
        name=name,
    )(*ops)


def aligned(x, n):
    return pl.multiple_of(x, n)


def after(x, *others):
    return lax.optimization_barrier((x, *others))[0]


def mine_of(k):
    return lax.div(lax.axis_index("dp"), 1 << k) & 1


def pack_body(w_qkv, gain_a, gain_m, w_up, w_down, w_out, qkv, keep, give):
    rows, half = w_up.shape[0], w_up.shape[1] // 2
    width = w_out.shape[0]
    mine = mine_of(0)
    qkv[...] = jnp.zeros_like(qkv)
    for c in range(3):
        qkv[:, c * PAD : c * PAD + width] = w_qkv[c]
    eye = lax.broadcasted_iota(jnp.int32, (rows, rows), 0) == lax.broadcasted_iota(jnp.int32, (rows, rows), 1)
    lane = lax.broadcasted_iota(jnp.int32, (rows, LANE), 1)
    cols = [jnp.sum(jnp.where(eye, g[...].astype(f32), 0.0), axis=1, keepdims=True) for g in (gain_a, gain_m)]
    qkv[:, 3 * PAD :] = jnp.where(lane == 0, cols[0], jnp.where(lane == 1, cols[1], 0.0)).astype(bf16)
    tiles = half // LANE
    for k in range(tiles):
        for to, which in ((keep, mine), (give, 1 - mine)):
            at = which * half + k * LANE
            to[k * rows : (k + 1) * rows] = w_up[:, pl.ds(aligned(at, LANE), LANE)]
            to[(tiles + k) * rows : (tiles + k + 1) * rows] = w_down[pl.ds(aligned(at, LANE), LANE), :].T
    base = 2 * tiles * rows
    back = w_out[...].astype(f32).T.astype(bf16)
    keep[base : base + rows] = back[:, 0:LANE]
    keep[base + rows : base + 2 * rows] = jnp.zeros((rows, LANE), bf16)
    keep[base + rows : base + 2 * rows, 0 : width - LANE] = back[:, LANE:width]


def unpack_qkv_body(near, far, w, gains):
    me = lax.axis_index("dp")
    rows = near.shape[1]
    count = near.shape[0]
    tail = []
    for p in range(2 * count):
        src = near if p < count else far
        mask = 2 * (p % count) + (1 if p >= count else 0)
        w[pl.ds(aligned((me ^ mask) * rows, 32), rows)] = src[p % count, :, : 3 * PAD]
    for b in range(2 * count):
        mask = me ^ b
        part = lax.div(mask, 2)
        col = jnp.where(
            (mask & 1) == 0, near[part, :, 3 * PAD :].astype(f32), far[part, :, 3 * PAD :].astype(f32)
        )
        tail.append(col)
    gains[...] = jnp.concatenate(tail, axis=0).T[0:8]


def norm_qkv_body(xa, xb, w, gains, normed, qa, qb):
    for half, (x, q) in enumerate(((xa, qa), (xb, qb))):
        size = x.shape[0]

        for r in range(0, size, 64):
            v = x[r : r + 64].astype(f32)
            c = v - jnp.mean(v, axis=-1, keepdims=True)
            rstd = lax.rsqrt(jnp.mean(c * c, axis=-1, keepdims=True) + EPS)
            normed[half * size + r : half * size + r + 64] = (c * rstd * gains[0:1]).astype(bf16)

        q[...] = nn(normed[half * size : (half + 1) * size], w[...]).astype(bf16).T


def stack_body(p0, p1, p2, p3, a, b):
    u = b.shape[1] // 2
    for s, p in enumerate((p0, p1, p2, p3)):
        a[s, 0:u] = p[0:u]
        b[s, 0:u] = p[u : 2 * u]
        a[s, u : 2 * u] = p[2 * u : 3 * u]
        b[s, u : 2 * u] = p[3 * u : 4 * u]
        a[s, 2 * u :] = p[4 * u :]


def unpack_body(*refs):
    ups, downs, (up, down, back) = refs[0:4], refs[4:8], refs[8:11]
    me = lax.axis_index("dp")
    rows = 96
    half = up.shape[1] // RING
    tiles = half // LANE
    span = tiles * rows
    for p in range(4):
        a, b = ups[p], downs[p]
        for rc in range(2):
            to_a = pl.ds(aligned((me ^ (2 * p + rc)) * rows, 32), rows)
            to_b = pl.ds(aligned((me ^ (2 * ((p & 1) * 2 + (p >> 1)) + rc)) * rows, 32), rows)
            for s in range(RING):
                for k in range(tiles):
                    cols = slice(s * half + k * LANE, s * half + (k + 1) * LANE)
                    src = slice(rc * span + k * rows, rc * span + (k + 1) * rows)
                    up[to_a, cols] = a[s, src]
                    down[to_b, cols] = b[s, src]
        where = lax.div(me ^ (2 * p), 2)
        for s in range(RING):
            for k in range(2):
                back[where, s, :, k * LANE : (k + 1) * LANE] = a[s, 2 * span + k * rows : 2 * span + (k + 1) * rows]


def project_body(x, a0, a1, a2, a3, near, far, gains, mixed, mlp, tokens_major, w):
    mine = mine_of(0)
    rows = near.shape[2]
    width = a0.shape[0]
    for b in range(near.shape[0]):
        for s in range(RING):
            w[s, pl.ds(aligned((2 * b + mine) * rows, 32), rows)] = near[b, s]
            w[s, pl.ds(aligned((2 * b + 1 - mine) * rows, 32), rows)] = far[b, s]
    zero = jnp.zeros((PAD - width, a0.shape[1]), bf16)
    for s, a in enumerate((a0, a1, a2, a3)):
        tokens_major[:, s * PAD : (s + 1) * PAD] = jnp.concatenate([a[...], zero], axis=0).T
    for r in range(0, x.shape[0], 128):
        total = x[r : r + 128].astype(f32)
        for s in range(RING):
            total = total + nt(tokens_major[r : r + 128, s * PAD : (s + 1) * PAD], w[s])
        mixed[r : r + 128] = total
    normalise(mixed, gains[1:2], mlp)


def normalise(rows, gain, out):
    for r in range(0, rows.shape[0], 64):
        at = slice(r, r + 64)
        v = rows[at]
        c = v - jnp.mean(v, axis=-1, keepdims=True)
        rstd = lax.rsqrt(jnp.mean(c * c, axis=-1, keepdims=True) + EPS)
        out[at] = (c * rstd * gain).astype(bf16)


def gelu_both(v):
    square = v * v
    t = jnp.tanh(v * (0.7978845608028654 + (0.7978845608028654 * 0.044715) * square))
    gate = 0.5 + 0.5 * t
    bend = v * (2 * 0.7978845608028654 + (6 * 0.7978845608028654 * 0.044715) * square)
    return v * gate, gate + gate * (1.0 - gate) * bend


def mlp_body(x0, x1, g0, g1, up, down, active, grad, hid, push):
    size = x0.shape[0]
    for half, (x, g) in enumerate(((x1, g1), (x0, g0))):
        hid[half] = nn(x[...], up[...])
        push[half] = nn(g[...], down[...])
    for half in range(2):
        for r in range(0, size, 64):
            rows = slice(r, r + 64)
            to = slice((1 - half) * size + r, (1 - half) * size + r + 64)
            value, slope = gelu_both(hid[half, rows])
            active[to] = value.astype(bf16)
            grad[to] = (push[half, rows] * slope).astype(bf16)


def mlp(x0, x1, g0, g1, up, down):
    tokens, dim = x0.shape
    hidden = up.shape[1]
    keep = pl.BlockSpec((tokens, dim), lambda n: (0, 0))
    cols = pl.BlockSpec((dim, BLOCK), lambda n: (0, n))
    wide = pl.BlockSpec((2 * tokens, BLOCK), lambda n: (0, n))
    return pl.pallas_call(
        mlp_body,
        out_shape=(sds((2 * tokens, hidden)), sds((2 * tokens, hidden))),
        grid=(hidden // BLOCK,),
        in_specs=[keep] * 4 + [cols] * 2,
        out_specs=(wide, wide),
        scratch_shapes=[pltpu.VMEM((2, tokens, BLOCK), f32), pltpu.VMEM((2, tokens, BLOCK), f32)],
        cost_estimate=pl.CostEstimate(flops=5_000_000_000, bytes_accessed=4_000_000, transcendentals=0),
        name="mlp",
    )(x0, x1, g0, g1, up, down)


def rows_by_body(a, w, out, *, start):
    for r in range(0, out.shape[0], 128):
        out[r : r + 128] = nt(a[start + r : start + r + 128], w[...]).astype(out.dtype)


def rows_by(a, w, start, count, dtype, name):
    body = functools.partial(rows_by_body, start=start)
    return call(body, [sds((count, w.shape[0]), dtype)], a, w, name=name)[0]


def norm_back(v, gain, grad):
    c = v - jnp.mean(v, axis=-1, keepdims=True)
    rstd = lax.rsqrt(jnp.mean(c * c, axis=-1, keepdims=True) + EPS)
    hat = c * rstd
    g = grad * gain
    return rstd * (g - jnp.mean(g, axis=-1, keepdims=True) - hat * jnp.mean(g * hat, axis=-1, keepdims=True))


def branch_body(mixed, part, far, grad_out, gains, w, grad_mixed, branch, heads):
    for r in range(0, mixed.shape[0], 64):
        at = slice(r, r + 64)
        grad = part[at] + far[at].astype(f32)
        total = grad_out[at].astype(f32) + norm_back(mixed[at], gains[1:2], grad)
        grad_mixed[at] = total
        branch[at] = total.astype(bf16)

    width = heads.shape[1]
    for s in range(RING):
        heads[s] = nn(branch[...], w[s]).astype(bf16).T[0:width]


def back_body(grad, w, out, *, blocks):
    for k, n in enumerate(blocks):
        out[k] = nt(grad[:, n * BLOCK : (n + 1) * BLOCK].T, w[...]).astype(bf16)


def finish_body(part, recv, x, grad_mixed, gains, out):
    for r in range(0, x.shape[0], 64):
        at = slice(r, r + 64)
        grad = part[at].astype(f32) + recv[at].astype(f32)
        out[at] = grad_mixed[at] + norm_back(x[at].astype(f32), gains[0:1], grad)


def turn(x, shift):
    return lax.ppermute(x, "tensor", [(i, (i + shift) % RING) for i in range(RING)])


def swap(x, axis, bit, size):
    return lax.ppermute(x, axis, [(i, i ^ bit) for i in range(size)])


def pick(x, index, axis=0):
    return lax.dynamic_index_in_dim(x, index, axis, keepdims=False)


def ring_gather(x):
    got = [x]
    for _ in range(RING - 1):
        got.append(turn(got[-1], 1))
    return got


def ring_reduce(chunks):
    moving = chunks[1].astype(bf16)
    for r in range(1, RING):
        moved = turn(moving, 1)
        total = moved.astype(f32) + chunks[(r + 1) % RING]
        moving = total.astype(bf16)
    return total


def spread_blocks(x, bits, size):
    for bit in bits:
        x = jnp.concatenate([x, swap(x, "dp", bit, size)])
    return x


def place_of(mask, bits):
    place = 0
    for k, bit in enumerate(bits):
        place = place + jnp.where(mask & bit != 0, 1 << k, 0)
    return place


def halve(blocks, left, bit, me, size):
    at = left.index(bit)
    lead, tail = 1 << at, 1 << (len(left) - at - 1)
    split = blocks.reshape((lead, 2, tail) + blocks.shape[1:])
    mine = jnp.where(me & bit != 0, 1, 0)
    send = pick(split, 1 - mine, 1).astype(bf16)
    keep = pick(split, mine, 1)
    total = keep.astype(f32) + swap(send, "dp", bit, size).astype(f32)
    return total.reshape((lead * tail,) + blocks.shape[1:]), [b for b in left if b != bit]


def centre(rows):
    shifted = rows - jnp.mean(rows, axis=-1, keepdims=True)
    rstd = lax.rsqrt(jnp.mean(shifted * shifted, axis=-1, keepdims=True) + EPS)
    return shifted * rstd, rstd


def norm_back_plain(grad_hat, hat, rstd):
    return rstd * (
        grad_hat
        - jnp.mean(grad_hat, axis=-1, keepdims=True)
        - hat * jnp.mean(grad_hat * hat, axis=-1, keepdims=True)
    )


def einf(spec, a, b):
    return jnp.einsum(spec, a, b, preferred_element_type=f32)


def shards(size, inputs, doc_ids, gain_attn, w_qkv, w_out, gain_mlp, w_up, w_down, grad_out):
    me = lax.axis_index("dp")
    z = lax.axis_index("tensor")
    odd = me & 1
    others = [1 << k for k in range(1, size.bit_length() - 1)]
    documents = doc_ids[0]
    tokens, dim = inputs.shape
    rows = dim // size
    hid = w_up.shape[1]
    half = hid // 2
    width = w_out.shape[0]
    scal = jnp.stack([z, jnp.sum(documents < 1), jnp.sum(documents < 2)]).astype(jnp.int32)

    pieces = [ring_gather(inputs[k : k + BLOCK]) for k in range(0, tokens, BLOCK)]

    gains = jnp.stack([gain_attn, gain_mlp])
    own = jnp.concatenate([w_qkv[0], w_qkv[1], w_qkv[2], jnp.pad(gains, ((0, 62), (0, 0))).T], axis=1)
    order = others + [1]
    spread_qkv = spread_blocks(own[None], order, size)
    full = jnp.concatenate([pick(spread_qkv, place_of(me ^ b, order)) for b in range(size)])
    full_qkv = full[:, : 3 * width]
    gain_one = full[:, 3 * width].astype(f32)
    gain_two = full[:, 3 * width + 1].astype(f32)

    out_rows = jnp.concatenate([w_out.T[: rows // 2], w_out.T[rows // 2 :]], axis=1)

    def pair_half(w):
        parts = w.reshape(rows, 2, half)
        return jnp.concatenate([pick(parts, odd, 1), swap(pick(parts, 1 - odd, 1), "dp", 1, size)])

    pack_a = jnp.concatenate([pair_half(w_up), out_rows])
    pack_b = pair_half(w_down.T)
    ring_a = jnp.stack(ring_gather(pack_a))
    ring_b = jnp.stack(ring_gather(pack_b))
    order_b = others[::-1]
    spread_a = spread_blocks(ring_a[None], others, size)
    spread_b = spread_blocks(ring_b[None], order_b, size)

    def assemble(spread_w, bits):
        blocks = []
        for b in range(size):
            mask = me ^ b
            block = pick(spread_w, place_of(mask, bits))[:, : 2 * rows]
            block = pick(block.reshape(RING, 2, rows, half), mask & 1, 1)
            blocks.append(block.transpose(1, 0, 2).reshape(rows, RING * half))
        return jnp.concatenate(blocks)

    full_up = assemble(spread_a, others)
    full_down = assemble(spread_b, order_b)
    out_part = spread_a[:, :, 2 * rows :]
    out_both = jnp.stack([out_part, swap(out_part, "dp", 1, size)])

    def out_block(b):
        mask = me ^ b
        block = pick(pick(out_both, mask & 1), place_of(mask, others))
        block = jnp.concatenate([block[..., :width], block[..., width:]], axis=1)
        return block.transpose(1, 0, 2).reshape(rows, RING * width)

    full_out = jnp.concatenate([out_block(b) for b in range(size)])
    grad_both = jnp.concatenate([grad_out, swap(grad_out, "dp", 1, size)])
    grad_active = einf("td,df->tf", grad_both, full_down)

    normed = []
    parts = []
    for s in range(RING):
        for piece in pieces:
            hat, _ = centre(piece[s].astype(f32))
            normed.append((hat * gain_one).astype(bf16))
            part = einf("de,td->et", full_qkv, normed[-1]).astype(bf16).reshape(3, width, BLOCK)
            parts.append(jnp.pad(part, ((0, 0), (0, PAD - width), (0, 0))).reshape(3 * PAD, BLOCK))
    normed = jnp.concatenate(normed)
    sent, lse = attn_fwd(scal, parts, width // HEAD_DIM)
    attended = jnp.concatenate([sent[0]] + [turn(sent[s], s) for s in range(1, RING)])
    mixed = inputs.astype(f32) + einf("et,de->td", attended, full_out)
    hat_two, rstd_two = centre(mixed)
    mlp_rows = (hat_two * gain_two).astype(bf16)
    mlp_both = jnp.concatenate([mlp_rows, swap(mlp_rows, "dp", 1, size)])
    hidden = einf("td,df->tf", mlp_both, full_up)
    value, slope = gelu_both(hidden)
    active = value.astype(bf16)
    grad_hidden = (grad_active * slope).astype(bf16)
    grad_part = einf("tf,df->td", grad_hidden, full_up)
    grad_mlp = grad_part[:tokens] + swap(grad_part[tokens:].astype(bf16), "dp", 1, size).astype(f32)
    grad_mixed = grad_out.astype(f32) + norm_back_plain(grad_mlp * gain_two, hat_two, rstd_two)
    grad_branch = grad_mixed.astype(bf16)
    grad_att = einf("de,td->et", full_out, grad_branch).astype(bf16).reshape(RING, width, tokens)
    grads = [grad_att[0]] + [turn(grad_att[s], -s) for s in range(1, RING)]

    out_pair = einf("tf,df->td", active, full_down)
    layer_out = (
        mixed + out_pair[:tokens] + swap(out_pair[tokens:].astype(bf16), "dp", 1, size).astype(f32)
    ).astype(bf16)

    bits = [1 << k for k in reversed(range(size.bit_length() - 1))]

    def scatter(grad, stages, last_width):
        blocks, left = grad.reshape(size, rows, grad.shape[1]), list(bits)
        for bit in stages:
            blocks, left = halve(blocks, left, bit, me, size)
        blocks = blocks.reshape(-1, blocks.shape[-1])
        return ring_reduce([blocks[:, s * last_width : (s + 1) * last_width] for s in range(RING)])

    def pair_whole(block):
        block = block.reshape(2, rows, half)
        send = pick(block, 1 - odd).astype(bf16)
        keep = pick(block, odd)
        other = swap(send, "dp", 1, size).astype(f32)
        return jnp.where(odd == 0, jnp.concatenate([keep, other], axis=1), jnp.concatenate([other, keep], axis=1))

    grad_down = pair_whole(scatter(einf("td,tf->df", grad_both, active), others, half)).T
    grad_up = pair_whole(scatter(einf("td,tf->df", mlp_both, grad_hidden), order_b, half))
    grad_o = scatter(einf("td,et->de", grad_branch, attended), [1] + order_b, width).T

    grad_parts = attn_bwd(scal, parts, sent, grads, lse)
    grad_parts = grad_parts.reshape(3, PAD, -1)[:, :width].reshape(3 * width, -1)
    grad_proj = einf("td,et->de", normed, grad_parts)
    blocks, left = grad_proj.reshape(size, rows, 3 * width), list(bits)
    for bit in [1] + order_b:
        blocks, left = halve(blocks, left, bit, me, size)
    grad_qkv = blocks[0].reshape(rows, 3, width).transpose(1, 0, 2)

    back = []
    for k in range(0, tokens, BLOCK):
        back.append(
            ring_reduce(
                [
                    einf("et,de->td", grad_parts[:, s * tokens + k : s * tokens + k + BLOCK], full_qkv)
                    for s in range(RING)
                ]
            )
        )
    grad_normed = jnp.concatenate(back)
    hat_one, rstd_one = centre(inputs.astype(f32))
    grad_inputs = grad_mixed + norm_back_plain(grad_normed * gain_one, hat_one, rstd_one)

    sums = jnp.stack(
        [
            jnp.sum(w_qkv.astype(f32) * grad_qkv, axis=(0, 2)),
            jnp.sum(w_up.astype(f32) * grad_up, axis=1),
        ]
    )
    for bit in (1, 2):
        sums = sums + swap(sums, "tensor", bit, RING)
    sums = sums / gains.astype(f32)
    return layer_out, grad_inputs, sums[0], grad_qkv, grad_o, sums[1], grad_up, grad_down


def add(a, b):
    return (a.astype(f32) + b.astype(f32)).astype(bf16)


def first_body(full, recv, send, keep, *, by_y):
    c = mine_of(0)
    mine = mine_of(2 if by_y else 1)
    for k in range(2):
        for which, to in ((mine, keep), (1 - mine, send)):
            at = which * 2 + k if by_y else k * 2 + which
            to[k] = add(full[at * 2 + c], recv[at])


def second_body(keep_in, recv, send, keep):
    mine = mine_of(1)
    keep[...] = add(keep_in[mine], recv[mine])
    send[...] = add(keep_in[1 - mine], recv[1 - mine])


def third_body(up, far_up, down, far_down, o, far_o, up_send, up_keep, mix_send, mix_keep):
    c, x, y = mine_of(0), mine_of(1), mine_of(2)
    rows = up.shape[1]
    tiles = up.shape[2] // RING // LANE
    span = tiles * rows
    for s in range(RING):
        for rc in range(2):
            side = jnp.bitwise_xor(c, rc)
            for k in range(tiles):
                cols = slice((s * tiles + k) * LANE, (s * tiles + k + 1) * LANE)
                to = slice(rc * span + k * rows, rc * span + (k + 1) * rows)
                for which, out in ((x, up_keep), (1 - x, up_send)):
                    out[s, to] = add(up[y * 4 + which * 2 + side, :, cols], far_up[which * 2 + side, :, cols])
                for which, out in ((y, mix_keep), (1 - y, mix_send)):
                    out[s, to] = add(down[which * 4 + x * 2 + side, :, cols], far_down[which * 2 + side, :, cols])
        for k in range(2):
            cols = slice((s * 2 + k) * LANE, (s * 2 + k + 1) * LANE)
            to = slice(2 * span + k * rows, 2 * span + (k + 1) * rows)
            for which, out in ((y, mix_keep), (1 - y, mix_send)):
                out[s, to] = add(o[which, :, cols], far_o[which, :, cols])


def fourth_body(up, far_up, mix, far_mix, first, rest):
    span = up.shape[1] // 2
    extra = mix.shape[1] - 2 * span
    for s in range(RING):
        for rc in range(2):
            src = slice(rc * span, (rc + 1) * span)
            at = rc * 2 * span
            rest[s, at : at + span] = add(up[s, src], far_up[s, src])
            rest[s, at + span : at + 2 * span] = add(mix[s, src], far_mix[s, src])
        tail = slice(2 * span, 2 * span + extra)
        rest[s, 4 * span : 4 * span + extra] = add(mix[s, tail], far_mix[s, tail])
    first[...] = rest[1]


def fifth_body(mine, far, up, down, o):
    c = mine_of(0)
    rows = up.shape[0]
    half = up.shape[1] // 2
    tiles = half // LANE
    for side, src in ((c, mine), (1 - c, far)):
        for k in range(tiles):
            at = pl.ds(aligned(side * half + k * LANE, LANE), LANE)
            up[:, at] = src[k * rows : (k + 1) * rows].astype(f32)
            down[at, :] = src[(tiles + k) * rows : (tiles + k + 1) * rows].astype(f32).T
    base = 4 * tiles * rows
    width = o.shape[0]
    o[0:LANE] = mine[base : base + rows].astype(f32).T
    o[LANE:width] = mine[base + rows : base + 2 * rows].astype(f32).T[0 : width - LANE]


def shards_small(size, inputs, doc_ids, gain_attn, w_qkv, w_out, gain_mlp, w_up, w_down, grad_out):
    me = lax.axis_index("dp")
    z = lax.axis_index("tensor")
    documents = doc_ids[0]
    tokens, dim = inputs.shape
    rows, hid = w_up.shape
    half = hid // 2
    width = w_out.shape[0]
    heads = width // HEAD_DIM
    hidden = RING * half
    scal = jnp.stack([z, jnp.sum(documents < 1), jnp.sum(documents < 2)]).astype(jnp.int32)

    def pair(x):
        return swap(x, "dp", 1, size)

    def along_x(x):
        return swap(x, "dp", 2, size)

    def along_y(x):
        return swap(x, "dp", 4, size)

    span = half * rows // LANE
    x_a, x_b = ([inputs[k : k + BLOCK]] for k in range(0, tokens, BLOCK))
    x_a.append(turn(x_a[0], 1))
    x_b.append(turn(x_b[0], 1))
    qkv, keep, give = call(
        pack_body,
        [sds((rows, 3 * PAD + LANE)), sds((2 * span + 2 * rows, LANE)), sds((2 * span, LANE))],
        w_qkv, gain_attn[None], gain_mlp[None], w_up, w_down, w_out, name="pack",
    )
    got = pair(give)
    qkv = jnp.stack([qkv, along_x(qkv)])
    packed = jnp.concatenate([keep[: 2 * span], got, keep[2 * span :]])
    ring = [packed, turn(packed, 1)]
    qkv = jnp.concatenate([qkv, along_y(qkv)])
    qkv_far = pair(qkv)
    x_a.append(turn(x_a[1], 1))
    x_b.append(turn(x_b[1], 1))
    ring.append(turn(after(ring[1], x_a[1], x_b[1]), 1))
    full_qkv, gains = call(
        unpack_qkv_body, [sds((dim, 3 * PAD)), sds((8, dim), f32)], qkv, qkv_far, name="unpack_qkv"
    )
    normed, parts = [], []

    def attention_rows(s):
        n, qa, qb = call(
            norm_qkv_body,
            [sds((tokens, dim)), sds((3 * PAD, BLOCK)), sds((3 * PAD, BLOCK))],
            x_a[s], x_b[s], full_qkv, gains, name="norm_qkv",
        )
        normed.append(n)
        parts.extend((qa, qb))
        return n

    attention_rows(0)
    ring.append(turn(after(ring[2], normed[0], x_a[2]), 1))
    grad_far = pair(grad_out)
    attention_rows(1)
    x_a.append(turn(x_a[2], 1))
    x_b.append(turn(x_b[2], 1))
    ups0, downs0 = call(
        stack_body,
        [sds((RING, 2 * span + 2 * rows, LANE)), sds((RING, 2 * span, LANE))],
        *ring[:3], after(ring[3], normed[1], x_b[2]), name="stack",
    )
    ups1, downs1 = along_x(ups0), along_y(downs0)
    ups2, downs2 = along_y(ups0), along_x(downs0)
    attention_rows(2)
    ups3, downs3 = along_y(after(ups1, normed[2])), along_x(after(downs1, normed[2]))
    attention_rows(3)

    sent, lse = attn_fwd(scal, parts, heads)
    attended = [sent[0]] + [turn(sent[s], s) for s in range(1, RING)]
    full_up, full_down, back_near = call(
        unpack_body,
        [sds((dim, hidden)), sds((dim, hidden)), sds((size // 2, RING, rows, PAD))],
        ups0, ups1, ups2, after(ups3, sent), downs0, downs1, downs2, after(downs3, sent), name="unpack",
    )
    back_far = pair(back_near)
    mixed, mlp_rows, att_tokens, full_out = call(
        project_body,
        [sds((tokens, dim), f32), sds((tokens, dim)), sds((tokens, RING * PAD)), sds((RING, dim, PAD))],
        inputs, *attended, back_near, back_far, gains, name="project",
    )
    mlp_far = pair(mlp_rows)
    active, grad_hidden = mlp(mlp_rows, mlp_far, grad_out, grad_far, full_up, full_down)
    part_far = rows_by(grad_hidden, full_up, tokens, tokens, bf16, "part_far")
    part_got = pair(part_far)
    part = rows_by(after(grad_hidden, part_far), full_up, 0, tokens, f32, "part")
    grad_mixed, branch, grad_att = call(
        branch_body,
        [sds((tokens, dim), f32), sds((tokens, dim)), sds((RING, width, tokens))],
        mixed, part, part_got, grad_out, gains, full_out, name="branch",
    )
    grads = [grad_att[0]] + [turn(grad_att[s], -s) for s in range(1, RING)]
    grad_hidden_late = after(grad_hidden, grads[1])
    active_late = after(active, grads[1])
    tokens_late = after(att_tokens, grads[2])

    x_bit, y_bit, c_bit = lax.div(me, 2) & 1, lax.div(me, 4) & 1, me & 1
    both_in = jnp.concatenate([mlp_rows, mlp_far])
    both_grad = jnp.concatenate([grad_out, grad_far])
    grad_up = einf("td,tf->df", both_in, grad_hidden_late).astype(bf16)
    grad_down = einf("td,tf->df", both_grad, active_late).astype(bf16)
    grad_o = einf("td,te->de", branch, tokens_late).astype(bf16)
    far_up = along_y(pick(grad_up.reshape(2, 4, rows, hidden), 1 - y_bit))
    far_down = along_x(pick(grad_down.reshape(2, 2, 2, rows, hidden), 1 - x_bit, 1).reshape(4, rows, hidden))
    far_o = pair(pick(grad_o.reshape(4, 2, rows, RING * PAD), 1 - c_bit, 1))
    o_shape = [sds((2, rows, RING * PAD))] * 2
    o_send, o_keep = call(
        functools.partial(first_body, by_y=False),
        o_shape, grad_o.reshape(size, rows, RING * PAD), far_o, name="first_o",
    )
    layer_far = pair(rows_by(after(active, grads[3]), full_down, tokens, tokens, bf16, "out_far"))
    layer_near = rows_by(after(active, grads[3]), full_down, 0, tokens, f32, "out_near")
    layer_out = (mixed + layer_near + layer_far.astype(f32)).astype(bf16)

    grad_parts = attn_bwd(scal, parts, sent, grads, after(lse, layer_near, o_keep, far_o))
    count = tokens // BLOCK

    def backs(blocks, name):
        return call(
            functools.partial(back_body, blocks=blocks),
            [sds((len(blocks), BLOCK, dim))], grad_parts, full_qkv, name=name,
        )[0]

    start = backs(list(range(count, 2 * count)), "back_first")
    later = backs(list(range(2 * count, RING * count)) + list(range(count)), "back_rest")
    came = [turn(start[k], 1) for k in range(count)]
    up_shape, mix_shape = sds((RING, 2 * span, LANE)), sds((RING, 2 * span + 2 * rows, LANE))
    up_send, up_keep, mix_send, mix_keep = call(
        third_body,
        [up_shape, up_shape, mix_shape, mix_shape],
        grad_up.reshape(size, rows, hidden), after(far_up, came[0]), grad_down.reshape(size, rows, hidden), far_down,
        o_keep, along_x(o_send), name="third",
    )
    came = [turn(add(later[k], came[k]), 1) for k in range(count)]
    total_shape = (4 * span + 2 * rows, LANE)
    moving, rest = call(
        fourth_body,
        [sds(total_shape), sds((RING, *total_shape))],
        up_keep, after(along_x(up_send), came[1]), mix_keep, along_y(mix_send), name="fourth",
    )

    came = [turn(add(later[count + k], came[k]), 1) for k in range(count)]
    grad_inputs = jnp.concatenate(
        [
            call(
                finish_body,
                [sds((BLOCK, dim), f32)],
                later[(RING - 2) * count + k], came[k], inputs[k * BLOCK : (k + 1) * BLOCK],
                grad_mixed[k * BLOCK : (k + 1) * BLOCK], gains, name="finish",
            )[0]
            for k in range(count)
        ]
    )

    grad_proj = einf("td,et->de", jnp.concatenate(normed), grad_parts).astype(bf16)
    far_qkv = pair(pick(grad_proj.reshape(4, 2, rows, 3 * PAD), 1 - c_bit, 1))
    q_send, q_keep = call(
        functools.partial(first_body, by_y=True),
        [sds((2, rows, 3 * PAD))] * 2, grad_proj.reshape(size, rows, 3 * PAD), far_qkv, name="first_qkv",
    )
    q_send, q_keep = call(
        second_body, [sds((rows, 3 * PAD))] * 2, q_keep, along_y(q_send), name="second_qkv"
    )
    grad_flat = q_keep.astype(f32) + along_x(q_send).astype(f32)
    grad_qkv = jnp.stack([grad_flat[:, c * PAD : c * PAD + width] for c in range(3)])

    for r in range(1, RING):
        moving = add(turn(moving, 1), rest[(r + 1) % RING])
    grad_up, grad_down, grad_o = call(
        fifth_body,
        [sds((rows, hid), f32), sds((hid, rows), f32), sds((width, rows), f32)],
        moving, pair(moving[2 * span : 4 * span]), name="fifth",
    )
    sums = jnp.stack(
        [
            jnp.sum(w_qkv.astype(f32) * grad_qkv, axis=(0, 2)),
            jnp.sum(w_up.astype(f32) * grad_up, axis=1),
        ]
    )
    for bit in (1, 2):
        sums = sums + swap(sums, "tensor", bit, RING)
    own = jnp.stack([gain_attn, gain_mlp]).astype(f32)
    sums = sums / own
    return layer_out, grad_inputs, sums[0], grad_qkv, grad_o, sums[1], grad_up, grad_down
def solution(mesh):
    both = P(("dp", "tensor"), None)
    weights = (P(None, "dp", "tensor"), P("tensor", "dp"), P("dp"), P("dp", "tensor"), P("tensor", "dp"))
    return jax.shard_map(
        functools.partial(shards_small if mesh.shape["dp"] == 8 else shards, mesh.shape["dp"]),
        mesh=mesh,
        in_specs=(both, P("dp", None), P("dp"), *weights, both),
        out_specs=(both, both, P("dp"), *weights),
        check_vma=False,
    )
```

```python
import functools

import jax
import jax.numpy as jnp
from jax import lax
from jax.experimental import pallas as pl
from jax.experimental.pallas import tpu as pltpu
from jax.sharding import PartitionSpec as P

HEAD_DIM = 64
BLOCK = 256
PAD = 256
RING = 4
EPS = 1e-05
LOG2E = 1.4426950408889634
f32 = jnp.float32
bf16 = jnp.bfloat16
HIDE = -1e30


def nn(a, b):
    return lax.dot_general(a, b, (((1,), (0,)), ((), ())), preferred_element_type=f32)


def nt(a, b):
    return lax.dot_general(a, b, (((1,), (1,)), ((), ())), preferred_element_type=f32)


def doc_of(place, ends):
    return jnp.where(place >= ends[1], 2, jnp.where(place >= ends[0], 1, 0))


def doc_start(row, ends):
    return jnp.where(row >= ends[1], ends[1], jnp.where(row >= ends[0], ends[0], 0))


def hidden_bias(i, j, ends):
    keys = j * BLOCK + lax.broadcasted_iota(jnp.int32, (BLOCK, BLOCK), 0)
    rows = i * BLOCK + lax.broadcasted_iota(jnp.int32, (1, BLOCK), 1)
    start = doc_start(rows, ends)
    stop = jnp.where(rows >= ends[1], 1 << 30, jnp.where(rows >= ends[0], ends[1], ends[0]))
    return jnp.where((keys >= start) & (keys < stop), 0.0, HIDE)


def signed(s, size):
    low = size.astype(bf16)
    return jnp.clip(s.astype(bf16) * bf16(1e38), -low, low)


def ring_blocks(z, count):
    for n in range(count):
        yield n, lax.rem(z - n // 2 + RING, RING) * 2 + n % 2


def walk(i, ends, step, carry):
    def body(j, carry):
        mixed = doc_of(j * BLOCK, ends) != doc_of(i * BLOCK + BLOCK - 1, ends)
        return lax.cond(mixed, lambda c: step(j, c, hidden_bias(i, j, ends)), lambda c: step(j, c, None), carry)

    first = lax.div(doc_start(i * BLOCK, ends), BLOCK)
    return lax.fori_loop(first, i + 1, body, carry)


def head_rows(h, base=0):
    return slice(base + h * HEAD_DIM, base + (h + 1) * HEAD_DIM)


def two_parts(q):
    scaled = q.astype(f32) * (0.125 * LOG2E)
    high = scaled.astype(bf16)
    return high, (scaled - high.astype(f32)).astype(bf16)


def twice(k):
    return jnp.concatenate([k, k], axis=0).T


CHUNK = 64


def chunks():
    return [slice(r, r + CHUNK) for r in range(0, BLOCK, CHUNK)]


def size_of(s, bias, rows):
    a = jnp.abs(s)
    return a if bias is None else a + bias[rows]


def attn_fwd_body(scal, *refs):
    parts, refs = refs[:-12], refs[-12:]
    outs, (lse, qs, vs, ks, acc, held, low, out) = refs[:RING], refs[RING:]
    i = pl.program_id(0)
    heads, width = ks.shape[0], vs.shape[1]
    z = scal[0]
    ends = (scal[1], scal[2])

    @pl.when(i == 0)
    def _():
        for n, b in ring_blocks(z, len(parts)):
            ref = parts[n]
            vs[b] = ref[2 * PAD : 2 * PAD + width]
            for h in range(heads):
                high, rest = two_parts(ref[head_rows(h)])
                qs[h, b, 0:HEAD_DIM] = high
                qs[h, b, HEAD_DIM : 2 * HEAD_DIM] = rest
                ks[h, b] = twice(ref[head_rows(h, PAD)])

    acc[...] = jnp.zeros_like(acc)

    def largest(j, carry, bias):
        new = []
        for h in range(heads):
            s = nn(ks[h, j], qs[h, i])
            held[h, j] = s
            top = carry[h]
            for rows in chunks():
                top = jnp.maximum(top, jnp.max(size_of(s[rows], bias, rows).reshape(-1, 8, BLOCK), axis=0))
            new.append(top)
        return tuple(new)

    zero = jnp.zeros((8, BLOCK), f32)
    tops = walk(i, ends, largest, (zero,) * heads)
    tops = [jnp.max(t, axis=0, keepdims=True) for t in tops]

    def weigh(j, carry, bias):
        new = []
        for h in range(heads):
            total = carry[h]
            for rows in chunks():
                s = held[h, j, rows]
                p = jnp.exp2(size_of(s, bias, rows) - tops[h])
                total = total + jnp.sum(p.reshape(-1, 8, BLOCK), axis=0)
                low[h, rows] = signed(s, p)
            new.append(total)
        for h in range(heads):
            acc[head_rows(h)] += nn(vs[j, head_rows(h)], low[h])
        return tuple(new)

    totals = walk(i, ends, weigh, (zero,) * heads)
    t = lax.div(i, 2)
    cols = pl.ds(pl.multiple_of(lax.rem(i, 2) * BLOCK, BLOCK), BLOCK)
    dest = lax.rem(t - z + RING, RING)
    for h in range(heads):
        l = jnp.sum(totals[h], axis=0, keepdims=True)
        out[dest, head_rows(h), cols] = (acc[head_rows(h)] / l).astype(bf16)
        lse[i, h : h + 1, :] = tops[h] + jnp.log(l) * LOG2E

    @pl.when(i == pl.num_programs(0) - 1)
    def _():
        for s, ref in enumerate(outs):
            ref[...] = out[s]


def whole(shape):
    return pl.BlockSpec(shape, lambda *_: (0,) * len(shape))


def sds(shape, dtype=bf16):
    return jax.ShapeDtypeStruct(shape, dtype)


def attn_fwd(scal, parts, heads):
    nb = len(parts)
    width, cols = heads * HEAD_DIM, nb // RING * BLOCK
    return pl.pallas_call(
        attn_fwd_body,
        out_shape=(*[sds((width, cols))] * RING, sds((nb, 8, BLOCK), f32)),
        grid_spec=pltpu.PrefetchScalarGridSpec(
            num_scalar_prefetch=1,
            grid=(nb,),
            in_specs=[whole(p.shape) for p in parts],
            out_specs=(*[whole((width, cols))] * RING, whole((nb, 8, BLOCK))),
            scratch_shapes=[
                pltpu.VMEM((heads, nb, 2 * HEAD_DIM, BLOCK), bf16),
                pltpu.VMEM((nb, width, BLOCK), bf16),
                pltpu.VMEM((heads, nb, BLOCK, 2 * HEAD_DIM), bf16),
                pltpu.VMEM((width, BLOCK), f32),
                pltpu.VMEM((heads, nb, BLOCK, BLOCK), f32),
                pltpu.VMEM((heads, BLOCK, BLOCK), bf16),
                pltpu.VMEM((RING, width, cols), bf16),
            ],
        ),
        compiler_params=pltpu.CompilerParams(dimension_semantics=("arbitrary",)),
        cost_estimate=cost("attn_fwd"),
        name="attn_fwd",
    )(scal, *parts)


def attn_bwd_body(scal, *refs):
    parts, refs = refs[:-24], refs[-24:]
    o, refs = refs[:RING], refs[RING:]
    g0, g1, g2, g3, lse, grad, q2, qs, kts, gs, ks, vns, inner, dq, dk, dv, held, push, low, dlow = refs
    i = pl.program_id(0)
    nb = pl.num_programs(0)
    heads, width = ks.shape[0], qs.shape[1]
    z = scal[0]
    ends = (scal[1], scal[2])

    @pl.when(i == 0)
    def _():
        for n, b in ring_blocks(z, len(parts)):
            ref = parts[n]
            qs[b] = ref[0:width] * bf16(0.125)
            kts[b] = ref[PAD : PAD + width]
            for h in range(heads):
                high, low = two_parts(ref[head_rows(h)])
                q2[h, b, 0:HEAD_DIM] = high
                q2[h, b, HEAD_DIM : 2 * HEAD_DIM] = low
                ks[h, b] = twice(ref[head_rows(h, PAD)])
                vns[h, b] = ref[head_rows(h, 2 * PAD)].T
        for s, ref in enumerate((g0, g1, g2, g3)):
            t = lax.rem(z + s, RING)
            for half in range(2):
                cols = slice(half * BLOCK, (half + 1) * BLOCK)
                gs[t * 2 + half] = ref[:, cols]
                both = ref[:, cols].astype(f32) * o[s][:, cols].astype(f32)
                for h in range(heads):
                    inner[t * 2 + half, h : h + 1, :] = jnp.sum(both[head_rows(h)], axis=0, keepdims=True)
        dk[...] = jnp.zeros_like(dk)
        dv[...] = jnp.zeros_like(dv)

    dq[i] = jnp.zeros(dq.shape[1:], f32)

    bounds, levers = [], []
    for h in range(heads):
        part = inner[i, h : h + 1, :]
        bounds.append(jnp.abs(part))
        levers.append(jnp.where(part < 0, -1e38, 1e38))

    def products(j, h):
        held[h] = nn(ks[h, j], q2[h, i])
        push[h] = nn(vns[h, j], gs[i, head_rows(h)])

    def step(j, carry, bias):
        products(j, 0)
        for h in range(heads):
            if h + 1 < heads:
                products(j, h + 1)
            for rows in chunks():
                s = held[h, rows]
                mag = jnp.exp2(size_of(s, bias, rows) - lse[i, h : h + 1, :])
                low[h, rows] = signed(s, mag)
                ds = mag * (push[h, rows] - jnp.clip(s * levers[h], -bounds[h], bounds[h]))
                dlow[h, rows] = ds.astype(bf16)
            rows = head_rows(h)
            dv[j, rows] += nt(gs[i, rows], low[h])
            dk[j, rows] += nt(qs[i, rows], dlow[h])
            dq[i, rows] += nn(kts[j, rows], dlow[h])
        return carry

    walk(i, ends, step, 0)

    @pl.when(i == nb - 1)
    def _():
        grad[...] = jnp.zeros_like(grad)
        for n, b in ring_blocks(z, len(parts)):
            cols = slice(n * BLOCK, (n + 1) * BLOCK)
            grad[0:width, cols] = (dq[b] * 0.125).astype(bf16)
            grad[PAD : PAD + width, cols] = dk[b].astype(bf16)
            grad[2 * PAD : 2 * PAD + width, cols] = dv[b].astype(bf16)


def attn_bwd(scal, parts, attended, grads, lse):
    nb = len(parts)
    width = attended[0].shape[0]
    heads = width // HEAD_DIM
    ops = (*parts, *attended, *grads, lse)
    result = (3 * PAD, nb * BLOCK)
    return pl.pallas_call(
        attn_bwd_body,
        out_shape=sds(result),
        grid_spec=pltpu.PrefetchScalarGridSpec(
            num_scalar_prefetch=1,
            grid=(nb,),
            in_specs=[whole(p.shape) for p in ops],
            out_specs=whole(result),
            scratch_shapes=[
                pltpu.VMEM((heads, nb, 2 * HEAD_DIM, BLOCK), bf16),
                pltpu.VMEM((nb, width, BLOCK), bf16),
                pltpu.VMEM((nb, width, BLOCK), bf16),
                pltpu.VMEM((nb, width, BLOCK), bf16),
                pltpu.VMEM((heads, nb, BLOCK, 2 * HEAD_DIM), bf16),
                pltpu.VMEM((heads, nb, BLOCK, HEAD_DIM), bf16),
                pltpu.VMEM((nb, 8, BLOCK), f32),
                pltpu.VMEM((nb, width, BLOCK), f32),
                pltpu.VMEM((nb, width, BLOCK), f32),
                pltpu.VMEM((nb, width, BLOCK), f32),
                pltpu.VMEM((heads, BLOCK, BLOCK), f32),
                pltpu.VMEM((heads, BLOCK, BLOCK), f32),
                pltpu.VMEM((heads, BLOCK, BLOCK), bf16),
                pltpu.VMEM((heads, BLOCK, BLOCK), bf16),
            ],
        ),
        compiler_params=pltpu.CompilerParams(dimension_semantics=("arbitrary",)),
        cost_estimate=cost("attn_bwd"),
        name="attn_bwd",
    )(scal, *ops)


LANE = 128


LENGTH = {
    "pack": 2, "unpack_qkv": 2.5, "norm_qkv": 3.4, "stack": 2.5, "unpack": 6, "project": 6.4, "branch": 5.8,
    "first_o": 2.7, "back_first": 4, "back_rest": 5.6, "third": 5.4, "fourth": 3.2, "first_qkv": 2.3,
    "second_qkv": 1.8, "fifth": 2, "finish": 5.5, "attn_fwd": 18, "attn_bwd": 25, "mlp": 11,
}
FLOPS_PER_US = 1_000_000_000


def cost(name):
    return pl.CostEstimate(flops=int(LENGTH[name] * FLOPS_PER_US), bytes_accessed=100_000, transcendentals=0)


def call(body, outs, *ops, scratch=(), name=None):
    near = pl.BlockSpec(memory_space=pltpu.VMEM)
    return pl.pallas_call(
        body,
        out_shape=tuple(outs),
        in_specs=[near] * len(ops),
        out_specs=(near,) * len(outs),
        scratch_shapes=list(scratch),
        cost_estimate=cost(name),
        name=name,
    )(*ops)


def aligned(x, n):
    return pl.multiple_of(x, n)


def after(x, *others):
    return lax.optimization_barrier((x, *others))[0]


def mine_of(k):
    return lax.div(lax.axis_index("dp"), 1 << k) & 1


def pack_body(w_qkv, gain_a, gain_m, w_up, w_down, w_out, qkv, keep, give):
    rows, half = w_up.shape[0], w_up.shape[1] // 2
    width = w_out.shape[0]
    mine = mine_of(0)
    qkv[...] = jnp.zeros_like(qkv)
    for c in range(3):
        qkv[:, c * PAD : c * PAD + width] = w_qkv[c]
    eye = lax.broadcasted_iota(jnp.int32, (rows, rows), 0) == lax.broadcasted_iota(jnp.int32, (rows, rows), 1)
    lane = lax.broadcasted_iota(jnp.int32, (rows, LANE), 1)
    cols = [jnp.sum(jnp.where(eye, g[...].astype(f32), 0.0), axis=1, keepdims=True) for g in (gain_a, gain_m)]
    qkv[:, 3 * PAD :] = jnp.where(lane == 0, cols[0], jnp.where(lane == 1, cols[1], 0.0)).astype(bf16)
    tiles = half // LANE
    for k in range(tiles):
        for to, which in ((keep, mine), (give, 1 - mine)):
            at = which * half + k * LANE
            to[k * rows : (k + 1) * rows] = w_up[:, pl.ds(aligned(at, LANE), LANE)]
            to[(tiles + k) * rows : (tiles + k + 1) * rows] = w_down[:, pl.ds(aligned(at, LANE), LANE)]
    base = 2 * tiles * rows
    back = w_out[...].astype(f32).T.astype(bf16)
    keep[base : base + rows] = back[:, 0:LANE]
    keep[base + rows : base + 2 * rows] = jnp.zeros((rows, LANE), bf16)
    keep[base + rows : base + 2 * rows, 0 : width - LANE] = back[:, LANE:width]


def unpack_qkv_body(near, far, w, gains):
    me = lax.axis_index("dp")
    rows = near.shape[1]
    count = near.shape[0]
    tail = []
    for p in range(2 * count):
        src = near if p < count else far
        mask = 2 * (p % count) + (1 if p >= count else 0)
        w[pl.ds(aligned((me ^ mask) * rows, 32), rows)] = src[p % count, :, : 3 * PAD]
    for b in range(2 * count):
        mask = me ^ b
        part = lax.div(mask, 2)
        col = jnp.where(
            (mask & 1) == 0, near[part, :, 3 * PAD :].astype(f32), far[part, :, 3 * PAD :].astype(f32)
        )
        tail.append(col)
    gains[...] = jnp.concatenate(tail, axis=0).T[0:8]


def norm_qkv_body(xa, xb, w, gains, normed, qa, qb):
    for half, (x, q) in enumerate(((xa, qa), (xb, qb))):
        size = x.shape[0]

        for r in range(0, size, 64):
            v = x[r : r + 64].astype(f32)
            c = v - jnp.mean(v, axis=-1, keepdims=True)
            rstd = lax.rsqrt(jnp.mean(c * c, axis=-1, keepdims=True) + EPS)
            normed[half * size + r : half * size + r + 64] = (c * rstd * gains[0:1]).astype(bf16)

        q[...] = nn(normed[half * size : (half + 1) * size], w[...]).astype(bf16).T


def stack_body(*refs):
    parts, (a, b) = refs[:-2], refs[-2:]
    u = b.shape[1] // 2
    for s, p in enumerate(parts):
        a[s, 0:u] = p[0:u]
        b[s, 0:u] = p[u : 2 * u]
        a[s, u : 2 * u] = p[2 * u : 3 * u]
        b[s, u : 2 * u] = p[3 * u : 4 * u]
        a[s, 2 * u :] = p[4 * u :]


def unpack_body(*refs):
    early, late, (up, down, back) = refs[0:8], refs[8:16], refs[16:19]
    me = lax.axis_index("dp")
    rows = 96
    half = up.shape[1] // RING
    tiles = half // LANE
    span = tiles * rows
    for p in range(4):
        for s in range(RING):
            came = early if s < early[0].shape[0] else late
            a, b, at = came[p], came[4 + p], s % early[0].shape[0]
            for rc in range(2):
                to_a = pl.ds(aligned((me ^ (2 * p + rc)) * rows, 32), rows)
                to_b = pl.ds(aligned((me ^ (2 * ((p & 1) * 2 + (p >> 1)) + rc)) * rows, 32), rows)
                for k in range(tiles):
                    cols = slice(s * half + k * LANE, s * half + (k + 1) * LANE)
                    src = slice(rc * span + k * rows, rc * span + (k + 1) * rows)
                    up[to_a, cols] = a[at, src]
                    down[to_b, cols] = b[at, src]
            where = lax.div(me ^ (2 * p), 2)
            for k in range(2):
                back[where, s, :, k * LANE : (k + 1) * LANE] = a[at, 2 * span + k * rows : 2 * span + (k + 1) * rows]


def project_body(x, a0, a1, a2, a3, near, far, gains, mixed, mlp, tokens_major, w):
    mine = mine_of(0)
    rows = near.shape[2]
    width = a0.shape[0]
    for b in range(near.shape[0]):
        for s in range(RING):
            w[s, pl.ds(aligned((2 * b + mine) * rows, 32), rows)] = near[b, s]
            w[s, pl.ds(aligned((2 * b + 1 - mine) * rows, 32), rows)] = far[b, s]
    zero = jnp.zeros((PAD - width, a0.shape[1]), bf16)
    for s, a in enumerate((a0, a1, a2, a3)):
        tokens_major[:, s * PAD : (s + 1) * PAD] = jnp.concatenate([a[...], zero], axis=0).T
    for r in range(0, x.shape[0], 128):
        total = x[r : r + 128].astype(f32)
        for s in range(RING):
            total = total + nt(tokens_major[r : r + 128, s * PAD : (s + 1) * PAD], w[s])
        mixed[r : r + 128] = total
    normalise(mixed, gains[1:2], mlp)


def normalise(rows, gain, out):
    for r in range(0, rows.shape[0], 64):
        at = slice(r, r + 64)
        v = rows[at]
        c = v - jnp.mean(v, axis=-1, keepdims=True)
        rstd = lax.rsqrt(jnp.mean(c * c, axis=-1, keepdims=True) + EPS)
        out[at] = (c * rstd * gain).astype(bf16)


def gelu_both(v):
    square = v * v
    t = jnp.tanh(v * (0.7978845608028654 + (0.7978845608028654 * 0.044715) * square))
    gate = 0.5 + 0.5 * t
    bend = v * (2 * 0.7978845608028654 + (6 * 0.7978845608028654 * 0.044715) * square)
    return v * gate, gate + gate * (1.0 - gate) * bend


def mlp_body(x0, x1, g0, g1, up, down, active, grad, hid, push):
    size = x0.shape[0]
    for half, (x, g) in enumerate(((x1, g1), (x0, g0))):
        hid[half] = nn(x[...], up[...])
        push[half] = nn(g[...], down[...])
    for half in range(2):
        for r in range(0, size, 64):
            rows = slice(r, r + 64)
            to = slice((1 - half) * size + r, (1 - half) * size + r + 64)
            value, slope = gelu_both(hid[half, rows])
            active[to] = value.astype(bf16)
            grad[to] = (push[half, rows] * slope).astype(bf16)


def mlp(x0, x1, g0, g1, up, down):
    tokens, dim = x0.shape
    hidden = up.shape[1]
    keep = pl.BlockSpec((tokens, dim), lambda n: (0, 0))
    cols = pl.BlockSpec((dim, BLOCK), lambda n: (0, n))
    wide = pl.BlockSpec((2 * tokens, BLOCK), lambda n: (0, n))
    return pl.pallas_call(
        mlp_body,
        out_shape=(sds((2 * tokens, hidden)), sds((2 * tokens, hidden))),
        grid=(hidden // BLOCK,),
        in_specs=[keep] * 4 + [cols] * 2,
        out_specs=(wide, wide),
        scratch_shapes=[pltpu.VMEM((2, tokens, BLOCK), f32), pltpu.VMEM((2, tokens, BLOCK), f32)],
        cost_estimate=cost("mlp"),
        name="mlp",
    )(x0, x1, g0, g1, up, down)


def norm_back(v, gain, grad):
    c = v - jnp.mean(v, axis=-1, keepdims=True)
    rstd = lax.rsqrt(jnp.mean(c * c, axis=-1, keepdims=True) + EPS)
    hat = c * rstd
    g = grad * gain
    return rstd * (g - jnp.mean(g, axis=-1, keepdims=True) - hat * jnp.mean(g * hat, axis=-1, keepdims=True))


def branch_body(mixed, part, far, grad_out, gains, w, grad_mixed, branch, *heads):
    for r in range(0, mixed.shape[0], 64):
        at = slice(r, r + 64)
        grad = part[at] + far[at].astype(f32)
        total = grad_out[at].astype(f32) + norm_back(mixed[at], gains[1:2], grad)
        grad_mixed[at] = total
        branch[at] = total.astype(bf16)

    width = heads[0].shape[0]
    for s in range(RING):
        heads[s][...] = nn(branch[...], w[s]).astype(bf16).T[0:width]


def back_body(grad, w, *outs, blocks):
    for out, n in zip(outs, blocks):
        out[...] = nt(grad[:, n * BLOCK : (n + 1) * BLOCK].T, w[...]).astype(bf16)


def finish_body(*refs):
    parts, recvs, (x, grad_mixed, gains, out) = refs[0:2], refs[2:4], refs[4:]
    for k, (part, recv) in enumerate(zip(parts, recvs)):
        for r in range(0, BLOCK, 64):
            grad = part[r : r + 64].astype(f32) + recv[r : r + 64].astype(f32)
            at = slice(k * BLOCK + r, k * BLOCK + r + 64)
            out[at] = grad_mixed[at] + norm_back(x[at].astype(f32), gains[0:1], grad)


def turn(x, shift):
    return lax.ppermute(x, "tensor", [(i, (i + shift) % RING) for i in range(RING)])


def swap(x, axis, bit, size):
    return lax.ppermute(x, axis, [(i, i ^ bit) for i in range(size)])


def pick(x, index, axis=0):
    return lax.dynamic_index_in_dim(x, index, axis, keepdims=False)


def ring_gather(x):
    got = [x]
    for _ in range(RING - 1):
        got.append(turn(got[-1], 1))
    return got


def ring_reduce(chunks):
    moving = chunks[1].astype(bf16)
    for r in range(1, RING):
        moved = turn(moving, 1)
        total = moved.astype(f32) + chunks[(r + 1) % RING]
        moving = total.astype(bf16)
    return total


def spread_blocks(x, bits, size):
    for bit in bits:
        x = jnp.concatenate([x, swap(x, "dp", bit, size)])
    return x


def place_of(mask, bits):
    place = 0
    for k, bit in enumerate(bits):
        place = place + jnp.where(mask & bit != 0, 1 << k, 0)
    return place


def halve(blocks, left, bit, me, size):
    at = left.index(bit)
    lead, tail = 1 << at, 1 << (len(left) - at - 1)
    split = blocks.reshape((lead, 2, tail) + blocks.shape[1:])
    mine = jnp.where(me & bit != 0, 1, 0)
    send = pick(split, 1 - mine, 1).astype(bf16)
    keep = pick(split, mine, 1)
    total = keep.astype(f32) + swap(send, "dp", bit, size).astype(f32)
    return total.reshape((lead * tail,) + blocks.shape[1:]), [b for b in left if b != bit]


def centre(rows):
    shifted = rows - jnp.mean(rows, axis=-1, keepdims=True)
    rstd = lax.rsqrt(jnp.mean(shifted * shifted, axis=-1, keepdims=True) + EPS)
    return shifted * rstd, rstd


def norm_back_plain(grad_hat, hat, rstd):
    return rstd * (
        grad_hat
        - jnp.mean(grad_hat, axis=-1, keepdims=True)
        - hat * jnp.mean(grad_hat * hat, axis=-1, keepdims=True)
    )


def einf(spec, a, b):
    return jnp.einsum(spec, a, b, preferred_element_type=f32)


def shards(size, inputs, doc_ids, gain_attn, w_qkv, w_out, gain_mlp, w_up, w_down, grad_out):
    me = lax.axis_index("dp")
    z = lax.axis_index("tensor")
    odd = me & 1
    others = [1 << k for k in range(1, size.bit_length() - 1)]
    documents = doc_ids[0]
    tokens, dim = inputs.shape
    rows = dim // size
    hid = w_up.shape[1]
    half = hid // 2
    width = w_out.shape[0]
    scal = jnp.stack([z, jnp.sum(documents < 1), jnp.sum(documents < 2)]).astype(jnp.int32)

    pieces = [ring_gather(inputs[k : k + BLOCK]) for k in range(0, tokens, BLOCK)]

    gains = jnp.stack([gain_attn, gain_mlp])
    own = jnp.concatenate([w_qkv[0], w_qkv[1], w_qkv[2], jnp.pad(gains, ((0, 62), (0, 0))).T], axis=1)
    order = others + [1]
    spread_qkv = spread_blocks(own[None], order, size)
    full = jnp.concatenate([pick(spread_qkv, place_of(me ^ b, order)) for b in range(size)])
    full_qkv = full[:, : 3 * width]
    gain_one = full[:, 3 * width].astype(f32)
    gain_two = full[:, 3 * width + 1].astype(f32)

    out_rows = jnp.concatenate([w_out.T[: rows // 2], w_out.T[rows // 2 :]], axis=1)

    def pair_half(w):
        parts = w.reshape(rows, 2, half)
        return jnp.concatenate([pick(parts, odd, 1), swap(pick(parts, 1 - odd, 1), "dp", 1, size)])

    pack_a = jnp.concatenate([pair_half(w_up), out_rows])
    pack_b = pair_half(w_down.T)
    ring_a = jnp.stack(ring_gather(pack_a))
    ring_b = jnp.stack(ring_gather(pack_b))
    order_b = others[::-1]
    spread_a = spread_blocks(ring_a[None], others, size)
    spread_b = spread_blocks(ring_b[None], order_b, size)

    def assemble(spread_w, bits):
        blocks = []
        for b in range(size):
            mask = me ^ b
            block = pick(spread_w, place_of(mask, bits))[:, : 2 * rows]
            block = pick(block.reshape(RING, 2, rows, half), mask & 1, 1)
            blocks.append(block.transpose(1, 0, 2).reshape(rows, RING * half))
        return jnp.concatenate(blocks)

    full_up = assemble(spread_a, others)
    full_down = assemble(spread_b, order_b)
    out_part = spread_a[:, :, 2 * rows :]
    out_both = jnp.stack([out_part, swap(out_part, "dp", 1, size)])

    def out_block(b):
        mask = me ^ b
        block = pick(pick(out_both, mask & 1), place_of(mask, others))
        block = jnp.concatenate([block[..., :width], block[..., width:]], axis=1)
        return block.transpose(1, 0, 2).reshape(rows, RING * width)

    full_out = jnp.concatenate([out_block(b) for b in range(size)])
    grad_both = jnp.concatenate([grad_out, swap(grad_out, "dp", 1, size)])
    grad_active = einf("td,df->tf", grad_both, full_down)

    normed = []
    parts = []
    for s in range(RING):
        for piece in pieces:
            hat, _ = centre(piece[s].astype(f32))
            normed.append((hat * gain_one).astype(bf16))
            part = einf("de,td->et", full_qkv, normed[-1]).astype(bf16).reshape(3, width, BLOCK)
            parts.append(jnp.pad(part, ((0, 0), (0, PAD - width), (0, 0))).reshape(3 * PAD, BLOCK))
    normed = jnp.concatenate(normed)
    *sent, lse = attn_fwd(scal, parts, width // HEAD_DIM)
    attended = jnp.concatenate([sent[0]] + [turn(sent[s], s) for s in range(1, RING)])
    mixed = inputs.astype(f32) + einf("et,de->td", attended, full_out)
    hat_two, rstd_two = centre(mixed)
    mlp_rows = (hat_two * gain_two).astype(bf16)
    mlp_both = jnp.concatenate([mlp_rows, swap(mlp_rows, "dp", 1, size)])
    hidden = einf("td,df->tf", mlp_both, full_up)
    value, slope = gelu_both(hidden)
    active = value.astype(bf16)
    grad_hidden = (grad_active * slope).astype(bf16)
    grad_part = einf("tf,df->td", grad_hidden, full_up)
    grad_mlp = grad_part[:tokens] + swap(grad_part[tokens:].astype(bf16), "dp", 1, size).astype(f32)
    grad_mixed = grad_out.astype(f32) + norm_back_plain(grad_mlp * gain_two, hat_two, rstd_two)
    grad_branch = grad_mixed.astype(bf16)
    grad_att = einf("de,td->et", full_out, grad_branch).astype(bf16).reshape(RING, width, tokens)
    grads = [grad_att[0]] + [turn(grad_att[s], -s) for s in range(1, RING)]

    out_pair = einf("tf,df->td", active, full_down)
    layer_out = (
        mixed + out_pair[:tokens] + swap(out_pair[tokens:].astype(bf16), "dp", 1, size).astype(f32)
    ).astype(bf16)

    bits = [1 << k for k in reversed(range(size.bit_length() - 1))]

    def scatter(grad, stages, last_width):
        blocks, left = grad.reshape(size, rows, grad.shape[1]), list(bits)
        for bit in stages:
            blocks, left = halve(blocks, left, bit, me, size)
        blocks = blocks.reshape(-1, blocks.shape[-1])
        return ring_reduce([blocks[:, s * last_width : (s + 1) * last_width] for s in range(RING)])

    def pair_whole(block):
        block = block.reshape(2, rows, half)
        send = pick(block, 1 - odd).astype(bf16)
        keep = pick(block, odd)
        other = swap(send, "dp", 1, size).astype(f32)
        return jnp.where(odd == 0, jnp.concatenate([keep, other], axis=1), jnp.concatenate([other, keep], axis=1))

    grad_down = pair_whole(scatter(einf("td,tf->df", grad_both, active), others, half)).T
    grad_up = pair_whole(scatter(einf("td,tf->df", mlp_both, grad_hidden), order_b, half))
    grad_o = scatter(einf("td,et->de", grad_branch, attended), [1] + order_b, width).T

    grad_parts = attn_bwd(scal, parts, sent, grads, lse)
    grad_parts = grad_parts.reshape(3, PAD, -1)[:, :width].reshape(3 * width, -1)
    grad_proj = einf("td,et->de", normed, grad_parts)
    blocks, left = grad_proj.reshape(size, rows, 3 * width), list(bits)
    for bit in [1] + order_b:
        blocks, left = halve(blocks, left, bit, me, size)
    grad_qkv = blocks[0].reshape(rows, 3, width).transpose(1, 0, 2)

    back = []
    for k in range(0, tokens, BLOCK):
        back.append(
            ring_reduce(
                [
                    einf("et,de->td", grad_parts[:, s * tokens + k : s * tokens + k + BLOCK], full_qkv)
                    for s in range(RING)
                ]
            )
        )
    grad_normed = jnp.concatenate(back)
    hat_one, rstd_one = centre(inputs.astype(f32))
    grad_inputs = grad_mixed + norm_back_plain(grad_normed * gain_one, hat_one, rstd_one)

    sums = jnp.stack(
        [
            jnp.sum(w_qkv.astype(f32) * grad_qkv, axis=(0, 2)),
            jnp.sum(w_up.astype(f32) * grad_up, axis=1),
        ]
    )
    for bit in (1, 2):
        sums = sums + swap(sums, "tensor", bit, RING)
    sums = sums / gains.astype(f32)
    return layer_out, grad_inputs, sums[0], grad_qkv, grad_o, sums[1], grad_up, grad_down


def add(a, b):
    return (a.astype(f32) + b.astype(f32)).astype(bf16)


def first_body(full, recv, send, keep, *, by_y):
    c = mine_of(0)
    mine = mine_of(2 if by_y else 1)
    for k in range(2):
        for which, to in ((mine, keep), (1 - mine, send)):
            at = which * 2 + k if by_y else k * 2 + which
            to[k] = add(full[at * 2 + c], recv[at])


def second_body(keep_in, recv, send, keep):
    mine = mine_of(1)
    keep[...] = add(keep_in[mine], recv[mine])
    send[...] = add(keep_in[1 - mine], recv[1 - mine])


def third_body(up, far_up, down, far_down, o, far_o, up_send, up_keep, mix_send, mix_keep):
    c, x, y = mine_of(0), mine_of(1), mine_of(2)
    rows = up.shape[1]
    tiles = up.shape[2] // RING // LANE
    span = tiles * rows
    for s in range(RING):
        for rc in range(2):
            side = jnp.bitwise_xor(c, rc)
            for k in range(tiles):
                cols = slice((s * tiles + k) * LANE, (s * tiles + k + 1) * LANE)
                to = slice(rc * span + k * rows, rc * span + (k + 1) * rows)
                for which, out in ((x, up_keep), (1 - x, up_send)):
                    out[s, to] = add(up[y * 4 + which * 2 + side, :, cols], far_up[which * 2 + side, :, cols])
                for which, out in ((y, mix_keep), (1 - y, mix_send)):
                    out[s, to] = add(down[which * 4 + x * 2 + side, :, cols], far_down[which * 2 + side, :, cols])
        for k in range(2):
            cols = slice((s * 2 + k) * LANE, (s * 2 + k + 1) * LANE)
            to = slice(2 * span + k * rows, 2 * span + (k + 1) * rows)
            for which, out in ((y, mix_keep), (1 - y, mix_send)):
                out[s, to] = add(o[which, :, cols], far_o[which, :, cols])


def fourth_body(up, far_up, mix, far_mix, first, rest):
    span = up.shape[1] // 2
    extra = mix.shape[1] - 2 * span
    for s in range(RING):
        for rc in range(2):
            src = slice(rc * span, (rc + 1) * span)
            at = rc * 2 * span
            rest[s, at : at + span] = add(up[s, src], far_up[s, src])
            rest[s, at + span : at + 2 * span] = add(mix[s, src], far_mix[s, src])
        tail = slice(2 * span, 2 * span + extra)
        rest[s, 4 * span : 4 * span + extra] = add(mix[s, tail], far_mix[s, tail])
    first[...] = rest[1]


def fifth_body(mine, far, up, down, o):
    c = mine_of(0)
    rows = up.shape[0]
    half = up.shape[1] // 2
    tiles = half // LANE
    for side, src in ((c, mine), (1 - c, far)):
        for k in range(tiles):
            at = pl.ds(aligned(side * half + k * LANE, LANE), LANE)
            up[:, at] = src[k * rows : (k + 1) * rows].astype(f32)
            down[:, at] = src[(tiles + k) * rows : (tiles + k + 1) * rows].astype(f32)
    base = 4 * tiles * rows
    width = o.shape[0]
    o[0:LANE] = mine[base : base + rows].astype(f32).T
    o[LANE:width] = mine[base + rows : base + 2 * rows].astype(f32).T[0 : width - LANE]


def shards_small(size, inputs, doc_ids, gain_attn, w_qkv, w_out, gain_mlp, w_up, w_down, grad_out):
    me = lax.axis_index("dp")
    z = lax.axis_index("tensor")
    documents = doc_ids[0]
    tokens, dim = inputs.shape
    rows, hid = w_up.shape
    half = hid // 2
    width = w_out.shape[0]
    heads = width // HEAD_DIM
    hidden = RING * half
    scal = jnp.stack([z, jnp.sum(documents < 1), jnp.sum(documents < 2)]).astype(jnp.int32)

    def pair(x):
        return swap(x, "dp", 1, size)

    def along_x(x):
        return swap(x, "dp", 2, size)

    def along_y(x):
        return swap(x, "dp", 4, size)

    span = half * rows // LANE
    x_a, x_b = ([inputs[k : k + BLOCK]] for k in range(0, tokens, BLOCK))

    def hop():
        x_a.append(turn(x_a[-1], 1))
        x_b.append(turn(x_b[-1], 1))

    hop()
    qkv, keep, give = call(
        pack_body,
        [sds((rows, 3 * PAD + LANE)), sds((2 * span + 2 * rows, LANE)), sds((2 * span, LANE))],
        w_qkv, gain_attn[None], gain_mlp[None], w_up, w_down.T, w_out, name="pack",
    )
    got = pair(give)
    qkv = jnp.stack([qkv, along_x(qkv)])
    packed = jnp.concatenate([keep[: 2 * span], got, keep[2 * span :]])
    qkv = jnp.concatenate([qkv, along_y(qkv)])
    qkv_far = pair(qkv)
    ring = [packed, turn(after(packed, x_a[1], x_b[1]), 1)]
    hop()
    ring.append(turn(after(ring[1], x_a[2], x_b[2]), 1))
    hop()
    ring.append(turn(after(ring[2], x_a[3], x_b[3]), 1))
    grad_far = pair(after(grad_out, x_a[2]))
    full_qkv, gains = call(
        unpack_qkv_body, [sds((dim, 3 * PAD)), sds((8, dim), f32)], qkv, qkv_far, name="unpack_qkv"
    )
    normed, parts = [], []
    for s in range(RING):
        n, qa, qb = call(
            norm_qkv_body,
            [sds((tokens, dim)), sds((3 * PAD, BLOCK)), sds((3 * PAD, BLOCK))],
            x_a[s], x_b[s], full_qkv, gains, name="norm_qkv",
        )
        normed.append(n)
        parts.extend((qa, qb))

    def spread(*shares):
        n = len(shares)
        u0, d0 = call(
            stack_body, [sds((n, 2 * span + 2 * rows, LANE)), sds((n, 2 * span, LANE))], *shares, name="stack"
        )
        u1, d1 = along_x(u0), along_y(d0)
        u2, d2 = along_y(u0), along_x(d0)
        return u0, u1, u2, along_y(u1), d0, d1, d2, along_x(d1)

    early = spread(*ring[:3])

    *sent, lse = attn_fwd(scal, parts, heads)
    attended = [sent[0]] + [turn(sent[s], s) for s in range(1, RING)]
    late = spread(after(ring[3], sent[0]))
    full_up, full_down, back_near = call(
        unpack_body,
        [sds((dim, hidden)), sds((dim, hidden)), sds((size // 2, RING, rows, PAD))],
        *early, *late, name="unpack",
    )
    back_far = pair(back_near)
    mixed, mlp_rows, att_tokens, full_out = call(
        project_body,
        [sds((tokens, dim), f32), sds((tokens, dim)), sds((tokens, RING * PAD)), sds((RING, dim, PAD))],
        inputs, *attended, back_near, back_far, gains, name="project",
    )
    mlp_far = pair(mlp_rows)
    active, grad_hidden = mlp(mlp_rows, mlp_far, grad_out, grad_far, full_up, full_down)
    part_got = pair(einf("tf,df->td", grad_hidden[tokens:], full_up).astype(bf16))
    part = einf("tf,df->td", grad_hidden[:tokens], full_up)
    grad_mixed, branch, *grad_att = call(
        branch_body,
        [sds((tokens, dim), f32), sds((tokens, dim)), *[sds((width, tokens))] * RING],
        mixed, part, part_got, grad_out, gains, full_out, name="branch",
    )
    grads = [grad_att[0]] + [turn(grad_att[s], -s) for s in range(1, RING)]
    grad_hidden_late = after(grad_hidden, branch)
    active_late = after(active, branch)

    x_bit, y_bit, c_bit = lax.div(me, 2) & 1, lax.div(me, 4) & 1, me & 1
    both_in = jnp.concatenate([mlp_rows, mlp_far])
    both_grad = jnp.concatenate([grad_out, grad_far])
    grad_up = einf("td,tf->df", both_in, grad_hidden_late).astype(bf16)
    grad_down = einf("td,tf->df", both_grad, active_late).astype(bf16)
    far_up = along_y(pick(grad_up.reshape(2, 4, rows, hidden), 1 - y_bit))
    far_down = along_x(pick(grad_down.reshape(2, 2, 2, rows, hidden), 1 - x_bit, 1).reshape(4, rows, hidden))
    grad_o = einf("td,te->de", branch, att_tokens).astype(bf16)
    far_o = pair(pick(grad_o.reshape(4, 2, rows, RING * PAD), 1 - c_bit, 1))
    layer_far = pair(einf("tf,df->td", active_late[tokens:], full_down).astype(bf16))
    layer_near = einf("tf,df->td", active_late[:tokens], full_down)
    layer_out = (mixed + layer_near + layer_far.astype(f32)).astype(bf16)

    grad_parts = attn_bwd(scal, parts, sent, grads, after(lse, layer_out, far_o))
    count = tokens // BLOCK

    def backs(grad, blocks, name):
        return call(
            functools.partial(back_body, blocks=blocks), [sds((BLOCK, dim))] * len(blocks), grad, full_qkv, name=name
        )

    start = backs(grad_parts, list(range(count, 2 * count)), "back_first")
    came = [turn(start[k], 1) for k in range(count)]
    later = backs(
        after(grad_parts, *start), list(range(2 * count, RING * count)) + list(range(count)), "back_rest"
    )
    o_send, o_keep = call(
        functools.partial(first_body, by_y=False),
        [sds((2, rows, RING * PAD))] * 2, after(grad_o, start[0]).reshape(size, rows, RING * PAD), far_o, name="first_o",
    )
    up_shape, mix_shape = sds((RING, 2 * span, LANE)), sds((RING, 2 * span + 2 * rows, LANE))
    up_send, up_keep, mix_send, mix_keep = call(
        third_body,
        [up_shape, up_shape, mix_shape, mix_shape],
        grad_up.reshape(size, rows, hidden), far_up, grad_down.reshape(size, rows, hidden), far_down,
        o_keep, along_x(o_send), name="third",
    )
    far_up_two, far_mix_two = along_x(up_send), along_y(mix_send)
    came = [turn(add(later[k], came[k]), 1) for k in range(count)]
    total_shape = (4 * span + 2 * rows, LANE)
    moving, rest = call(
        fourth_body,
        [sds(total_shape), sds((RING, *total_shape))],
        up_keep, far_up_two, mix_keep, far_mix_two, name="fourth",
    )

    came = [turn(add(later[count + k], came[k]), 1) for k in range(count)]
    grad_inputs = call(
        finish_body,
        [sds((tokens, dim), f32)],
        *later[(RING - 2) * count :], *came, inputs, grad_mixed, gains, name="finish",
    )[0]

    grad_proj = einf("td,et->de", jnp.concatenate(normed), grad_parts).astype(bf16)
    far_qkv = pair(pick(grad_proj.reshape(4, 2, rows, 3 * PAD), 1 - c_bit, 1))
    q_send, q_keep = call(
        functools.partial(first_body, by_y=True),
        [sds((2, rows, 3 * PAD))] * 2, grad_proj.reshape(size, rows, 3 * PAD), far_qkv, name="first_qkv",
    )
    q_send, q_keep = call(
        second_body, [sds((rows, 3 * PAD))] * 2, q_keep, along_y(q_send), name="second_qkv"
    )
    grad_flat = q_keep.astype(f32) + along_x(q_send).astype(f32)
    grad_qkv = jnp.stack([grad_flat[:, c * PAD : c * PAD + width] for c in range(3)])

    for r in range(1, RING):
        moving = add(turn(moving, 1), rest[(r + 1) % RING])
    grad_up, grad_down, grad_o = call(
        fifth_body,
        [sds((rows, hid), f32), sds((rows, hid), f32), sds((width, rows), f32)],
        moving, pair(moving[2 * span : 4 * span]), name="fifth",
    )
    sums = jnp.stack(
        [
            jnp.sum(w_qkv.astype(f32) * grad_qkv, axis=(0, 2)),
            jnp.sum(w_up.astype(f32) * grad_up, axis=1),
        ]
    )
    for bit in (1, 2):
        sums = sums + swap(sums, "tensor", bit, RING)
    own = jnp.stack([gain_attn, gain_mlp]).astype(f32)
    sums = sums / own
    return layer_out, grad_inputs, sums[0], grad_qkv, grad_o, sums[1], grad_up, grad_down.T


def solution(mesh):
    both = P(("dp", "tensor"), None)
    weights = (P(None, "dp", "tensor"), P("tensor", "dp"), P("dp"), P("dp", "tensor"), P("tensor", "dp"))
    return jax.shard_map(
        functools.partial(shards_small if mesh.shape["dp"] == 8 else shards, mesh.shape["dp"]),
        mesh=mesh,
        in_specs=(both, P("dp", None), P("dp"), *weights, both),
        out_specs=(both, both, P("dp"), *weights),
        check_vma=False,
    )
```

```python
import functools

import jax
import jax.numpy as jnp
from jax import lax
from jax.experimental import pallas as pl
from jax.experimental.pallas import tpu as pltpu
from jax.sharding import PartitionSpec as P

HEAD_DIM = 64
BLOCK = 256
PAD = 256
RING = 4
EPS = 1e-05
LOG2E = 1.4426950408889634
f32 = jnp.float32
bf16 = jnp.bfloat16
HIDE = -1e30


def nn(a, b):
    return lax.dot_general(a, b, (((1,), (0,)), ((), ())), preferred_element_type=f32)


def nt(a, b):
    return lax.dot_general(a, b, (((1,), (1,)), ((), ())), preferred_element_type=f32)


def doc_of(place, ends):
    return jnp.where(place >= ends[1], 2, jnp.where(place >= ends[0], 1, 0))


def doc_start(row, ends):
    return jnp.where(row >= ends[1], ends[1], jnp.where(row >= ends[0], ends[0], 0))


def hidden_bias(i, j, ends):
    keys = j * BLOCK + lax.broadcasted_iota(jnp.int32, (BLOCK, BLOCK), 0)
    rows = i * BLOCK + lax.broadcasted_iota(jnp.int32, (1, BLOCK), 1)
    start = doc_start(rows, ends)
    stop = jnp.where(rows >= ends[1], 1 << 30, jnp.where(rows >= ends[0], ends[1], ends[0]))
    return jnp.where((keys >= start) & (keys < stop), 0.0, HIDE)


def signed(s, size):
    low = size.astype(bf16)
    return jnp.clip(s.astype(bf16) * bf16(1e38), -low, low)


def ring_blocks(z, count):
    for n in range(count):
        yield n, lax.rem(z - n // 2 + RING, RING) * 2 + n % 2


def walk(i, ends, step, carry):
    def body(j, carry):
        mixed = doc_of(j * BLOCK, ends) != doc_of(i * BLOCK + BLOCK - 1, ends)
        return lax.cond(mixed, lambda c: step(j, c, hidden_bias(i, j, ends)), lambda c: step(j, c, None), carry)

    first = lax.div(doc_start(i * BLOCK, ends), BLOCK)
    return lax.fori_loop(first, i + 1, body, carry)


def head_rows(h, base=0):
    return slice(base + h * HEAD_DIM, base + (h + 1) * HEAD_DIM)


def two_parts(q):
    scaled = q.astype(f32) * (0.125 * LOG2E)
    high = scaled.astype(bf16)
    return high, (scaled - high.astype(f32)).astype(bf16)


def twice(k):
    return jnp.concatenate([k, k], axis=0).T


CHUNK = 64


def chunks():
    return [slice(r, r + CHUNK) for r in range(0, BLOCK, CHUNK)]


def size_of(s, bias, rows):
    a = jnp.abs(s)
    return a if bias is None else a + bias[rows]


def attn_fwd_body(scal, *refs):
    parts, refs = refs[:-12], refs[-12:]
    outs, (lse, qs, vs, ks, acc, held, low, out) = refs[:RING], refs[RING:]
    i = pl.program_id(0)
    heads, width = ks.shape[0], vs.shape[1]
    z = scal[0]
    ends = (scal[1], scal[2])

    @pl.when(i == 0)
    def _():
        for n, b in ring_blocks(z, len(parts)):
            ref = parts[n]
            vs[b] = ref[2 * PAD : 2 * PAD + width]
            for h in range(heads):
                high, rest = two_parts(ref[head_rows(h)])
                qs[h, b, 0:HEAD_DIM] = high
                qs[h, b, HEAD_DIM : 2 * HEAD_DIM] = rest
                ks[h, b] = twice(ref[head_rows(h, PAD)])

    acc[...] = jnp.zeros_like(acc)

    def largest(j, carry, bias):
        new = []
        for h in range(heads):
            s = nn(ks[h, j], qs[h, i])
            held[h, j] = s
            top = carry[h]
            for rows in chunks():
                top = jnp.maximum(top, jnp.max(size_of(s[rows], bias, rows).reshape(-1, 8, BLOCK), axis=0))
            new.append(top)
        return tuple(new)

    zero = jnp.zeros((8, BLOCK), f32)
    tops = walk(i, ends, largest, (zero,) * heads)
    tops = [jnp.max(t, axis=0, keepdims=True) for t in tops]

    def weigh(j, carry, bias):
        new = []
        for h in range(heads):
            total = carry[h]
            for rows in chunks():
                s = held[h, j, rows]
                p = jnp.exp2(size_of(s, bias, rows) - tops[h])
                total = total + jnp.sum(p.reshape(-1, 8, BLOCK), axis=0)
                low[h, rows] = signed(s, p)
            new.append(total)
        for h in range(heads):
            acc[head_rows(h)] += nn(vs[j, head_rows(h)], low[h])
        return tuple(new)

    totals = walk(i, ends, weigh, (zero,) * heads)
    t = lax.div(i, 2)
    cols = pl.ds(pl.multiple_of(lax.rem(i, 2) * BLOCK, BLOCK), BLOCK)
    dest = lax.rem(t - z + RING, RING)
    for h in range(heads):
        l = jnp.sum(totals[h], axis=0, keepdims=True)
        out[dest, head_rows(h), cols] = (acc[head_rows(h)] / l).astype(bf16)
        lse[i, h : h + 1, :] = tops[h] + jnp.log(l) * LOG2E

    @pl.when(i == pl.num_programs(0) - 1)
    def _():
        for s, ref in enumerate(outs):
            ref[...] = out[s]


def whole(shape):
    return pl.BlockSpec(shape, lambda *_: (0,) * len(shape))


def sds(shape, dtype=bf16):
    return jax.ShapeDtypeStruct(shape, dtype)


def attn_fwd(scal, parts, heads):
    nb = len(parts)
    width, cols = heads * HEAD_DIM, nb // RING * BLOCK
    return pl.pallas_call(
        attn_fwd_body,
        out_shape=(*[sds((width, cols))] * RING, sds((nb, 8, BLOCK), f32)),
        grid_spec=pltpu.PrefetchScalarGridSpec(
            num_scalar_prefetch=1,
            grid=(nb,),
            in_specs=[whole(p.shape) for p in parts],
            out_specs=(*[whole((width, cols))] * RING, whole((nb, 8, BLOCK))),
            scratch_shapes=[
                pltpu.VMEM((heads, nb, 2 * HEAD_DIM, BLOCK), bf16),
                pltpu.VMEM((nb, width, BLOCK), bf16),
                pltpu.VMEM((heads, nb, BLOCK, 2 * HEAD_DIM), bf16),
                pltpu.VMEM((width, BLOCK), f32),
                pltpu.VMEM((heads, nb, BLOCK, BLOCK), f32),
                pltpu.VMEM((heads, BLOCK, BLOCK), bf16),
                pltpu.VMEM((RING, width, cols), bf16),
            ],
        ),
        compiler_params=pltpu.CompilerParams(dimension_semantics=("arbitrary",)),
        cost_estimate=cost("attn_fwd"),
        name="attn_fwd",
    )(scal, *parts)


def attn_bwd_body(scal, *refs):
    parts, refs = refs[:-24], refs[-24:]
    o, refs = refs[:RING], refs[RING:]
    g0, g1, g2, g3, lse, grad, q2, qs, kts, gs, ks, vns, inner, dq, dk, dv, held, push, low, dlow = refs
    i = pl.program_id(0)
    nb = pl.num_programs(0)
    heads, width = ks.shape[0], qs.shape[1]
    z = scal[0]
    ends = (scal[1], scal[2])

    @pl.when(i == 0)
    def _():
        for n, b in ring_blocks(z, len(parts)):
            ref = parts[n]
            qs[b] = ref[0:width] * bf16(0.125)
            kts[b] = ref[PAD : PAD + width]
            for h in range(heads):
                high, low = two_parts(ref[head_rows(h)])
                q2[h, b, 0:HEAD_DIM] = high
                q2[h, b, HEAD_DIM : 2 * HEAD_DIM] = low
                ks[h, b] = twice(ref[head_rows(h, PAD)])
                vns[h, b] = ref[head_rows(h, 2 * PAD)].T
        for s, ref in enumerate((g0, g1, g2, g3)):
            t = lax.rem(z + s, RING)
            for half in range(2):
                cols = slice(half * BLOCK, (half + 1) * BLOCK)
                gs[t * 2 + half] = ref[:, cols]
                both = ref[:, cols].astype(f32) * o[s][:, cols].astype(f32)
                for h in range(heads):
                    inner[t * 2 + half, h : h + 1, :] = jnp.sum(both[head_rows(h)], axis=0, keepdims=True)
        dk[...] = jnp.zeros_like(dk)
        dv[...] = jnp.zeros_like(dv)

    dq[i] = jnp.zeros(dq.shape[1:], f32)

    bounds, levers = [], []
    for h in range(heads):
        part = inner[i, h : h + 1, :]
        bounds.append(jnp.abs(part))
        levers.append(jnp.where(part < 0, -1e38, 1e38))

    def products(j, h):
        held[h] = nn(ks[h, j], q2[h, i])
        push[h] = nn(vns[h, j], gs[i, head_rows(h)])

    def step(j, carry, bias):
        products(j, 0)
        for h in range(heads):
            if h + 1 < heads:
                products(j, h + 1)
            for rows in chunks():
                s = held[h, rows]
                mag = jnp.exp2(size_of(s, bias, rows) - lse[i, h : h + 1, :])
                low[h, rows] = signed(s, mag)
                ds = mag * (push[h, rows] - jnp.clip(s * levers[h], -bounds[h], bounds[h]))
                dlow[h, rows] = ds.astype(bf16)
            rows = head_rows(h)
            dv[j, rows] += nt(gs[i, rows], low[h])
            dk[j, rows] += nt(qs[i, rows], dlow[h])
            dq[i, rows] += nn(kts[j, rows], dlow[h])
        return carry

    walk(i, ends, step, 0)

    @pl.when(i == nb - 1)
    def _():
        grad[...] = jnp.zeros_like(grad)
        for n, b in ring_blocks(z, len(parts)):
            cols = slice(n * BLOCK, (n + 1) * BLOCK)
            grad[0:width, cols] = (dq[b] * 0.125).astype(bf16)
            grad[PAD : PAD + width, cols] = dk[b].astype(bf16)
            grad[2 * PAD : 2 * PAD + width, cols] = dv[b].astype(bf16)


def attn_bwd(scal, parts, attended, grads, lse):
    nb = len(parts)
    width = attended[0].shape[0]
    heads = width // HEAD_DIM
    ops = (*parts, *attended, *grads, lse)
    result = (3 * PAD, nb * BLOCK)
    return pl.pallas_call(
        attn_bwd_body,
        out_shape=sds(result),
        grid_spec=pltpu.PrefetchScalarGridSpec(
            num_scalar_prefetch=1,
            grid=(nb,),
            in_specs=[whole(p.shape) for p in ops],
            out_specs=whole(result),
            scratch_shapes=[
                pltpu.VMEM((heads, nb, 2 * HEAD_DIM, BLOCK), bf16),
                pltpu.VMEM((nb, width, BLOCK), bf16),
                pltpu.VMEM((nb, width, BLOCK), bf16),
                pltpu.VMEM((nb, width, BLOCK), bf16),
                pltpu.VMEM((heads, nb, BLOCK, 2 * HEAD_DIM), bf16),
                pltpu.VMEM((heads, nb, BLOCK, HEAD_DIM), bf16),
                pltpu.VMEM((nb, 8, BLOCK), f32),
                pltpu.VMEM((nb, width, BLOCK), f32),
                pltpu.VMEM((nb, width, BLOCK), f32),
                pltpu.VMEM((nb, width, BLOCK), f32),
                pltpu.VMEM((heads, BLOCK, BLOCK), f32),
                pltpu.VMEM((heads, BLOCK, BLOCK), f32),
                pltpu.VMEM((heads, BLOCK, BLOCK), bf16),
                pltpu.VMEM((heads, BLOCK, BLOCK), bf16),
            ],
        ),
        compiler_params=pltpu.CompilerParams(dimension_semantics=("arbitrary",)),
        cost_estimate=cost("attn_bwd"),
        name="attn_bwd",
    )(scal, *ops)


LANE = 128


LENGTH = {
    "pack": 2, "unpack_qkv": 2.5, "norm_qkv": 3.4, "stack": 2.5, "unpack": 6, "project": 6.4, "branch": 5.8,
    "first_o": 2.7, "back_first": 4, "back_rest": 5.6, "third": 5.4, "fourth": 3.2, "first_qkv": 2.3,
    "second_qkv": 1.8, "fifth": 2, "finish": 5.5, "attn_fwd": 18, "attn_bwd": 25, "mlp": 11,
}
FLOPS_PER_US = 1_000_000_000


def cost(name):
    return pl.CostEstimate(flops=int(LENGTH[name] * FLOPS_PER_US), bytes_accessed=100_000, transcendentals=0)


def call(body, outs, *ops, scratch=(), name=None):
    near = pl.BlockSpec(memory_space=pltpu.VMEM)
    return pl.pallas_call(
        body,
        out_shape=tuple(outs),
        in_specs=[near] * len(ops),
        out_specs=(near,) * len(outs),
        scratch_shapes=list(scratch),
        cost_estimate=cost(name),
        name=name,
    )(*ops)


def aligned(x, n):
    return pl.multiple_of(x, n)


def after(x, *others):
    return lax.optimization_barrier((x, *others))[0]


def mine_of(k):
    return lax.div(lax.axis_index("dp"), 1 << k) & 1


def pack_body(w_qkv, gain_a, gain_m, w_up, w_down, w_out, qkv, keep, give):
    rows, half = w_up.shape[0], w_up.shape[1] // 2
    width = w_out.shape[0]
    mine = mine_of(0)
    qkv[...] = jnp.zeros_like(qkv)
    for c in range(3):
        qkv[:, c * PAD : c * PAD + width] = w_qkv[c]
    eye = lax.broadcasted_iota(jnp.int32, (rows, rows), 0) == lax.broadcasted_iota(jnp.int32, (rows, rows), 1)
    lane = lax.broadcasted_iota(jnp.int32, (rows, LANE), 1)
    cols = [jnp.sum(jnp.where(eye, g[...].astype(f32), 0.0), axis=1, keepdims=True) for g in (gain_a, gain_m)]
    qkv[:, 3 * PAD :] = jnp.where(lane == 0, cols[0], jnp.where(lane == 1, cols[1], 0.0)).astype(bf16)
    tiles = half // LANE
    for k in range(tiles):
        for to, which in ((keep, mine), (give, 1 - mine)):
            at = which * half + k * LANE
            to[k * rows : (k + 1) * rows] = w_up[:, pl.ds(aligned(at, LANE), LANE)]
            to[(tiles + k) * rows : (tiles + k + 1) * rows] = w_down[:, pl.ds(aligned(at, LANE), LANE)]
    base = 2 * tiles * rows
    back = w_out[...].astype(f32).T.astype(bf16)
    keep[base : base + rows] = back[:, 0:LANE]
    keep[base + rows : base + 2 * rows] = jnp.zeros((rows, LANE), bf16)
    keep[base + rows : base + 2 * rows, 0 : width - LANE] = back[:, LANE:width]


def unpack_qkv_body(near, far, w, gains):
    me = lax.axis_index("dp")
    rows = near.shape[1]
    count = near.shape[0]
    tail = []
    for p in range(2 * count):
        src = near if p < count else far
        mask = 2 * (p % count) + (1 if p >= count else 0)
        w[pl.ds(aligned((me ^ mask) * rows, 32), rows)] = src[p % count, :, : 3 * PAD]
    for b in range(2 * count):
        mask = me ^ b
        part = lax.div(mask, 2)
        col = jnp.where(
            (mask & 1) == 0, near[part, :, 3 * PAD :].astype(f32), far[part, :, 3 * PAD :].astype(f32)
        )
        tail.append(col)
    gains[...] = jnp.concatenate(tail, axis=0).T[0:8]


def norm_qkv_body(xa, xb, w, gains, normed, qa, qb):
    for half, (x, q) in enumerate(((xa, qa), (xb, qb))):
        size = x.shape[0]

        for r in range(0, size, 64):
            v = x[r : r + 64].astype(f32)
            c = v - jnp.mean(v, axis=-1, keepdims=True)
            rstd = lax.rsqrt(jnp.mean(c * c, axis=-1, keepdims=True) + EPS)
            normed[half * size + r : half * size + r + 64] = (c * rstd * gains[0:1]).astype(bf16)

        q[...] = nn(normed[half * size : (half + 1) * size], w[...]).astype(bf16).T


def stack_body(*refs):
    parts, (a, b) = refs[:-2], refs[-2:]
    u = b.shape[1] // 2
    for s, p in enumerate(parts):
        a[s, 0:u] = p[0:u]
        b[s, 0:u] = p[u : 2 * u]
        a[s, u : 2 * u] = p[2 * u : 3 * u]
        b[s, u : 2 * u] = p[3 * u : 4 * u]
        a[s, 2 * u :] = p[4 * u :]


def unpack_body(*refs):
    early, late, (up, down, back) = refs[0:8], refs[8:16], refs[16:19]
    me = lax.axis_index("dp")
    rows = 96
    half = up.shape[1] // RING
    tiles = half // LANE
    span = tiles * rows
    for p in range(4):
        for s in range(RING):
            came = early if s < early[0].shape[0] else late
            a, b, at = came[p], came[4 + p], s % early[0].shape[0]
            for rc in range(2):
                to_a = pl.ds(aligned((me ^ (2 * p + rc)) * rows, 32), rows)
                to_b = pl.ds(aligned((me ^ (2 * ((p & 1) * 2 + (p >> 1)) + rc)) * rows, 32), rows)
                for k in range(tiles):
                    cols = slice(s * half + k * LANE, s * half + (k + 1) * LANE)
                    src = slice(rc * span + k * rows, rc * span + (k + 1) * rows)
                    up[to_a, cols] = a[at, src]
                    down[to_b, cols] = b[at, src]
            where = lax.div(me ^ (2 * p), 2)
            for k in range(2):
                back[where, s, :, k * LANE : (k + 1) * LANE] = a[at, 2 * span + k * rows : 2 * span + (k + 1) * rows]


def project_body(x, a0, a1, a2, a3, near, far, gains, mixed, mlp, tokens_major, w):
    mine = mine_of(0)
    rows = near.shape[2]
    width = a0.shape[0]
    for b in range(near.shape[0]):
        for s in range(RING):
            w[s, pl.ds(aligned((2 * b + mine) * rows, 32), rows)] = near[b, s]
            w[s, pl.ds(aligned((2 * b + 1 - mine) * rows, 32), rows)] = far[b, s]
    zero = jnp.zeros((PAD - width, a0.shape[1]), bf16)
    for s, a in enumerate((a0, a1, a2, a3)):
        tokens_major[:, s * PAD : (s + 1) * PAD] = jnp.concatenate([a[...], zero], axis=0).T
    for r in range(0, x.shape[0], 128):
        total = x[r : r + 128].astype(f32)
        for s in range(RING):
            total = total + nt(tokens_major[r : r + 128, s * PAD : (s + 1) * PAD], w[s])
        mixed[r : r + 128] = total
    normalise(mixed, gains[1:2], mlp)


def normalise(rows, gain, out):
    for r in range(0, rows.shape[0], 64):
        at = slice(r, r + 64)
        v = rows[at]
        c = v - jnp.mean(v, axis=-1, keepdims=True)
        rstd = lax.rsqrt(jnp.mean(c * c, axis=-1, keepdims=True) + EPS)
        out[at] = (c * rstd * gain).astype(bf16)


def gelu_both(v):
    square = v * v
    t = jnp.tanh(v * (0.7978845608028654 + (0.7978845608028654 * 0.044715) * square))
    gate = 0.5 + 0.5 * t
    bend = v * (2 * 0.7978845608028654 + (6 * 0.7978845608028654 * 0.044715) * square)
    return v * gate, gate + gate * (1.0 - gate) * bend


def mlp_body(x0, x1, g0, g1, up, down, active, grad, hid, push):
    size = x0.shape[0]
    for half, (x, g) in enumerate(((x1, g1), (x0, g0))):
        hid[half] = nn(x[...], up[...])
        push[half] = nn(g[...], down[...])
    for half in range(2):
        for r in range(0, size, 64):
            rows = slice(r, r + 64)
            to = slice((1 - half) * size + r, (1 - half) * size + r + 64)
            value, slope = gelu_both(hid[half, rows])
            active[to] = value.astype(bf16)
            grad[to] = (push[half, rows] * slope).astype(bf16)


def mlp(x0, x1, g0, g1, up, down):
    tokens, dim = x0.shape
    hidden = up.shape[1]
    keep = pl.BlockSpec((tokens, dim), lambda n: (0, 0))
    cols = pl.BlockSpec((dim, BLOCK), lambda n: (0, n))
    wide = pl.BlockSpec((2 * tokens, BLOCK), lambda n: (0, n))
    return pl.pallas_call(
        mlp_body,
        out_shape=(sds((2 * tokens, hidden)), sds((2 * tokens, hidden))),
        grid=(hidden // BLOCK,),
        in_specs=[keep] * 4 + [cols] * 2,
        out_specs=(wide, wide),
        scratch_shapes=[pltpu.VMEM((2, tokens, BLOCK), f32), pltpu.VMEM((2, tokens, BLOCK), f32)],
        cost_estimate=cost("mlp"),
        name="mlp",
    )(x0, x1, g0, g1, up, down)


def norm_back(v, gain, grad):
    c = v - jnp.mean(v, axis=-1, keepdims=True)
    rstd = lax.rsqrt(jnp.mean(c * c, axis=-1, keepdims=True) + EPS)
    hat = c * rstd
    g = grad * gain
    return rstd * (g - jnp.mean(g, axis=-1, keepdims=True) - hat * jnp.mean(g * hat, axis=-1, keepdims=True))


def branch_body(mixed, part, far, grad_out, gains, w, grad_mixed, branch, *heads):
    for r in range(0, mixed.shape[0], 64):
        at = slice(r, r + 64)
        grad = part[at] + far[at].astype(f32)
        total = grad_out[at].astype(f32) + norm_back(mixed[at], gains[1:2], grad)
        grad_mixed[at] = total
        branch[at] = total.astype(bf16)

    width = heads[0].shape[0]
    for s in range(RING):
        heads[s][...] = nn(branch[...], w[s]).astype(bf16).T[0:width]


def back_body(grad, w, *outs, blocks):
    for out, n in zip(outs, blocks):
        out[...] = nt(grad[:, n * BLOCK : (n + 1) * BLOCK].T, w[...]).astype(bf16)


def finish_body(*refs):
    parts, recvs, (x, grad_mixed, gains, out) = refs[0:2], refs[2:4], refs[4:]
    for k, (part, recv) in enumerate(zip(parts, recvs)):
        for r in range(0, BLOCK, 64):
            grad = part[r : r + 64].astype(f32) + recv[r : r + 64].astype(f32)
            at = slice(k * BLOCK + r, k * BLOCK + r + 64)
            out[at] = grad_mixed[at] + norm_back(x[at].astype(f32), gains[0:1], grad)


def turn(x, shift):
    return lax.ppermute(x, "tensor", [(i, (i + shift) % RING) for i in range(RING)])


def swap(x, axis, bit, size):
    return lax.ppermute(x, axis, [(i, i ^ bit) for i in range(size)])


def pick(x, index, axis=0):
    return lax.dynamic_index_in_dim(x, index, axis, keepdims=False)


def ring_gather(x):
    got = [x]
    for _ in range(RING - 1):
        got.append(turn(got[-1], 1))
    return got


def ring_reduce(chunks):
    moving = chunks[1].astype(bf16)
    for r in range(1, RING):
        moved = turn(moving, 1)
        total = moved.astype(f32) + chunks[(r + 1) % RING]
        moving = total.astype(bf16)
    return total


def spread_blocks(x, bits, size):
    for bit in bits:
        x = jnp.concatenate([x, swap(x, "dp", bit, size)])
    return x


def place_of(mask, bits):
    place = 0
    for k, bit in enumerate(bits):
        place = place + jnp.where(mask & bit != 0, 1 << k, 0)
    return place


def halve(blocks, left, bit, me, size):
    at = left.index(bit)
    lead, tail = 1 << at, 1 << (len(left) - at - 1)
    split = blocks.reshape((lead, 2, tail) + blocks.shape[1:])
    mine = jnp.where(me & bit != 0, 1, 0)
    send = pick(split, 1 - mine, 1).astype(bf16)
    keep = pick(split, mine, 1)
    total = keep.astype(f32) + swap(send, "dp", bit, size).astype(f32)
    return total.reshape((lead * tail,) + blocks.shape[1:]), [b for b in left if b != bit]


def centre(rows):
    shifted = rows - jnp.mean(rows, axis=-1, keepdims=True)
    rstd = lax.rsqrt(jnp.mean(shifted * shifted, axis=-1, keepdims=True) + EPS)
    return shifted * rstd, rstd


def norm_back_plain(grad_hat, hat, rstd):
    return rstd * (
        grad_hat
        - jnp.mean(grad_hat, axis=-1, keepdims=True)
        - hat * jnp.mean(grad_hat * hat, axis=-1, keepdims=True)
    )


def einf(spec, a, b):
    return jnp.einsum(spec, a, b, preferred_element_type=f32)


def shards(size, inputs, doc_ids, gain_attn, w_qkv, w_out, gain_mlp, w_up, w_down, grad_out):
    me = lax.axis_index("dp")
    z = lax.axis_index("tensor")
    odd = me & 1
    others = [1 << k for k in range(1, size.bit_length() - 1)]
    documents = doc_ids[0]
    tokens, dim = inputs.shape
    rows = dim // size
    hid = w_up.shape[1]
    half = hid // 2
    width = w_out.shape[0]
    scal = jnp.stack([z, jnp.sum(documents < 1), jnp.sum(documents < 2)]).astype(jnp.int32)

    pieces = [ring_gather(inputs[k : k + BLOCK]) for k in range(0, tokens, BLOCK)]

    gains = jnp.stack([gain_attn, gain_mlp])
    own = jnp.concatenate([w_qkv[0], w_qkv[1], w_qkv[2], jnp.pad(gains, ((0, 62), (0, 0))).T], axis=1)
    order = others + [1]
    spread_qkv = spread_blocks(own[None], order, size)
    full = jnp.concatenate([pick(spread_qkv, place_of(me ^ b, order)) for b in range(size)])
    full_qkv = full[:, : 3 * width]
    gain_one = full[:, 3 * width].astype(f32)
    gain_two = full[:, 3 * width + 1].astype(f32)

    out_rows = jnp.concatenate([w_out.T[: rows // 2], w_out.T[rows // 2 :]], axis=1)

    def pair_half(w):
        parts = w.reshape(rows, 2, half)
        return jnp.concatenate([pick(parts, odd, 1), swap(pick(parts, 1 - odd, 1), "dp", 1, size)])

    pack_a = jnp.concatenate([pair_half(w_up), out_rows])
    pack_b = pair_half(w_down.T)
    ring_a = jnp.stack(ring_gather(pack_a))
    ring_b = jnp.stack(ring_gather(pack_b))
    order_b = others[::-1]
    spread_a = spread_blocks(ring_a[None], others, size)
    spread_b = spread_blocks(ring_b[None], order_b, size)

    def assemble(spread_w, bits):
        blocks = []
        for b in range(size):
            mask = me ^ b
            block = pick(spread_w, place_of(mask, bits))[:, : 2 * rows]
            block = pick(block.reshape(RING, 2, rows, half), mask & 1, 1)
            blocks.append(block.transpose(1, 0, 2).reshape(rows, RING * half))
        return jnp.concatenate(blocks)

    full_up = assemble(spread_a, others)
    full_down = assemble(spread_b, order_b)
    out_part = spread_a[:, :, 2 * rows :]
    out_both = jnp.stack([out_part, swap(out_part, "dp", 1, size)])

    def out_block(b):
        mask = me ^ b
        block = pick(pick(out_both, mask & 1), place_of(mask, others))
        block = jnp.concatenate([block[..., :width], block[..., width:]], axis=1)
        return block.transpose(1, 0, 2).reshape(rows, RING * width)

    full_out = jnp.concatenate([out_block(b) for b in range(size)])
    grad_both = jnp.concatenate([grad_out, swap(grad_out, "dp", 1, size)])
    grad_active = einf("td,df->tf", grad_both, full_down)

    normed = []
    parts = []
    for s in range(RING):
        for piece in pieces:
            hat, _ = centre(piece[s].astype(f32))
            normed.append((hat * gain_one).astype(bf16))
            part = einf("de,td->et", full_qkv, normed[-1]).astype(bf16).reshape(3, width, BLOCK)
            parts.append(jnp.pad(part, ((0, 0), (0, PAD - width), (0, 0))).reshape(3 * PAD, BLOCK))
    normed = jnp.concatenate(normed)
    *sent, lse = attn_fwd(scal, parts, width // HEAD_DIM)
    attended = jnp.concatenate([sent[0]] + [turn(sent[s], s) for s in range(1, RING)])
    mixed = inputs.astype(f32) + einf("et,de->td", attended, full_out)
    hat_two, rstd_two = centre(mixed)
    mlp_rows = (hat_two * gain_two).astype(bf16)
    mlp_both = jnp.concatenate([mlp_rows, swap(mlp_rows, "dp", 1, size)])
    hidden = einf("td,df->tf", mlp_both, full_up)
    value, slope = gelu_both(hidden)
    active = value.astype(bf16)
    grad_hidden = (grad_active * slope).astype(bf16)
    grad_part = einf("tf,df->td", grad_hidden, full_up)
    grad_mlp = grad_part[:tokens] + swap(grad_part[tokens:].astype(bf16), "dp", 1, size).astype(f32)
    grad_mixed = grad_out.astype(f32) + norm_back_plain(grad_mlp * gain_two, hat_two, rstd_two)
    grad_branch = grad_mixed.astype(bf16)
    grad_att = einf("de,td->et", full_out, grad_branch).astype(bf16).reshape(RING, width, tokens)
    grads = [grad_att[0]] + [turn(grad_att[s], -s) for s in range(1, RING)]

    out_pair = einf("tf,df->td", active, full_down)
    layer_out = (
        mixed + out_pair[:tokens] + swap(out_pair[tokens:].astype(bf16), "dp", 1, size).astype(f32)
    ).astype(bf16)

    bits = [1 << k for k in reversed(range(size.bit_length() - 1))]

    def scatter(grad, stages, last_width):
        blocks, left = grad.reshape(size, rows, grad.shape[1]), list(bits)
        for bit in stages:
            blocks, left = halve(blocks, left, bit, me, size)
        blocks = blocks.reshape(-1, blocks.shape[-1])
        return ring_reduce([blocks[:, s * last_width : (s + 1) * last_width] for s in range(RING)])

    def pair_whole(block):
        block = block.reshape(2, rows, half)
        send = pick(block, 1 - odd).astype(bf16)
        keep = pick(block, odd)
        other = swap(send, "dp", 1, size).astype(f32)
        return jnp.where(odd == 0, jnp.concatenate([keep, other], axis=1), jnp.concatenate([other, keep], axis=1))

    grad_down = pair_whole(scatter(einf("td,tf->df", grad_both, active), others, half)).T
    grad_up = pair_whole(scatter(einf("td,tf->df", mlp_both, grad_hidden), order_b, half))
    grad_o = scatter(einf("td,et->de", grad_branch, attended), [1] + order_b, width).T

    grad_parts = attn_bwd(scal, parts, sent, grads, lse)
    grad_parts = grad_parts.reshape(3, PAD, -1)[:, :width].reshape(3 * width, -1)
    grad_proj = einf("td,et->de", normed, grad_parts)
    blocks, left = grad_proj.reshape(size, rows, 3 * width), list(bits)
    for bit in [1] + order_b:
        blocks, left = halve(blocks, left, bit, me, size)
    grad_qkv = blocks[0].reshape(rows, 3, width).transpose(1, 0, 2)

    back = []
    for k in range(0, tokens, BLOCK):
        back.append(
            ring_reduce(
                [
                    einf("et,de->td", grad_parts[:, s * tokens + k : s * tokens + k + BLOCK], full_qkv)
                    for s in range(RING)
                ]
            )
        )
    grad_normed = jnp.concatenate(back)
    hat_one, rstd_one = centre(inputs.astype(f32))
    grad_inputs = grad_mixed + norm_back_plain(grad_normed * gain_one, hat_one, rstd_one)

    sums = jnp.stack(
        [
            jnp.sum(w_qkv.astype(f32) * grad_qkv, axis=(0, 2)),
            jnp.sum(w_up.astype(f32) * grad_up, axis=1),
        ]
    )
    for bit in (1, 2):
        sums = sums + swap(sums, "tensor", bit, RING)
    sums = sums / gains.astype(f32)
    return layer_out, grad_inputs, sums[0], grad_qkv, grad_o, sums[1], grad_up, grad_down


def add(a, b):
    return (a.astype(f32) + b.astype(f32)).astype(bf16)


def first_body(full, recv, send, keep, *, by_y):
    c = mine_of(0)
    mine = mine_of(2 if by_y else 1)
    for k in range(2):
        for which, to in ((mine, keep), (1 - mine, send)):
            at = which * 2 + k if by_y else k * 2 + which
            to[k] = add(full[at * 2 + c], recv[at])


def second_body(keep_in, recv, send, keep):
    mine = mine_of(1)
    keep[...] = add(keep_in[mine], recv[mine])
    send[...] = add(keep_in[1 - mine], recv[1 - mine])


def third_body(up, far_up, down, far_down, o, far_o, up_send, up_keep, mix_send, mix_keep):
    c, x, y = mine_of(0), mine_of(1), mine_of(2)
    rows = up.shape[1]
    tiles = up.shape[2] // RING // LANE
    span = tiles * rows
    for s in range(RING):
        for rc in range(2):
            side = jnp.bitwise_xor(c, rc)
            for k in range(tiles):
                cols = slice((s * tiles + k) * LANE, (s * tiles + k + 1) * LANE)
                to = slice(rc * span + k * rows, rc * span + (k + 1) * rows)
                for which, out in ((x, up_keep), (1 - x, up_send)):
                    out[s, to] = add(up[y * 4 + which * 2 + side, :, cols], far_up[which * 2 + side, :, cols])
                for which, out in ((y, mix_keep), (1 - y, mix_send)):
                    out[s, to] = add(down[which * 4 + x * 2 + side, :, cols], far_down[which * 2 + side, :, cols])
        for k in range(2):
            cols = slice((s * 2 + k) * LANE, (s * 2 + k + 1) * LANE)
            to = slice(2 * span + k * rows, 2 * span + (k + 1) * rows)
            for which, out in ((y, mix_keep), (1 - y, mix_send)):
                out[s, to] = add(o[which, :, cols], far_o[which, :, cols])


def fourth_body(up, far_up, mix, far_mix, first, rest):
    span = up.shape[1] // 2
    extra = mix.shape[1] - 2 * span
    for s in range(RING):
        for rc in range(2):
            src = slice(rc * span, (rc + 1) * span)
            at = rc * 2 * span
            rest[s, at : at + span] = add(up[s, src], far_up[s, src])
            rest[s, at + span : at + 2 * span] = add(mix[s, src], far_mix[s, src])
        tail = slice(2 * span, 2 * span + extra)
        rest[s, 4 * span : 4 * span + extra] = add(mix[s, tail], far_mix[s, tail])
    first[...] = rest[1]


def fifth_body(mine, far, up, down, o):
    c = mine_of(0)
    rows = up.shape[0]
    half = up.shape[1] // 2
    tiles = half // LANE
    for side, src in ((c, mine), (1 - c, far)):
        for k in range(tiles):
            at = pl.ds(aligned(side * half + k * LANE, LANE), LANE)
            up[:, at] = src[k * rows : (k + 1) * rows].astype(f32)
            down[:, at] = src[(tiles + k) * rows : (tiles + k + 1) * rows].astype(f32)
    base = 4 * tiles * rows
    width = o.shape[0]
    o[0:LANE] = mine[base : base + rows].astype(f32).T
    o[LANE:width] = mine[base + rows : base + 2 * rows].astype(f32).T[0 : width - LANE]


def shards_small(size, inputs, doc_ids, gain_attn, w_qkv, w_out, gain_mlp, w_up, w_down, grad_out):
    me = lax.axis_index("dp")
    z = lax.axis_index("tensor")
    documents = doc_ids[0]
    tokens, dim = inputs.shape
    rows, hid = w_up.shape
    half = hid // 2
    width = w_out.shape[0]
    heads = width // HEAD_DIM
    hidden = RING * half
    scal = jnp.stack([z, jnp.sum(documents < 1), jnp.sum(documents < 2)]).astype(jnp.int32)

    def pair(x):
        return swap(x, "dp", 1, size)

    def along_x(x):
        return swap(x, "dp", 2, size)

    def along_y(x):
        return swap(x, "dp", 4, size)

    span = half * rows // LANE
    x_a, x_b = ([inputs[k : k + BLOCK]] for k in range(0, tokens, BLOCK))

    def hop():
        x_a.append(turn(x_a[-1], 1))
        x_b.append(turn(x_b[-1], 1))

    hop()
    qkv, keep, give = call(
        pack_body,
        [sds((rows, 3 * PAD + LANE)), sds((2 * span + 2 * rows, LANE)), sds((2 * span, LANE))],
        w_qkv, gain_attn[None], gain_mlp[None], w_up, w_down.T, w_out, name="pack",
    )
    got = pair(after(give, x_a[1]))
    qkv = jnp.stack([qkv, along_x(qkv)])
    packed = jnp.concatenate([keep[: 2 * span], got, keep[2 * span :]])
    qkv = jnp.concatenate([qkv, along_y(qkv)])
    qkv_far = pair(qkv)
    ring = [packed, turn(after(packed, x_a[1], x_b[1]), 1)]
    hop()
    ring.append(turn(after(ring[1], x_a[2], x_b[2]), 1))
    hop()
    grad_far = pair(after(grad_out, x_a[2]))
    full_qkv, gains = call(
        unpack_qkv_body, [sds((dim, 3 * PAD)), sds((8, dim), f32)], qkv, qkv_far, name="unpack_qkv"
    )
    normed, parts = [], []
    for s in range(RING):
        n, qa, qb = call(
            norm_qkv_body,
            [sds((tokens, dim)), sds((3 * PAD, BLOCK)), sds((3 * PAD, BLOCK))],
            x_a[s], x_b[s], full_qkv, gains, name="norm_qkv",
        )
        normed.append(n)
        parts.extend((qa, qb))

    ring.append(turn(after(ring[2], normed[0]), 1))

    def spread(*shares):
        n = len(shares)
        u0, d0 = call(
            stack_body, [sds((n, 2 * span + 2 * rows, LANE)), sds((n, 2 * span, LANE))], *shares, name="stack"
        )
        u1, d1 = along_x(u0), along_y(d0)
        u2, d2 = along_y(u0), along_x(d0)
        return u0, u1, u2, d0, d1, d2

    def spread_on(blocks, *others):
        u0, u1, u2, d0, d1, d2 = blocks
        return u0, u1, u2, along_y(after(u1, *others)), d0, d1, d2, along_x(after(d1, *others))

    early = spread_on(spread(*ring[:2], after(ring[2], normed[0], normed[1])), normed[2])
    late = spread(ring[3])

    *sent, lse = attn_fwd(after(scal, late[0]), parts, heads)
    attended = [sent[0]] + [turn(sent[s], s) for s in range(1, RING)]
    late = spread_on(late, sent[0])
    full_up, full_down, back_near = call(
        unpack_body,
        [sds((dim, hidden)), sds((dim, hidden)), sds((size // 2, RING, rows, PAD))],
        *early, *late[:-1], after(late[-1], *attended[1:]), name="unpack",
    )
    back_far = pair(back_near)
    mixed, mlp_rows, att_tokens, full_out = call(
        project_body,
        [sds((tokens, dim), f32), sds((tokens, dim)), sds((tokens, RING * PAD)), sds((RING, dim, PAD))],
        inputs, *attended, back_near, back_far, gains, name="project",
    )
    mlp_far = pair(mlp_rows)
    active, grad_hidden = mlp(mlp_rows, mlp_far, grad_out, grad_far, full_up, full_down)
    part_got = pair(einf("tf,df->td", grad_hidden[tokens:], full_up).astype(bf16))
    part = einf("tf,df->td", grad_hidden[:tokens], full_up)
    grad_mixed, branch, *grad_att = call(
        branch_body,
        [sds((tokens, dim), f32), sds((tokens, dim)), *[sds((width, tokens))] * RING],
        mixed, part, part_got, grad_out, gains, full_out, name="branch",
    )
    grads = [grad_att[0]] + [turn(grad_att[s], -s) for s in range(1, RING)]
    grad_hidden_late = after(grad_hidden, branch)
    active_late = after(active, branch)

    x_bit, y_bit, c_bit = lax.div(me, 2) & 1, lax.div(me, 4) & 1, me & 1
    both_in = jnp.concatenate([mlp_rows, mlp_far])
    both_grad = jnp.concatenate([grad_out, grad_far])
    grad_up = einf("td,tf->df", both_in, grad_hidden_late).astype(bf16)
    grad_down = einf("td,tf->df", both_grad, active_late).astype(bf16)
    far_up = along_y(pick(grad_up.reshape(2, 4, rows, hidden), 1 - y_bit))
    far_down = along_x(pick(grad_down.reshape(2, 2, 2, rows, hidden), 1 - x_bit, 1).reshape(4, rows, hidden))
    grad_o = einf("td,te->de", branch, att_tokens).astype(bf16)
    far_o = pair(pick(grad_o.reshape(4, 2, rows, RING * PAD), 1 - c_bit, 1))
    layer_far = pair(einf("tf,df->td", active_late[tokens:], full_down).astype(bf16))
    layer_near = einf("tf,df->td", active_late[:tokens], full_down)
    layer_out = (mixed + layer_near + layer_far.astype(f32)).astype(bf16)

    o_send, o_keep = call(
        functools.partial(first_body, by_y=False),
        [sds((2, rows, RING * PAD))] * 2, grad_o.reshape(size, rows, RING * PAD), far_o, name="first_o",
    )

    grad_parts = attn_bwd(scal, parts, sent, grads, after(lse, layer_out, o_send))
    count = tokens // BLOCK

    def backs(grad, blocks, name):
        return call(
            functools.partial(back_body, blocks=blocks), [sds((BLOCK, dim))] * len(blocks), grad, full_qkv, name=name
        )

    start = backs(grad_parts, list(range(count, 2 * count)), "back_first")
    came = [turn(start[k], 1) for k in range(count)]
    later = backs(
        after(grad_parts, *start), list(range(2 * count, RING * count)) + list(range(count)), "back_rest"
    )
    up_shape, mix_shape = sds((RING, 2 * span, LANE)), sds((RING, 2 * span + 2 * rows, LANE))
    up_send, up_keep, mix_send, mix_keep = call(
        third_body,
        [up_shape, up_shape, mix_shape, mix_shape],
        grad_up.reshape(size, rows, hidden), far_up, grad_down.reshape(size, rows, hidden), far_down,
        o_keep, along_x(o_send), name="third",
    )
    far_up_two, far_mix_two = along_x(up_send), along_y(mix_send)
    sums = [add(after(later[k], up_send), came[k]) for k in range(count)]
    came = [turn(x, 1) for x in sums]
    total_shape = (4 * span + 2 * rows, LANE)
    moving, rest = call(
        fourth_body,
        [sds(total_shape), sds((RING, *total_shape))],
        up_keep, far_up_two, mix_keep, far_mix_two, name="fourth",
    )

    came = [turn(add(later[count + k], came[k]), 1) for k in range(count)]
    grad_inputs = call(
        finish_body,
        [sds((tokens, dim), f32)],
        *later[(RING - 2) * count :], *came, inputs, grad_mixed, gains, name="finish",
    )[0]

    grad_proj = einf("td,et->de", jnp.concatenate(normed), after(grad_parts, up_send, *sums)).astype(bf16)
    far_qkv = pair(pick(grad_proj.reshape(4, 2, rows, 3 * PAD), 1 - c_bit, 1))
    q_send, q_keep = call(
        functools.partial(first_body, by_y=True),
        [sds((2, rows, 3 * PAD))] * 2, grad_proj.reshape(size, rows, 3 * PAD), far_qkv, name="first_qkv",
    )
    q_send, q_keep = call(
        second_body, [sds((rows, 3 * PAD))] * 2, q_keep, along_y(q_send), name="second_qkv"
    )
    grad_flat = q_keep.astype(f32) + along_x(q_send).astype(f32)
    grad_qkv = jnp.stack([grad_flat[:, c * PAD : c * PAD + width] for c in range(3)])

    for r in range(1, RING):
        moving = add(turn(moving, 1), rest[(r + 1) % RING])
    grad_up, grad_down, grad_o = call(
        fifth_body,
        [sds((rows, hid), f32), sds((rows, hid), f32), sds((width, rows), f32)],
        after(moving, grad_inputs), pair(moving[2 * span : 4 * span]), name="fifth",
    )
    sums = jnp.stack(
        [
            jnp.sum(w_qkv.astype(f32) * grad_qkv, axis=(0, 2)),
            jnp.sum(w_up.astype(f32) * grad_up, axis=1),
        ]
    )
    sums = sums + turn(sums, 1) + turn(sums, 2) + turn(sums, 3)
    own = jnp.stack([gain_attn, gain_mlp]).astype(f32)
    sums = sums / own
    return layer_out, grad_inputs, sums[0], grad_qkv, grad_o, sums[1], grad_up, grad_down.T


def solution(mesh):
    both = P(("dp", "tensor"), None)
    weights = (P(None, "dp", "tensor"), P("tensor", "dp"), P("dp"), P("dp", "tensor"), P("tensor", "dp"))
    return jax.shard_map(
        functools.partial(shards_small if mesh.shape["dp"] == 8 else shards, mesh.shape["dp"]),
        mesh=mesh,
        in_specs=(both, P("dp", None), P("dp"), *weights, both),
        out_specs=(both, both, P("dp"), *weights),
        check_vma=False,
    )
```

```python
import functools

import jax
import jax.numpy as jnp
from jax import lax
from jax.experimental import pallas as pl
from jax.experimental.pallas import tpu as pltpu
from jax.sharding import PartitionSpec as P

HEAD_DIM = 64
BLOCK = 256
PAD = 256
RING = 4
EPS = 1e-05
LOG2E = 1.4426950408889634
f32 = jnp.float32
bf16 = jnp.bfloat16
HIDE = -1e30


def nn(a, b):
    return lax.dot_general(a, b, (((1,), (0,)), ((), ())), preferred_element_type=f32)


def nt(a, b):
    return lax.dot_general(a, b, (((1,), (1,)), ((), ())), preferred_element_type=f32)


def doc_of(place, ends):
    return jnp.where(place >= ends[1], 2, jnp.where(place >= ends[0], 1, 0))


def doc_start(row, ends):
    return jnp.where(row >= ends[1], ends[1], jnp.where(row >= ends[0], ends[0], 0))


def hidden_bias(i, j, ends):
    keys = j * BLOCK + lax.broadcasted_iota(jnp.int32, (BLOCK, BLOCK), 0)
    rows = i * BLOCK + lax.broadcasted_iota(jnp.int32, (1, BLOCK), 1)
    start = doc_start(rows, ends)
    stop = jnp.where(rows >= ends[1], 1 << 30, jnp.where(rows >= ends[0], ends[1], ends[0]))
    return jnp.where((keys >= start) & (keys < stop), 0.0, HIDE)


def signed(s, size):
    low = size.astype(bf16)
    return jnp.clip(s.astype(bf16) * bf16(1e38), -low, low)


def ring_blocks(z, count):
    for n in range(count):
        yield n, lax.rem(z - n // 2 + RING, RING) * 2 + n % 2


def walk(i, ends, step, carry):
    def body(j, carry):
        mixed = doc_of(j * BLOCK, ends) != doc_of(i * BLOCK + BLOCK - 1, ends)
        return lax.cond(mixed, lambda c: step(j, c, hidden_bias(i, j, ends)), lambda c: step(j, c, None), carry)

    first = lax.div(doc_start(i * BLOCK, ends), BLOCK)
    return lax.fori_loop(first, i + 1, body, carry)


def head_rows(h, base=0):
    return slice(base + h * HEAD_DIM, base + (h + 1) * HEAD_DIM)


def two_parts(q):
    scaled = q.astype(f32) * (0.125 * LOG2E)
    high = scaled.astype(bf16)
    return high, (scaled - high.astype(f32)).astype(bf16)


def twice(k):
    return jnp.concatenate([k, k], axis=0).T


CHUNK = 64


def chunks():
    return [slice(r, r + CHUNK) for r in range(0, BLOCK, CHUNK)]


def size_of(s, bias, rows):
    a = jnp.abs(s)
    return a if bias is None else a + bias[rows]


def attn_fwd_body(scal, *refs):
    parts, refs = refs[:-12], refs[-12:]
    outs, (lse, qs, vs, ks, acc, held, low, out) = refs[:RING], refs[RING:]
    i = pl.program_id(0)
    heads, width = ks.shape[0], vs.shape[1]
    z = scal[0]
    ends = (scal[1], scal[2])

    @pl.when(i == 0)
    def _():
        for n, b in ring_blocks(z, len(parts)):
            ref = parts[n]
            vs[b] = ref[2 * PAD : 2 * PAD + width]
            for h in range(heads):
                high, rest = two_parts(ref[head_rows(h)])
                qs[h, b, 0:HEAD_DIM] = high
                qs[h, b, HEAD_DIM : 2 * HEAD_DIM] = rest
                ks[h, b] = twice(ref[head_rows(h, PAD)])

    acc[...] = jnp.zeros_like(acc)

    def largest(j, carry, bias):
        new = []
        for h in range(heads):
            s = nn(ks[h, j], qs[h, i])
            held[h, j] = s
            top = carry[h]
            for rows in chunks():
                top = jnp.maximum(top, jnp.max(size_of(s[rows], bias, rows).reshape(-1, 8, BLOCK), axis=0))
            new.append(top)
        return tuple(new)

    zero = jnp.zeros((8, BLOCK), f32)
    tops = walk(i, ends, largest, (zero,) * heads)
    tops = [jnp.max(t, axis=0, keepdims=True) for t in tops]

    def weigh(j, carry, bias):
        new = []
        for h in range(heads):
            total = carry[h]
            for rows in chunks():
                s = held[h, j, rows]
                p = jnp.exp2(size_of(s, bias, rows) - tops[h])
                total = total + jnp.sum(p.reshape(-1, 8, BLOCK), axis=0)
                low[h, rows] = signed(s, p)
            new.append(total)
        for h in range(heads):
            acc[head_rows(h)] += nn(vs[j, head_rows(h)], low[h])
        return tuple(new)

    totals = walk(i, ends, weigh, (zero,) * heads)
    t = lax.div(i, 2)
    cols = pl.ds(pl.multiple_of(lax.rem(i, 2) * BLOCK, BLOCK), BLOCK)
    dest = lax.rem(t - z + RING, RING)
    for h in range(heads):
        l = jnp.sum(totals[h], axis=0, keepdims=True)
        out[dest, head_rows(h), cols] = (acc[head_rows(h)] / l).astype(bf16)
        lse[i, h : h + 1, :] = tops[h] + jnp.log(l) * LOG2E

    @pl.when(i == pl.num_programs(0) - 1)
    def _():
        for s, ref in enumerate(outs):
            ref[...] = out[s]


def whole(shape):
    return pl.BlockSpec(shape, lambda *_: (0,) * len(shape))


def sds(shape, dtype=bf16):
    return jax.ShapeDtypeStruct(shape, dtype)


def attn_fwd(scal, parts, heads):
    nb = len(parts)
    width, cols = heads * HEAD_DIM, nb // RING * BLOCK
    return pl.pallas_call(
        attn_fwd_body,
        out_shape=(*[sds((width, cols))] * RING, sds((nb, 8, BLOCK), f32)),
        grid_spec=pltpu.PrefetchScalarGridSpec(
            num_scalar_prefetch=1,
            grid=(nb,),
            in_specs=[whole(p.shape) for p in parts],
            out_specs=(*[whole((width, cols))] * RING, whole((nb, 8, BLOCK))),
            scratch_shapes=[
                pltpu.VMEM((heads, nb, 2 * HEAD_DIM, BLOCK), bf16),
                pltpu.VMEM((nb, width, BLOCK), bf16),
                pltpu.VMEM((heads, nb, BLOCK, 2 * HEAD_DIM), bf16),
                pltpu.VMEM((width, BLOCK), f32),
                pltpu.VMEM((heads, nb, BLOCK, BLOCK), f32),
                pltpu.VMEM((heads, BLOCK, BLOCK), bf16),
                pltpu.VMEM((RING, width, cols), bf16),
            ],
        ),
        compiler_params=pltpu.CompilerParams(dimension_semantics=("arbitrary",)),
        cost_estimate=cost("attn_fwd"),
        name="attn_fwd",
    )(scal, *parts)


def attn_bwd_body(scal, *refs):
    parts, refs = refs[:-24], refs[-24:]
    o, refs = refs[:RING], refs[RING:]
    g0, g1, g2, g3, lse, grad, q2, qs, kts, gs, ks, vns, inner, dq, dk, dv, held, push, low, dlow = refs
    i = pl.program_id(0)
    nb = pl.num_programs(0)
    heads, width = ks.shape[0], qs.shape[1]
    z = scal[0]
    ends = (scal[1], scal[2])

    @pl.when(i == 0)
    def _():
        for n, b in ring_blocks(z, len(parts)):
            ref = parts[n]
            qs[b] = ref[0:width] * bf16(0.125)
            kts[b] = ref[PAD : PAD + width]
            for h in range(heads):
                high, low = two_parts(ref[head_rows(h)])
                q2[h, b, 0:HEAD_DIM] = high
                q2[h, b, HEAD_DIM : 2 * HEAD_DIM] = low
                ks[h, b] = twice(ref[head_rows(h, PAD)])
                vns[h, b] = ref[head_rows(h, 2 * PAD)].T
        for s, ref in enumerate((g0, g1, g2, g3)):
            t = lax.rem(z + s, RING)
            for half in range(2):
                cols = slice(half * BLOCK, (half + 1) * BLOCK)
                gs[t * 2 + half] = ref[:, cols]
                both = ref[:, cols].astype(f32) * o[s][:, cols].astype(f32)
                for h in range(heads):
                    inner[t * 2 + half, h : h + 1, :] = jnp.sum(both[head_rows(h)], axis=0, keepdims=True)
        dk[...] = jnp.zeros_like(dk)
        dv[...] = jnp.zeros_like(dv)

    dq[i] = jnp.zeros(dq.shape[1:], f32)

    bounds, levers = [], []
    for h in range(heads):
        part = inner[i, h : h + 1, :]
        bounds.append(jnp.abs(part))
        levers.append(jnp.where(part < 0, -1e38, 1e38))

    def products(j, h):
        held[h] = nn(ks[h, j], q2[h, i])
        push[h] = nn(vns[h, j], gs[i, head_rows(h)])

    def step(j, carry, bias):
        products(j, 0)
        for h in range(heads):
            if h + 1 < heads:
                products(j, h + 1)
            for rows in chunks():
                s = held[h, rows]
                mag = jnp.exp2(size_of(s, bias, rows) - lse[i, h : h + 1, :])
                low[h, rows] = signed(s, mag)
                ds = mag * (push[h, rows] - jnp.clip(s * levers[h], -bounds[h], bounds[h]))
                dlow[h, rows] = ds.astype(bf16)
            rows = head_rows(h)
            dv[j, rows] += nt(gs[i, rows], low[h])
            dk[j, rows] += nt(qs[i, rows], dlow[h])
            dq[i, rows] += nn(kts[j, rows], dlow[h])
        return carry

    walk(i, ends, step, 0)

    @pl.when(i == nb - 1)
    def _():
        grad[...] = jnp.zeros_like(grad)
        for n, b in ring_blocks(z, len(parts)):
            cols = slice(n * BLOCK, (n + 1) * BLOCK)
            grad[0:width, cols] = (dq[b] * 0.125).astype(bf16)
            grad[PAD : PAD + width, cols] = dk[b].astype(bf16)
            grad[2 * PAD : 2 * PAD + width, cols] = dv[b].astype(bf16)


def attn_bwd(scal, parts, attended, grads, lse):
    nb = len(parts)
    width = attended[0].shape[0]
    heads = width // HEAD_DIM
    ops = (*parts, *attended, *grads, lse)
    result = (3 * PAD, nb * BLOCK)
    return pl.pallas_call(
        attn_bwd_body,
        out_shape=sds(result),
        grid_spec=pltpu.PrefetchScalarGridSpec(
            num_scalar_prefetch=1,
            grid=(nb,),
            in_specs=[whole(p.shape) for p in ops],
            out_specs=whole(result),
            scratch_shapes=[
                pltpu.VMEM((heads, nb, 2 * HEAD_DIM, BLOCK), bf16),
                pltpu.VMEM((nb, width, BLOCK), bf16),
                pltpu.VMEM((nb, width, BLOCK), bf16),
                pltpu.VMEM((nb, width, BLOCK), bf16),
                pltpu.VMEM((heads, nb, BLOCK, 2 * HEAD_DIM), bf16),
                pltpu.VMEM((heads, nb, BLOCK, HEAD_DIM), bf16),
                pltpu.VMEM((nb, 8, BLOCK), f32),
                pltpu.VMEM((nb, width, BLOCK), f32),
                pltpu.VMEM((nb, width, BLOCK), f32),
                pltpu.VMEM((nb, width, BLOCK), f32),
                pltpu.VMEM((heads, BLOCK, BLOCK), f32),
                pltpu.VMEM((heads, BLOCK, BLOCK), f32),
                pltpu.VMEM((heads, BLOCK, BLOCK), bf16),
                pltpu.VMEM((heads, BLOCK, BLOCK), bf16),
            ],
        ),
        compiler_params=pltpu.CompilerParams(dimension_semantics=("arbitrary",)),
        cost_estimate=cost("attn_bwd"),
        name="attn_bwd",
    )(scal, *ops)


LANE = 128


LENGTH = {
    "pack": 2, "unpack_qkv": 2.5, "norm_qkv": 3.4, "stack": 2.5, "unpack": 6, "project": 6.4, "branch": 5.8,
    "first_o": 2.7, "back_first": 4, "back_rest": 5.6, "third": 5.4, "fourth": 3.2, "first_qkv": 2.3,
    "second_qkv": 1.8, "fifth": 2, "finish": 5.5, "attn_fwd": 18, "attn_bwd": 25, "mlp": 11,
}
FLOPS_PER_US = 1_000_000_000


def cost(name):
    return pl.CostEstimate(flops=int(LENGTH[name] * FLOPS_PER_US), bytes_accessed=100_000, transcendentals=0)


def call(body, outs, *ops, scratch=(), name=None):
    near = pl.BlockSpec(memory_space=pltpu.VMEM)
    return pl.pallas_call(
        body,
        out_shape=tuple(outs),
        in_specs=[near] * len(ops),
        out_specs=(near,) * len(outs),
        scratch_shapes=list(scratch),
        cost_estimate=cost(name),
        name=name,
    )(*ops)


def aligned(x, n):
    return pl.multiple_of(x, n)


def after(x, *others):
    return lax.optimization_barrier((x, *others))[0]


def mine_of(k):
    return lax.div(lax.axis_index("dp"), 1 << k) & 1


def pack_body(w_qkv, gain_a, gain_m, w_up, w_down, w_out, qkv, keep, give):
    rows, half = w_up.shape[0], w_up.shape[1] // 2
    width = w_out.shape[0]
    mine = mine_of(0)
    qkv[...] = jnp.zeros_like(qkv)
    for c in range(3):
        qkv[:, c * PAD : c * PAD + width] = w_qkv[c]
    eye = lax.broadcasted_iota(jnp.int32, (rows, rows), 0) == lax.broadcasted_iota(jnp.int32, (rows, rows), 1)
    lane = lax.broadcasted_iota(jnp.int32, (rows, LANE), 1)
    cols = [jnp.sum(jnp.where(eye, g[...].astype(f32), 0.0), axis=1, keepdims=True) for g in (gain_a, gain_m)]
    qkv[:, 3 * PAD :] = jnp.where(lane == 0, cols[0], jnp.where(lane == 1, cols[1], 0.0)).astype(bf16)
    tiles = half // LANE
    for k in range(tiles):
        for to, which in ((keep, mine), (give, 1 - mine)):
            at = which * half + k * LANE
            to[k * rows : (k + 1) * rows] = w_up[:, pl.ds(aligned(at, LANE), LANE)]
            to[(tiles + k) * rows : (tiles + k + 1) * rows] = w_down[:, pl.ds(aligned(at, LANE), LANE)]
    base = 2 * tiles * rows
    back = w_out[...].astype(f32).T.astype(bf16)
    keep[base : base + rows] = back[:, 0:LANE]
    keep[base + rows : base + 2 * rows] = jnp.zeros((rows, LANE), bf16)
    keep[base + rows : base + 2 * rows, 0 : width - LANE] = back[:, LANE:width]


def unpack_qkv_body(near, far, w, gains):
    me = lax.axis_index("dp")
    rows = near.shape[1]
    count = near.shape[0]
    tail = []
    for p in range(2 * count):
        src = near if p < count else far
        mask = 2 * (p % count) + (1 if p >= count else 0)
        w[pl.ds(aligned((me ^ mask) * rows, 32), rows)] = src[p % count, :, : 3 * PAD]
    for b in range(2 * count):
        mask = me ^ b
        part = lax.div(mask, 2)
        col = jnp.where(
            (mask & 1) == 0, near[part, :, 3 * PAD :].astype(f32), far[part, :, 3 * PAD :].astype(f32)
        )
        tail.append(col)
    gains[...] = jnp.concatenate(tail, axis=0).T[0:8]


def norm_qkv_body(xa, xb, w, gains, normed, qa, qb):
    for half, (x, q) in enumerate(((xa, qa), (xb, qb))):
        size = x.shape[0]

        for n in range(size // 64):
            v = x[pl.ds(n * 64, 64)].astype(f32)
            c = v - jnp.mean(v, axis=-1, keepdims=True)
            rstd = lax.rsqrt(jnp.mean(c * c, axis=-1, keepdims=True) + EPS)
            normed[pl.ds(half * size + n * 64, 64)] = (c * rstd * gains[0:1]).astype(bf16)

        q[...] = nn(normed[half * size : (half + 1) * size], w[...]).astype(bf16).T


def stack_body(*refs):
    parts, (a, b) = refs[:-2], refs[-2:]
    u = b.shape[1] // 2
    for s, p in enumerate(parts):
        a[s, 0:u] = p[0:u]
        b[s, 0:u] = p[u : 2 * u]
        a[s, u : 2 * u] = p[2 * u : 3 * u]
        b[s, u : 2 * u] = p[3 * u : 4 * u]
        a[s, 2 * u :] = p[4 * u :]


def unpack_body(*refs):
    early, late, (up, down, back) = refs[0:8], refs[8:16], refs[16:19]
    me = lax.axis_index("dp")
    rows = 96
    half = up.shape[1] // RING
    tiles = half // LANE
    span = tiles * rows
    for p in range(4):
        for s in range(RING):
            came = early if s < early[0].shape[0] else late
            a, b, at = came[p], came[4 + p], s % early[0].shape[0]
            for rc in range(2):
                to_a = pl.ds(aligned((me ^ (2 * p + rc)) * rows, 32), rows)
                to_b = pl.ds(aligned((me ^ (2 * ((p & 1) * 2 + (p >> 1)) + rc)) * rows, 32), rows)
                for k in range(tiles):
                    cols = slice(s * half + k * LANE, s * half + (k + 1) * LANE)
                    src = slice(rc * span + k * rows, rc * span + (k + 1) * rows)
                    up[to_a, cols] = a[at, src]
                    down[to_b, cols] = b[at, src]
            where = lax.div(me ^ (2 * p), 2)
            for k in range(2):
                back[where, s, :, k * LANE : (k + 1) * LANE] = a[at, 2 * span + k * rows : 2 * span + (k + 1) * rows]


def project_body(x, a0, a1, a2, a3, near, far, gains, mixed, mlp, tokens_major, w):
    mine = mine_of(0)
    rows = near.shape[2]
    width = a0.shape[0]
    for b in range(near.shape[0]):
        for s in range(RING):
            w[s, pl.ds(aligned((2 * b + mine) * rows, 32), rows)] = near[b, s]
            w[s, pl.ds(aligned((2 * b + 1 - mine) * rows, 32), rows)] = far[b, s]
    zero = jnp.zeros((PAD - width, a0.shape[1]), bf16)
    for s, a in enumerate((a0, a1, a2, a3)):
        tokens_major[:, s * PAD : (s + 1) * PAD] = jnp.concatenate([a[...], zero], axis=0).T
    for r in range(0, x.shape[0], 128):
        total = x[r : r + 128].astype(f32)
        for s in range(RING):
            total = total + nt(tokens_major[r : r + 128, s * PAD : (s + 1) * PAD], w[s])
        mixed[r : r + 128] = total
    normalise(mixed, gains[1:2], mlp)


def normalise(rows, gain, out):
    for r in range(0, rows.shape[0], 64):
        at = slice(r, r + 64)
        v = rows[at]
        c = v - jnp.mean(v, axis=-1, keepdims=True)
        rstd = lax.rsqrt(jnp.mean(c * c, axis=-1, keepdims=True) + EPS)
        out[at] = (c * rstd * gain).astype(bf16)


def gelu_both(v):
    square = v * v
    t = jnp.tanh(v * (0.7978845608028654 + (0.7978845608028654 * 0.044715) * square))
    gate = 0.5 + 0.5 * t
    bend = v * (2 * 0.7978845608028654 + (6 * 0.7978845608028654 * 0.044715) * square)
    return v * gate, gate + gate * (1.0 - gate) * bend


def mlp_body(x0, x1, g0, g1, up, down, active, grad, hid, push):
    size = x0.shape[0]
    for half, (x, g) in enumerate(((x1, g1), (x0, g0))):
        hid[half] = nn(x[...], up[...])
        push[half] = nn(g[...], down[...])
    for half in range(2):
        @pl.loop(0, size // BLOCK)
        def _(n):
            for r in range(0, BLOCK, 64):
                rows = pl.ds(aligned(n * BLOCK + r, 64), 64)
                to = pl.ds(aligned((1 - half) * size + n * BLOCK + r, 64), 64)
                value, slope = gelu_both(hid[half, rows])
                active[to] = value.astype(bf16)
                grad[to] = (push[half, rows] * slope).astype(bf16)


def mlp(x0, x1, g0, g1, up, down):
    tokens, dim = x0.shape
    hidden = up.shape[1]
    keep = pl.BlockSpec((tokens, dim), lambda n: (0, 0))
    cols = pl.BlockSpec((dim, BLOCK), lambda n: (0, n))
    wide = pl.BlockSpec((2 * tokens, BLOCK), lambda n: (0, n))
    return pl.pallas_call(
        mlp_body,
        out_shape=(sds((2 * tokens, hidden)), sds((2 * tokens, hidden))),
        grid=(hidden // BLOCK,),
        in_specs=[keep] * 4 + [cols] * 2,
        out_specs=(wide, wide),
        scratch_shapes=[pltpu.VMEM((2, tokens, BLOCK), f32), pltpu.VMEM((2, tokens, BLOCK), f32)],
        cost_estimate=cost("mlp"),
        name="mlp",
    )(x0, x1, g0, g1, up, down)


def norm_back(v, gain, grad):
    c = v - jnp.mean(v, axis=-1, keepdims=True)
    rstd = lax.rsqrt(jnp.mean(c * c, axis=-1, keepdims=True) + EPS)
    hat = c * rstd
    g = grad * gain
    return rstd * (g - jnp.mean(g, axis=-1, keepdims=True) - hat * jnp.mean(g * hat, axis=-1, keepdims=True))


def branch_body(mixed, part, far, grad_out, gains, w, grad_mixed, branch, *heads):
    @pl.loop(0, mixed.shape[0] // BLOCK)
    def _(n):
        for r in range(0, BLOCK, 64):
            at = pl.ds(aligned(n * BLOCK + r, 64), 64)
            grad = part[at] + far[at].astype(f32)
            total = grad_out[at].astype(f32) + norm_back(mixed[at], gains[1:2], grad)
            grad_mixed[at] = total
            branch[at] = total.astype(bf16)

    width = heads[0].shape[0]
    for s in range(RING):
        heads[s][...] = nn(branch[...], w[s]).astype(bf16).T[0:width]


def back_body(grad, w, *outs, blocks):
    for out, n in zip(outs, blocks):
        out[...] = nt(grad[:, n * BLOCK : (n + 1) * BLOCK].T, w[...]).astype(bf16)


def finish_body(*refs):
    parts, recvs, (x, grad_mixed, gains, out) = refs[0:2], refs[2:4], refs[4:]
    for k, (part, recv) in enumerate(zip(parts, recvs)):
        for r in range(0, BLOCK, 64):
            grad = part[r : r + 64].astype(f32) + recv[r : r + 64].astype(f32)
            at = slice(k * BLOCK + r, k * BLOCK + r + 64)
            out[at] = grad_mixed[at] + norm_back(x[at].astype(f32), gains[0:1], grad)


def turn(x, shift):
    return lax.ppermute(x, "tensor", [(i, (i + shift) % RING) for i in range(RING)])


def swap(x, axis, bit, size):
    return lax.ppermute(x, axis, [(i, i ^ bit) for i in range(size)])


def pick(x, index, axis=0):
    return lax.dynamic_index_in_dim(x, index, axis, keepdims=False)


def ring_gather(x):
    got = [x]
    for _ in range(RING - 1):
        got.append(turn(got[-1], 1))
    return got


def ring_reduce(chunks):
    moving = chunks[1].astype(bf16)
    for r in range(1, RING):
        moved = turn(moving, 1)
        total = moved.astype(f32) + chunks[(r + 1) % RING]
        moving = total.astype(bf16)
    return total


def spread_blocks(x, bits, size):
    for bit in bits:
        x = jnp.concatenate([x, swap(x, "dp", bit, size)])
    return x


def place_of(mask, bits):
    place = 0
    for k, bit in enumerate(bits):
        place = place + jnp.where(mask & bit != 0, 1 << k, 0)
    return place


def halve(blocks, left, bit, me, size):
    at = left.index(bit)
    lead, tail = 1 << at, 1 << (len(left) - at - 1)
    split = blocks.reshape((lead, 2, tail) + blocks.shape[1:])
    mine = jnp.where(me & bit != 0, 1, 0)
    send = pick(split, 1 - mine, 1).astype(bf16)
    keep = pick(split, mine, 1)
    total = keep.astype(f32) + swap(send, "dp", bit, size).astype(f32)
    return total.reshape((lead * tail,) + blocks.shape[1:]), [b for b in left if b != bit]


def centre(rows):
    shifted = rows - jnp.mean(rows, axis=-1, keepdims=True)
    rstd = lax.rsqrt(jnp.mean(shifted * shifted, axis=-1, keepdims=True) + EPS)
    return shifted * rstd, rstd


def norm_back_plain(grad_hat, hat, rstd):
    return rstd * (
        grad_hat
        - jnp.mean(grad_hat, axis=-1, keepdims=True)
        - hat * jnp.mean(grad_hat * hat, axis=-1, keepdims=True)
    )


def einf(spec, a, b):
    return jnp.einsum(spec, a, b, preferred_element_type=f32)


def shards(size, inputs, doc_ids, gain_attn, w_qkv, w_out, gain_mlp, w_up, w_down, grad_out):
    me = lax.axis_index("dp")
    z = lax.axis_index("tensor")
    odd = me & 1
    others = [1 << k for k in range(1, size.bit_length() - 1)]
    documents = doc_ids[0]
    tokens, dim = inputs.shape
    rows = dim // size
    hid = w_up.shape[1]
    half = hid // 2
    width = w_out.shape[0]
    scal = jnp.stack([z, jnp.sum(documents < 1), jnp.sum(documents < 2)]).astype(jnp.int32)

    pieces = [ring_gather(inputs[k : k + BLOCK]) for k in range(0, tokens, BLOCK)]

    gains = jnp.stack([gain_attn, gain_mlp])
    own = jnp.concatenate([w_qkv[0], w_qkv[1], w_qkv[2], jnp.pad(gains, ((0, 62), (0, 0))).T], axis=1)
    order = others + [1]
    spread_qkv = spread_blocks(own[None], order, size)
    full = jnp.concatenate([pick(spread_qkv, place_of(me ^ b, order)) for b in range(size)])
    full_qkv = full[:, : 3 * width]
    gain_one = full[:, 3 * width].astype(f32)
    gain_two = full[:, 3 * width + 1].astype(f32)

    out_rows = jnp.concatenate([w_out.T[: rows // 2], w_out.T[rows // 2 :]], axis=1)

    def pair_half(w):
        parts = w.reshape(rows, 2, half)
        return jnp.concatenate([pick(parts, odd, 1), swap(pick(parts, 1 - odd, 1), "dp", 1, size)])

    pack_a = jnp.concatenate([pair_half(w_up), out_rows])
    pack_b = pair_half(w_down.T)
    ring_a = jnp.stack(ring_gather(pack_a))
    ring_b = jnp.stack(ring_gather(pack_b))
    order_b = others[::-1]
    spread_a = spread_blocks(ring_a[None], others, size)
    spread_b = spread_blocks(ring_b[None], order_b, size)

    def assemble(spread_w, bits):
        blocks = []
        for b in range(size):
            mask = me ^ b
            block = pick(spread_w, place_of(mask, bits))[:, : 2 * rows]
            block = pick(block.reshape(RING, 2, rows, half), mask & 1, 1)
            blocks.append(block.transpose(1, 0, 2).reshape(rows, RING * half))
        return jnp.concatenate(blocks)

    full_up = assemble(spread_a, others)
    full_down = assemble(spread_b, order_b)
    out_part = spread_a[:, :, 2 * rows :]
    out_both = jnp.stack([out_part, swap(out_part, "dp", 1, size)])

    def out_block(b):
        mask = me ^ b
        block = pick(pick(out_both, mask & 1), place_of(mask, others))
        block = jnp.concatenate([block[..., :width], block[..., width:]], axis=1)
        return block.transpose(1, 0, 2).reshape(rows, RING * width)

    full_out = jnp.concatenate([out_block(b) for b in range(size)])
    grad_both = jnp.concatenate([grad_out, swap(grad_out, "dp", 1, size)])
    grad_active = einf("td,df->tf", grad_both, full_down)

    normed = []
    parts = []
    for s in range(RING):
        for piece in pieces:
            hat, _ = centre(piece[s].astype(f32))
            normed.append((hat * gain_one).astype(bf16))
            part = einf("de,td->et", full_qkv, normed[-1]).astype(bf16).reshape(3, width, BLOCK)
            parts.append(jnp.pad(part, ((0, 0), (0, PAD - width), (0, 0))).reshape(3 * PAD, BLOCK))
    normed = jnp.concatenate(normed)
    *sent, lse = attn_fwd(scal, parts, width // HEAD_DIM)
    attended = jnp.concatenate([sent[0]] + [turn(sent[s], s) for s in range(1, RING)])
    mixed = inputs.astype(f32) + einf("et,de->td", attended, full_out)
    hat_two, rstd_two = centre(mixed)
    mlp_rows = (hat_two * gain_two).astype(bf16)
    mlp_both = jnp.concatenate([mlp_rows, swap(mlp_rows, "dp", 1, size)])
    hidden = einf("td,df->tf", mlp_both, full_up)
    value, slope = gelu_both(hidden)
    active = value.astype(bf16)
    grad_hidden = (grad_active * slope).astype(bf16)
    grad_part = einf("tf,df->td", grad_hidden, full_up)
    grad_mlp = grad_part[:tokens] + swap(grad_part[tokens:].astype(bf16), "dp", 1, size).astype(f32)
    grad_mixed = grad_out.astype(f32) + norm_back_plain(grad_mlp * gain_two, hat_two, rstd_two)
    grad_branch = grad_mixed.astype(bf16)
    grad_att = einf("de,td->et", full_out, grad_branch).astype(bf16).reshape(RING, width, tokens)
    grads = [grad_att[0]] + [turn(grad_att[s], -s) for s in range(1, RING)]

    out_pair = einf("tf,df->td", active, full_down)
    layer_out = (
        mixed + out_pair[:tokens] + swap(out_pair[tokens:].astype(bf16), "dp", 1, size).astype(f32)
    ).astype(bf16)

    bits = [1 << k for k in reversed(range(size.bit_length() - 1))]

    def scatter(grad, stages, last_width):
        blocks, left = grad.reshape(size, rows, grad.shape[1]), list(bits)
        for bit in stages:
            blocks, left = halve(blocks, left, bit, me, size)
        blocks = blocks.reshape(-1, blocks.shape[-1])
        return ring_reduce([blocks[:, s * last_width : (s + 1) * last_width] for s in range(RING)])

    def pair_whole(block):
        block = block.reshape(2, rows, half)
        send = pick(block, 1 - odd).astype(bf16)
        keep = pick(block, odd)
        other = swap(send, "dp", 1, size).astype(f32)
        return jnp.where(odd == 0, jnp.concatenate([keep, other], axis=1), jnp.concatenate([other, keep], axis=1))

    grad_down = pair_whole(scatter(einf("td,tf->df", grad_both, active), others, half)).T
    grad_up = pair_whole(scatter(einf("td,tf->df", mlp_both, grad_hidden), order_b, half))
    grad_o = scatter(einf("td,et->de", grad_branch, attended), [1] + order_b, width).T

    grad_parts = attn_bwd(scal, parts, sent, grads, lse)
    grad_parts = grad_parts.reshape(3, PAD, -1)[:, :width].reshape(3 * width, -1)
    grad_proj = einf("td,et->de", normed, grad_parts)
    blocks, left = grad_proj.reshape(size, rows, 3 * width), list(bits)
    for bit in [1] + order_b:
        blocks, left = halve(blocks, left, bit, me, size)
    grad_qkv = blocks[0].reshape(rows, 3, width).transpose(1, 0, 2)

    back = []
    for k in range(0, tokens, BLOCK):
        back.append(
            ring_reduce(
                [
                    einf("et,de->td", grad_parts[:, s * tokens + k : s * tokens + k + BLOCK], full_qkv)
                    for s in range(RING)
                ]
            )
        )
    grad_normed = jnp.concatenate(back)
    hat_one, rstd_one = centre(inputs.astype(f32))
    grad_inputs = grad_mixed + norm_back_plain(grad_normed * gain_one, hat_one, rstd_one)

    sums = jnp.stack(
        [
            jnp.sum(w_qkv.astype(f32) * grad_qkv, axis=(0, 2)),
            jnp.sum(w_up.astype(f32) * grad_up, axis=1),
        ]
    )
    for bit in (1, 2):
        sums = sums + swap(sums, "tensor", bit, RING)
    sums = sums / gains.astype(f32)
    return layer_out, grad_inputs, sums[0], grad_qkv, grad_o, sums[1], grad_up, grad_down


def add(a, b):
    return (a.astype(f32) + b.astype(f32)).astype(bf16)


def first_body(full, recv, send, keep, *, by_y):
    c = mine_of(0)
    mine = mine_of(2 if by_y else 1)
    for k in range(2):
        for which, to in ((mine, keep), (1 - mine, send)):
            at = which * 2 + k if by_y else k * 2 + which
            to[k] = add(full[at * 2 + c], recv[at])


def second_body(keep_in, recv, send, keep):
    mine = mine_of(1)
    keep[...] = add(keep_in[mine], recv[mine])
    send[...] = add(keep_in[1 - mine], recv[1 - mine])


def third_body(up, far_up, down, far_down, o, far_o, up_send, up_keep, mix_send, mix_keep):
    c, x, y = mine_of(0), mine_of(1), mine_of(2)
    rows = up.shape[1]
    tiles = up.shape[2] // RING // LANE
    span = tiles * rows
    for s in range(RING):
        for rc in range(2):
            side = jnp.bitwise_xor(c, rc)
            for k in range(tiles):
                cols = slice((s * tiles + k) * LANE, (s * tiles + k + 1) * LANE)
                to = slice(rc * span + k * rows, rc * span + (k + 1) * rows)
                for which, out in ((x, up_keep), (1 - x, up_send)):
                    out[s, to] = add(up[y * 4 + which * 2 + side, :, cols], far_up[which * 2 + side, :, cols])
                for which, out in ((y, mix_keep), (1 - y, mix_send)):
                    out[s, to] = add(down[which * 4 + x * 2 + side, :, cols], far_down[which * 2 + side, :, cols])
        for k in range(2):
            cols = slice((s * 2 + k) * LANE, (s * 2 + k + 1) * LANE)
            to = slice(2 * span + k * rows, 2 * span + (k + 1) * rows)
            for which, out in ((y, mix_keep), (1 - y, mix_send)):
                out[s, to] = add(o[which, :, cols], far_o[which, :, cols])


def fourth_body(up, far_up, mix, far_mix, first, rest):
    span = up.shape[1] // 2
    extra = mix.shape[1] - 2 * span
    for s in range(RING):
        for rc in range(2):
            src = slice(rc * span, (rc + 1) * span)
            at = rc * 2 * span
            rest[s, at : at + span] = add(up[s, src], far_up[s, src])
            rest[s, at + span : at + 2 * span] = add(mix[s, src], far_mix[s, src])
        tail = slice(2 * span, 2 * span + extra)
        rest[s, 4 * span : 4 * span + extra] = add(mix[s, tail], far_mix[s, tail])
    first[...] = rest[1]


def fifth_body(mine, far, up, down, o):
    c = mine_of(0)
    rows = up.shape[0]
    half = up.shape[1] // 2
    tiles = half // LANE
    for side, src in ((c, mine), (1 - c, far)):
        for k in range(tiles):
            at = pl.ds(aligned(side * half + k * LANE, LANE), LANE)
            up[:, at] = src[k * rows : (k + 1) * rows].astype(f32)
            down[:, at] = src[(tiles + k) * rows : (tiles + k + 1) * rows].astype(f32)
    base = 4 * tiles * rows
    width = o.shape[0]
    o[0:LANE] = mine[base : base + rows].astype(f32).T
    o[LANE:width] = mine[base + rows : base + 2 * rows].astype(f32).T[0 : width - LANE]


def shards_small(size, inputs, doc_ids, gain_attn, w_qkv, w_out, gain_mlp, w_up, w_down, grad_out):
    me = lax.axis_index("dp")
    z = lax.axis_index("tensor")
    documents = doc_ids[0]
    tokens, dim = inputs.shape
    rows, hid = w_up.shape
    half = hid // 2
    width = w_out.shape[0]
    heads = width // HEAD_DIM
    hidden = RING * half
    scal = jnp.stack([z, jnp.sum(documents < 1), jnp.sum(documents < 2)]).astype(jnp.int32)

    def pair(x):
        return swap(x, "dp", 1, size)

    def along_x(x):
        return swap(x, "dp", 2, size)

    def along_y(x):
        return swap(x, "dp", 4, size)

    span = half * rows // LANE
    x_a, x_b = ([inputs[k : k + BLOCK]] for k in range(0, tokens, BLOCK))

    def hop():
        x_a.append(turn(x_a[-1], 1))
        x_b.append(turn(x_b[-1], 1))

    hop()
    qkv, keep, give = call(
        pack_body,
        [sds((rows, 3 * PAD + LANE)), sds((2 * span + 2 * rows, LANE)), sds((2 * span, LANE))],
        w_qkv, gain_attn[None], gain_mlp[None], w_up, w_down.T, w_out, name="pack",
    )
    got = pair(after(give, x_a[1]))
    qkv = jnp.stack([qkv, along_x(qkv)])
    packed = jnp.concatenate([keep[: 2 * span], got, keep[2 * span :]])
    qkv = jnp.concatenate([qkv, along_y(qkv)])
    qkv_far = pair(qkv)
    ring = [packed, turn(after(packed, x_a[1], x_b[1]), 1)]
    hop()
    ring.append(turn(after(ring[1], x_a[2], x_b[2]), 1))
    hop()
    grad_far = pair(after(grad_out, x_a[2]))
    full_qkv, gains = call(
        unpack_qkv_body, [sds((dim, 3 * PAD)), sds((8, dim), f32)], qkv, qkv_far, name="unpack_qkv"
    )
    normed, parts = [], []
    for s in range(RING):
        n, qa, qb = call(
            norm_qkv_body,
            [sds((tokens, dim)), sds((3 * PAD, BLOCK)), sds((3 * PAD, BLOCK))],
            x_a[s], x_b[s], full_qkv, gains, name="norm_qkv",
        )
        normed.append(n)
        parts.extend((qa, qb))

    ring.append(turn(after(ring[2], normed[0]), 1))

    def spread(*shares):
        n = len(shares)
        u0, d0 = call(
            stack_body, [sds((n, 2 * span + 2 * rows, LANE)), sds((n, 2 * span, LANE))], *shares, name="stack"
        )
        u1, d1 = along_x(u0), along_y(d0)
        u2, d2 = along_y(u0), along_x(d0)
        return u0, u1, u2, d0, d1, d2

    def spread_on(blocks, *others):
        u0, u1, u2, d0, d1, d2 = blocks
        return u0, u1, u2, along_y(after(u1, *others)), d0, d1, d2, along_x(after(d1, *others))

    early = spread_on(spread(*ring[:2], after(ring[2], normed[0], normed[1])), normed[2])
    late = spread(ring[3])

    *sent, lse = attn_fwd(after(scal, late[0]), parts, heads)
    attended = [sent[0]] + [turn(sent[s], s) for s in range(1, RING)]
    late = spread_on(late, sent[0])
    full_up, full_down, back_near = call(
        unpack_body,
        [sds((dim, hidden)), sds((dim, hidden)), sds((size // 2, RING, rows, PAD))],
        *early, *late[:-1], after(late[-1], *attended[1:]), name="unpack",
    )
    back_far = pair(back_near)
    mixed, mlp_rows, att_tokens, full_out = call(
        project_body,
        [sds((tokens, dim), f32), sds((tokens, dim)), sds((tokens, RING * PAD)), sds((RING, dim, PAD))],
        inputs, *attended, back_near, back_far, gains, name="project",
    )
    mlp_far = pair(mlp_rows)
    active, grad_hidden = mlp(mlp_rows, mlp_far, grad_out, grad_far, full_up, full_down)
    part_got = pair(einf("tf,df->td", grad_hidden[tokens:], full_up).astype(bf16))
    part = einf("tf,df->td", grad_hidden[:tokens], full_up)
    grad_mixed, branch, *grad_att = call(
        branch_body,
        [sds((tokens, dim), f32), sds((tokens, dim)), *[sds((width, tokens))] * RING],
        mixed, part, part_got, grad_out, gains, full_out, name="branch",
    )
    grads = [grad_att[0]] + [turn(grad_att[s], -s) for s in range(1, RING)]
    grad_hidden_late = after(grad_hidden, branch)
    active_late = after(active, branch)

    x_bit, y_bit, c_bit = lax.div(me, 2) & 1, lax.div(me, 4) & 1, me & 1
    both_in = jnp.concatenate([mlp_rows, mlp_far])
    both_grad = jnp.concatenate([grad_out, grad_far])
    grad_up = einf("td,tf->df", both_in, grad_hidden_late).astype(bf16)
    grad_down = einf("td,tf->df", both_grad, active_late).astype(bf16)
    far_up = along_y(pick(grad_up.reshape(2, 4, rows, hidden), 1 - y_bit))
    far_down = along_x(pick(grad_down.reshape(2, 2, 2, rows, hidden), 1 - x_bit, 1).reshape(4, rows, hidden))
    grad_o = einf("td,te->de", branch, att_tokens).astype(bf16)
    far_o = pair(pick(grad_o.reshape(4, 2, rows, RING * PAD), 1 - c_bit, 1))
    layer_far = pair(einf("tf,df->td", active_late[tokens:], full_down).astype(bf16))
    layer_near = einf("tf,df->td", active_late[:tokens], full_down)
    layer_out = (mixed + layer_near + layer_far.astype(f32)).astype(bf16)

    o_send, o_keep = call(
        functools.partial(first_body, by_y=False),
        [sds((2, rows, RING * PAD))] * 2, grad_o.reshape(size, rows, RING * PAD), far_o, name="first_o",
    )

    grad_parts = attn_bwd(scal, parts, sent, grads, after(lse, layer_out, o_send))
    count = tokens // BLOCK

    def backs(grad, blocks, name):
        return call(
            functools.partial(back_body, blocks=blocks), [sds((BLOCK, dim))] * len(blocks), grad, full_qkv, name=name
        )

    start = backs(grad_parts, list(range(count, 2 * count)), "back_first")
    came = [turn(start[k], 1) for k in range(count)]
    later = backs(
        after(grad_parts, *start), list(range(2 * count, RING * count)) + list(range(count)), "back_rest"
    )
    up_shape, mix_shape = sds((RING, 2 * span, LANE)), sds((RING, 2 * span + 2 * rows, LANE))
    up_send, up_keep, mix_send, mix_keep = call(
        third_body,
        [up_shape, up_shape, mix_shape, mix_shape],
        grad_up.reshape(size, rows, hidden), far_up, grad_down.reshape(size, rows, hidden), far_down,
        o_keep, along_x(o_send), name="third",
    )
    far_up_two, far_mix_two = along_x(up_send), along_y(mix_send)
    sums = [add(after(later[k], up_send), came[k]) for k in range(count)]
    came = [turn(x, 1) for x in sums]
    total_shape = (4 * span + 2 * rows, LANE)
    moving, rest = call(
        fourth_body,
        [sds(total_shape), sds((RING, *total_shape))],
        up_keep, far_up_two, mix_keep, far_mix_two, name="fourth",
    )

    came = [turn(add(later[count + k], came[k]), 1) for k in range(count)]
    grad_inputs = call(
        finish_body,
        [sds((tokens, dim), f32)],
        *later[(RING - 2) * count :], *came, inputs, grad_mixed, gains, name="finish",
    )[0]

    grad_proj = einf("td,et->de", jnp.concatenate(normed), after(grad_parts, up_send, *sums)).astype(bf16)
    far_qkv = pair(pick(grad_proj.reshape(4, 2, rows, 3 * PAD), 1 - c_bit, 1))
    q_send, q_keep = call(
        functools.partial(first_body, by_y=True),
        [sds((2, rows, 3 * PAD))] * 2, grad_proj.reshape(size, rows, 3 * PAD), far_qkv, name="first_qkv",
    )
    q_send, q_keep = call(
        second_body, [sds((rows, 3 * PAD))] * 2, q_keep, along_y(q_send), name="second_qkv"
    )
    grad_flat = q_keep.astype(f32) + along_x(q_send).astype(f32)
    grad_qkv = jnp.stack([grad_flat[:, c * PAD : c * PAD + width] for c in range(3)])

    for r in range(1, RING):
        moving = add(turn(moving, 1), rest[(r + 1) % RING])
    grad_up, grad_down, grad_o = call(
        fifth_body,
        [sds((rows, hid), f32), sds((rows, hid), f32), sds((width, rows), f32)],
        after(moving, grad_inputs), pair(moving[2 * span : 4 * span]), name="fifth",
    )
    sums = jnp.stack(
        [
            jnp.sum(w_qkv.astype(f32) * grad_qkv, axis=(0, 2)),
            jnp.sum(w_up.astype(f32) * grad_up, axis=1),
        ]
    )
    sums = sums + turn(sums, 1) + turn(sums, 2) + turn(sums, 3)
    own = jnp.stack([gain_attn, gain_mlp]).astype(f32)
    sums = sums / own
    return layer_out, grad_inputs, sums[0], grad_qkv, grad_o, sums[1], grad_up, grad_down.T


def solution(mesh):
    both = P(("dp", "tensor"), None)
    weights = (P(None, "dp", "tensor"), P("tensor", "dp"), P("dp"), P("dp", "tensor"), P("tensor", "dp"))
    return jax.shard_map(
        functools.partial(shards_small if mesh.shape["dp"] == 8 else shards, mesh.shape["dp"]),
        mesh=mesh,
        in_specs=(both, P("dp", None), P("dp"), *weights, both),
        out_specs=(both, both, P("dp"), *weights),
        check_vma=False,
    )
```
